32 devices in a mesh: shard: 4 (over y, x), context: 2 (over core), tensor: 4 (over z).
Axes of the slice: x: 2, y: 2, z: 4, core: 2. Of those that a mesh axis runs over, the one named last changes fastest.
Arguments:
- tokens: bfloat16 [16, 1024, 768], P('shard', ('context', 'tensor')), may hold values from -6 to 6
- lengths: int32 [16], P('shard'), may hold values from 256 to 1024, as said below
- features: bfloat16 [12, 256, 64], P('tensor'), may hold values from -3 to 3, as said below
- w_qkv: bfloat16 [768, 3, 12, 64], P('shard', None, 'tensor'), may hold values from -0.3125 to 0.3125
- b_qkv: bfloat16 [3, 12, 64], P(None, 'tensor', 'shard'), may hold values from -1.5 to 1.5
- w_out: bfloat16 [768, 768], P('tensor', 'shard'), may hold values from -1.75 to 1.75
- b_out: bfloat16 [768], P('shard'), may hold values from -3 to 3
- gain_one: bfloat16 [768], P('shard'), may hold values from 0.099609375 to 1.8984375
- shift_one: bfloat16 [768], P('shard'), may hold values from -3 to 3
- w_up: bfloat16 [768, 3072], P('shard', 'tensor'), may hold values from -0.21875 to 0.21875
- b_up: bfloat16 [24, 128], P('tensor', 'shard'), may hold values from -3 to 3
- w_down: bfloat16 [3072, 768], P('tensor', 'shard'), may hold values from -0.109375 to 0.109375
- b_down: bfloat16 [768], P('shard'), may hold values from -3 to 3
- gain_two: bfloat16 [768], P('shard'), may hold values from 0.099609375 to 1.8984375
- shift_two: bfloat16 [768], P('shard'), may hold values from -3 to 3
- cotangent: bfloat16 [16, 1024, 768], P('shard', ('context', 'tensor')), may hold values from -6 to 6
Outputs:
- out: bfloat16 [16, 1024, 768], P('shard', ('context', 'tensor'))
- grad_tokens: float32 [16, 1024, 768], P('shard', ('context', 'tensor'))
- grad_w_qkv: float32 [768, 3, 12, 64], P('shard', None, 'tensor')
- grad_b_qkv: float32 [3, 12, 64], P(None, 'tensor', 'shard')
- grad_w_out: float32 [768, 768], P('tensor', 'shard')
- grad_b_out: float32 [768], P('shard')
- grad_gain_one: float32 [768], P('shard')
- grad_shift_one: float32 [768], P('shard')
- grad_w_up: float32 [768, 3072], P('shard', 'tensor')
- grad_b_up: float32 [24, 128], P('tensor', 'shard')
- grad_w_down: float32 [3072, 768], P('tensor', 'shard')
- grad_b_down: float32 [768], P('shard')
- grad_gain_two: float32 [768], P('shard')
- grad_shift_two: float32 [768], P('shard')
The draws below stay inside these ranges and needn't reach their ends.
Inputs may be any that keep to these rules, and one draw needn't show every extreme that they name: `lengths`: at least one sequence is valid in all 1024 slots and at least one in a quarter of them. `features`: independent entries of mean 0 and variance about 1.
All inputs are finite; a program needn't handle non-finite values.
Results may differ from the reference program's by a relative error of at most 0.034.
Values may be sent and summed in bfloat16 or wider, within the bound.
No kernel may reach another device: no remote copies, remote signals or barrier semaphores. Data moves between devices by JAX's collectives and lax.ppermute only.
A program may use at most 192 MiB of HBM per device.

```python
import jax
import jax.numpy as jnp
from jax import lax

D = 768
H = 12
HD = 64
FF = 3072
M = 256
LEN = 1024
SEQS = 16


def draw_lengths(key, part):
    first_key, second_key = jax.random.split(key)
    picks = jax.random.randint(first_key, (SEQS,), LEN // 4, LEN + 1)
    order = jax.random.permutation(second_key, SEQS)
    picks = picks.at[order[0]].set(LEN)
    picks = picks.at[order[1]].set(LEN // 4)
    return picks.astype(jnp.int32)


def draw_features(key, part):
    entries = jnp.clip(jax.random.normal(key, (H, M, HD), jnp.float32), -3.0, 3.0)
    return entries.astype(jnp.bfloat16)


def block_scale(rng, dims, cuts, smallest, top_value):
    level = 1.0
    for position, shards_of in cuts:
        steps = jax.random.uniform(jax.random.fold_in(jax.random.fold_in(rng, 6), position), (shards_of,), jnp.float32, smallest / len(cuts), top_value / len(cuts))
        level = level * jnp.repeat(jnp.exp(steps), dims[position] // shards_of).reshape((-1,) + (1,) * (len(dims) - 1 - position))
    return level


def centred(rng, dims, scale, most, cuts=(), dtype=jnp.bfloat16):
    array = scale * jax.random.normal(rng, dims, jnp.float32)
    if cuts:
        array = array * block_scale(rng, dims, cuts, -0.22, 0.18)
    return jnp.clip(array, -most, most).astype(dtype)


def setup_inputs(seed: int = 0) -> dict:
    key_of = jax.random.split(jax.random.key(seed), 17)
    tokens = centred(key_of[0], (SEQS, LEN, D), 1.0, 6.0, ((0, 4), (1, 8)))
    lengths = draw_lengths(jax.random.fold_in(key_of[16], 71), 0)
    features = draw_features(jax.random.fold_in(key_of[16], 71), 0)
    w_qkv = centred(key_of[3], (D, 3, H, HD), (D // 2) ** -0.5, 0.3125, ((0, 4), (2, 4)))
    b_qkv = centred(key_of[4], (3, H, HD), 0.1, 1.5, ((1, 4), (2, 4)))
    w_out = centred(key_of[5], (D, D), 12 ** -0.5, 1.75, ((0, 4), (1, 4)))
    b_out = centred(key_of[6], (D,), 0.2, 3.0, ((0, 4),))
    gain_one = jnp.clip(1.0 + 0.18 * jax.random.normal(key_of[7], (D,), jnp.float32), 0.099609375, 1.8984375).astype(jnp.bfloat16)
    shift_one = centred(key_of[8], (D,), 0.2, 3.0, ((0, 4),))
    w_up = centred(key_of[9], (D, FF), D ** -0.5, 0.21875, ((0, 4), (1, 4)))
    b_up = centred(key_of[10], (FF // 128, 128), 0.2, 3.0, ((0, 4), (1, 4)))
    w_down = centred(key_of[11], (FF, D), FF ** -0.5, 0.109375, ((0, 4), (1, 4)))
    b_down = centred(key_of[12], (D,), 0.2, 3.0, ((0, 4),))
    gain_two = jnp.clip(1.0 + 0.18 * jax.random.normal(key_of[13], (D,), jnp.float32), 0.099609375, 1.8984375).astype(jnp.bfloat16)
    shift_two = centred(key_of[14], (D,), 0.2, 3.0, ((0, 4),))
    cotangent = centred(key_of[15], (SEQS, LEN, D), 1.0, 6.0, ((0, 4), (1, 8)))
    return {"tokens": tokens, "lengths": lengths, "features": features, "w_qkv": w_qkv, "b_qkv": b_qkv, "w_out": w_out, "b_out": b_out, "gain_one": gain_one, "shift_one": shift_one, "w_up": w_up, "b_up": b_up, "w_down": w_down, "b_down": b_down, "gain_two": gain_two, "shift_two": shift_two, "cotangent": cotangent}


@jax.custom_vjp
def low(v):
    return lax.optimization_barrier(v.astype(jnp.bfloat16)).astype(jnp.float32)

@jax.custom_vjp
def low_back(v):
    return v

def low_keep(v):
    return (low(v), None)

def low_pass(kept, grad):
    return (grad,)

def back_keep(v):
    return (v, None)

def back_low(kept, grad):
    return (low(grad),)
low.defvjp(low_keep, low_pass)
low_back.defvjp(back_keep, back_low)

def layer_norm(residual, gain, offset):
    average = lax.optimization_barrier(jnp.mean(residual, axis=-1, keepdims=True))
    centered = residual - average
    variance = lax.optimization_barrier(jnp.mean(centered * centered, axis=-1, keepdims=True))
    return centered * lax.rsqrt(variance + 1e-05) * gain + offset

def encoder_layer(sequence, length, feature_table, w_qkv, b_qkv, w_out, b_out, gain_one, shift_one, w_up, b_up, w_down, b_down, gain_two, shift_two):
    highest = lax.Precision.HIGHEST
    qkv = low_back(jnp.einsum('td,dchk->tchk', sequence, w_qkv, precision=highest) + b_qkv[None])
    feature_scale = HD ** (-0.25)
    queries = low(qkv[:, 0] * feature_scale)
    key_rows = low(qkv[:, 1] * feature_scale)
    values = low(qkv[:, 2])
    validity = (jnp.arange(LEN) < length).astype(jnp.float32)[:, None, None]
    query_dash = low_back(jnp.einsum('thk,hmk->thm', queries, feature_table, precision=highest)) - 0.5 * lax.optimization_barrier(jnp.sum(queries * queries, axis=-1, keepdims=True))
    key_dash = low_back(jnp.einsum('thk,hmk->thm', key_rows, feature_table, precision=highest)) - 0.5 * lax.optimization_barrier(jnp.sum(key_rows * key_rows, axis=-1, keepdims=True))
    query_exp = jnp.exp(query_dash - jnp.floor(lax.optimization_barrier(jnp.max(query_dash, axis=-1, keepdims=True))))
    key_stab = jnp.floor(lax.optimization_barrier(jnp.max(jnp.where(validity > 0, key_dash, -1e+30), axis=(0, 2))))[None, :, None]
    key_exp = jnp.exp(jnp.where(validity > 0, key_dash - key_stab, -60.0)) * validity
    query_feat = low(query_exp)
    key_feat = low(key_exp)
    key_state = low(jnp.einsum('thm,thk->hmk', key_feat, values, precision=highest))
    key_total = low(lax.optimization_barrier(jnp.sum(key_feat, axis=0)))
    numerator = jnp.einsum('thm,hmk->thk', query_feat, key_state, precision=highest)
    denominator = jnp.einsum('thm,hm->th', query_feat, key_total, precision=highest)
    mixed_heads = low(low_back(numerator / denominator[:, :, None]))
    attention = low_back(jnp.dot(mixed_heads.reshape(LEN, D), w_out, precision=highest))
    normed = layer_norm(attention + b_out + sequence, gain_one, shift_one)
    up_input = low_back(jnp.dot(low(normed), w_up, precision=highest) + b_up.reshape(FF))
    activated = low(jax.nn.gelu(up_input, approximate=False))
    feedforward = low_back(jnp.dot(activated, w_down, precision=highest))
    return layer_norm(feedforward + b_down + normed, gain_two, shift_two)

def reference(tokens, lengths, features, w_qkv, b_qkv, w_out, b_out, gain_one, shift_one, w_up, b_up, w_down, b_down, gain_two, shift_two, cotangent):
    weight_list = tuple((p.astype(jnp.float32) for p in (w_qkv, b_qkv, w_out, b_out, gain_one, shift_one, w_up, b_up, w_down, b_down, gain_two, shift_two)))
    feature_table = features.astype(jnp.float32)

    def advance(running, element):
        sequence, length, upstream = element

        def forward(sequence_in, *weights):
            return encoder_layer(sequence_in, length, feature_table, *weights)
        result, pullback = jax.vjp(forward, sequence.astype(jnp.float32), *weight_list)
        gradients = pullback(upstream.astype(jnp.float32))
        running = tuple((a + b for a, b in zip(running, gradients[1:])))
        return (running, (result.astype(jnp.bfloat16), gradients[0]))
    initial = tuple((jnp.zeros(p.shape, jnp.float32) for p in weight_list))
    sums, (outputs, grad_rows) = lax.scan(advance, initial, (tokens, lengths, cotangent))
    return (outputs, grad_rows, sums[0], sums[1], sums[2], sums[3], sums[4], sums[5], sums[6], sums[7], sums[8], sums[9], sums[10], sums[11])
```

```python
import functools

import jax
import jax.numpy as jnp
from jax import lax
from jax.experimental import pallas as pl
from jax.experimental.pallas import tpu as pltpu
from jax.sharding import PartitionSpec as P

F = jnp.float32
B = jnp.bfloat16


def layer_stats(residual):
    average = jnp.mean(residual, axis=-1, keepdims=True)
    centered = residual - average
    variance = jnp.mean(centered * centered, axis=-1, keepdims=True)
    inverse = lax.rsqrt(variance + 1e-05)
    return (centered * inverse, inverse)


def layer_back(normal, inverse, gain, upstream):
    scaled = upstream * gain
    inner = (
        scaled
        - jnp.mean(scaled, axis=-1, keepdims=True)
        - normal * jnp.mean(scaled * normal, axis=-1, keepdims=True)
    )
    return (
        inner * inverse,
        jnp.sum(upstream * normal, axis=0),
        jnp.sum(upstream, axis=0),
    )


def wide_add(*terms):
    total = terms[0].astype(F)
    for term in terms[1:]:
        total = total + term.astype(F)
    return total


class Links:
    def __init__(self, sizes):
        self.sizes = sizes
        self.s = lax.axis_index("shard")
        self.c = lax.axis_index("context")
        self.t = lax.axis_index("tensor")
        self.core = self.c % 2

    def perm_t(self, value, step):
        n = self.sizes["tensor"]
        return lax.ppermute(value, "tensor", [(i, (i + step) % n) for i in range(n)])

    def perm_s(self, value, mask):
        n = self.sizes["shard"]
        return lax.ppermute(value, "shard", [(i, i ^ mask) for i in range(n)])

    def perm_c(self, value, mask=1):
        n = self.sizes["context"]
        return lax.ppermute(value, "context", [(i, i ^ mask) for i in range(n)])

    def deal(self, rows):
        n = self.sizes["tensor"]
        pieces = [lax.dynamic_index_in_dim(rows, self.t, 0, keepdims=False)]
        for d in range(1, n):
            piece = lax.dynamic_index_in_dim(rows, (self.t + d) % n, 0, keepdims=False)
            pieces.append(self.perm_t(piece, d))
        return jnp.concatenate(pieces, axis=0)

    def undeal(self, rows):
        n = self.sizes["tensor"]
        rows = rows.reshape(n, rows.shape[0] // n, rows.shape[1])
        result = jnp.zeros(rows.shape, rows.dtype)
        for d in range(n):
            piece = rows[d] if d == 0 else self.perm_t(rows[d], n - d)
            result = lax.dynamic_update_index_in_dim(result, piece, (self.t + d) % n, 0)
        return result

    def spread(self, local):
        n = self.sizes["tensor"]
        block = jnp.stack([local] + [self.perm_t(local, d) for d in range(1, n)])
        over_x = self.perm_s(block, 1)
        over_y = self.perm_s(block, 2)
        far = (self.perm_s(over_x[: n // 2], 2), self.perm_s(over_y[n // 2 :], 1))
        mine = [block, over_x, over_y, far[0], far[1]]
        other = [self.perm_c(piece) for piece in mine]
        return mine + other

    def half(self, local):
        rows = local.shape[0] // 2
        return lax.dynamic_slice_in_dim(local, self.core * rows, rows, 0)

    def collect(self, grad):
        n, m = self.sizes["tensor"], self.sizes["shard"]
        rows, cols = grad.shape[1] // m, grad.shape[2]
        parts = grad.reshape(n, m, 2, rows // 2, cols)
        keep = lax.dynamic_index_in_dim(parts, self.core, 2, keepdims=False)
        give = lax.dynamic_index_in_dim(parts, 1 - self.core, 2, keepdims=False)
        parts = wide_add(keep, self.perm_c(give)).astype(B)

        def to(mask):
            return lax.dynamic_index_in_dim(parts, self.s ^ mask, 1, keepdims=False)

        near, beside, above, far = to(0), to(1), to(2), to(3)
        h = n // 2
        via_y = self.perm_s(far[:h], 2)
        via_x = self.perm_s(far[h:], 1)
        beside = jnp.concatenate([wide_add(beside[:h], via_y).astype(B), beside[h:]])
        above = jnp.concatenate([above[:h], wide_add(above[h:], via_x).astype(B)])
        parts = wide_add(near, self.perm_s(beside, 1), self.perm_s(above, 2)).astype(B)
        total = wide_add(parts[0], *[self.perm_t(parts[d], n - d) for d in range(1, n)])
        mask = 2
        while mask < self.sizes["context"]:
            low = total.astype(B)
            total = wide_add(low, self.perm_c(low, mask))
            mask *= 2
        low = total.astype(B)
        other = self.perm_c(low)
        first = jnp.where(self.core == 0, low, other)
        second = jnp.where(self.core == 0, other, low)
        return jnp.concatenate([first, second])


def assemble(links, pieces, rows, extra):
    n, m = links.sizes["tensor"], links.sizes["shard"]
    cols = pieces[0].shape[-1]
    where = jnp.stack([links.s, links.core]).astype(jnp.int32)
    count = 2 * (n // 1) * 3 + 2 * n

    def body(where_ref, *refs):
        ins, outs, sems = refs[:10], refs[10:-1], refs[-1]
        s, c = where_ref[0], where_ref[1]
        copies = []
        for i in range(2):
            half = c if i == 0 else 1 - c
            for j in range(m):
                shard = s ^ j
                start = pl.multiple_of(shard * (2 * rows) + half * rows, 8)
                for t in range(n):
                    if j < 3:
                        src = ins[i * 5 + j].at[t]
                    elif t < n // 2:
                        src = ins[i * 5 + 3].at[t]
                    else:
                        src = ins[i * 5 + 4].at[t - n // 2]
                    copies.append((src.at[pl.ds(0, rows)], outs[0].at[t, pl.ds(start, rows)]))
                    if extra and i == 0:
                        copies.append((src.at[pl.ds(rows, extra)], outs[1].at[shard, t]))
        running = [
            pltpu.make_async_copy(a, b, sems.at[k]) for k, (a, b) in enumerate(copies)
        ]
        for r in running:
            r.start()
        for r in running:
            r.wait()

    shapes = [jax.ShapeDtypeStruct((n, m * 2 * rows, cols), B)]
    if extra:
        shapes.append(jax.ShapeDtypeStruct((m, n, extra, cols), B))
    total = 2 * m * n + (m * n if extra else 0)
    return pl.pallas_call(
        body,
        out_shape=shapes,
        in_specs=[pl.BlockSpec(memory_space=pltpu.SMEM)]
        + [pl.BlockSpec(memory_space=pl.ANY)] * 10,
        out_specs=[pl.BlockSpec(memory_space=pl.ANY)] * len(shapes),
        scratch_shapes=[pltpu.SemaphoreType.DMA((total,))],
        name="assemble",
    )(where, *pieces)


def on_device(
    sizes,
    tokens,
    lengths,
    features,
    w_qkv,
    b_qkv,
    w_out,
    b_out,
    gain_one,
    shift_one,
    w_up,
    b_up,
    w_down,
    b_down,
    gain_two,
    shift_two,
    cotangent,
):
    links = Links(sizes)
    n, m = sizes["tensor"], sizes["shard"]
    chunk = tokens.shape[1]
    width = tokens.shape[2]
    heads_local, feats, hd = features.shape
    heads = heads_local * n
    share = width // m
    qkv_cols = 3 * heads_local * hd
    small = jnp.concatenate(
        [b_out, gain_one, shift_one, b_down, gain_two, shift_two, b_qkv.reshape(-1), b_up.reshape(-1)]
    )
    used = small.shape[0]
    small = jnp.pad(small, (0, 8 * qkv_cols - used)).reshape(8, qkv_cols)
    flat_qkv = w_qkv.reshape(share, qkv_cols)
    first = jnp.concatenate([links.half(flat_qkv), small])
    pieces_qkv = links.spread(first)
    x = links.deal(tokens)
    feat_t = features.transpose(2, 0, 1).reshape(hd, heads_local * feats)
    feat_half = links.half(feat_t)
    feat_mine = jnp.stack([feat_half] + [links.perm_t(feat_half, d) for d in range(1, n)])
    feat_other = links.perm_c(feat_mine)
    feat_low = jnp.where(links.core == 0, feat_mine, feat_other)
    feat_high = jnp.where(links.core == 0, feat_other, feat_mine)
    feat = jnp.concatenate([feat_low, feat_high], axis=1)
    feat = feat.reshape(n, hd, heads_local, feats).transpose(0, 2, 1, 3).reshape(heads, hd, feats)
    mid = jnp.concatenate([links.half(w_out.T), links.half(w_up)], axis=1)
    pieces_mid = links.spread(mid)
    pieces_down = links.spread(links.half(w_down.T))
    upstream = links.deal(cotangent).astype(F)
    rows = share // 2
    wq, smalls = assemble(links, pieces_qkv, rows, 8)
    wm = assemble(links, pieces_mid, rows, 0)[0]
    wd = assemble(links, pieces_down, rows, 0)[0]
    smalls = smalls.reshape(m, n, 8 * qkv_cols).astype(F)
    vec = smalls[:, 0, : 6 * share].reshape(m, 6, share).transpose(1, 0, 2).reshape(6, width)
    bias_out, gain_first, offset_first, bias_down, gain_second, offset_second = vec
    a = 6 * share
    bq = b_qkv.size
    bias_qkv = (
        smalls[:, :, a : a + bq]
        .reshape(m, n, 3, heads_local, hd // m)
        .transpose(1, 2, 3, 0, 4)
        .reshape(n, qkv_cols)
    )
    a += bq
    bias_up = (
        smalls[:, :, a : a + b_up.size]
        .reshape((m, n) + b_up.shape)
        .transpose(1, 2, 0, 3)
        .reshape(n, -1)
    )
    hidden = b_up.size * m
    out_cols = heads_local * hd
    w_out_t = wm[:, :, :out_cols]
    w_up_t = wm[:, :, out_cols:]
    length = lax.dynamic_index_in_dim(lengths, links.t, 0, keepdims=False)
    order = (links.t - jnp.arange(n)) % n
    position = (links.c * (n * chunk) + order[:, None] * chunk + jnp.arange(chunk)[None]).reshape(-1)
    mask = (position < length)[:, None, None]
    dot = functools.partial(jnp.einsum, preferred_element_type=F)
    scale = hd ** (-0.25)
    qkv = dot("rd,tdj->rtj", x, wq) + bias_qkv[None]
    span = x.shape[0]
    qkv = qkv.reshape(span, n, 3, heads_local, hd)
    queries = (qkv[:, :, 0] * scale).astype(B).reshape(span, heads, hd)
    keys = (qkv[:, :, 1] * scale).astype(B).reshape(span, heads, hd)
    values = qkv[:, :, 2].astype(B).reshape(span, heads, hd)
    query_wide = queries.astype(F)
    key_wide = keys.astype(F)
    query_dash = dot("rhk,hkm->rhm", queries, feat) - 0.5 * jnp.sum(
        query_wide * query_wide, axis=-1, keepdims=True
    )
    key_dash = dot("rhk,hkm->rhm", keys, feat) - 0.5 * jnp.sum(
        key_wide * key_wide, axis=-1, keepdims=True
    )
    query_exp = jnp.exp(query_dash - jnp.floor(jnp.max(query_dash, axis=-1, keepdims=True)))
    local_top = jnp.max(jnp.where(mask, key_dash, -1e30), axis=(0, 2))
    key_stab = jnp.floor(lax.pmax(local_top, "context"))
    key_exp = jnp.exp(jnp.where(mask, key_dash - key_stab[None, :, None], -60.0)) * mask.astype(F)
    query_feat = query_exp.astype(B)
    key_feat = key_exp.astype(B)
    key_state = dot("rhm,rhk->hmk", key_feat, values)
    key_total = jnp.sum(key_feat, axis=0, dtype=F)
    state_low = lax.psum(key_state.astype(B), "context")
    total_low = lax.psum(key_total.astype(B), "context")
    numerator = dot("rhm,hmk->rhk", query_feat, state_low)
    denominator = dot("rhm,hm->rh", query_feat, total_low)
    ratio = numerator / denominator[..., None]
    mixed = ratio.astype(B)
    mixed_t = mixed.reshape(span, n, out_cols)
    attention = dot("rtk,tdk->rd", mixed_t, w_out_t)
    res_first = attention + bias_out + x.astype(F)
    normal_first, inverse_first = layer_stats(res_first)
    normed = normal_first * gain_first + offset_first
    normed_low = normed.astype(B)
    up_input = dot("rd,tdf->rtf", normed_low, w_up_t) + bias_up[None]
    activated = jax.nn.gelu(up_input, approximate=False).astype(B)
    feedforward = dot("rtf,tdf->rd", activated, wd)
    res_second = feedforward + bias_down + normed
    normal_second, inverse_second = layer_stats(res_second)
    result = links.undeal((normal_second * gain_second + offset_second).astype(B))
    d_res_second, grad_gain_two, grad_shift_two = layer_back(
        normal_second, inverse_second, gain_second, upstream
    )
    grad_b_down = jnp.sum(d_res_second, axis=0)
    d_ffn = d_res_second.astype(B)
    grad_down = dot("rd,rtf->tdf", d_ffn, activated).astype(B)
    own_down = links.collect(grad_down)
    d_act = dot("rd,tdf->rtf", d_ffn, wd)
    slope = (
        0.5 * (1.0 + lax.erf(up_input * 0.7071067811865476))
        + up_input * jnp.exp(-0.5 * up_input * up_input) * 0.3989422804014327
    )
    d_up = (d_act * slope).astype(B)
    grad_up = dot("rd,rtf->tdf", normed_low, d_up).astype(B)
    grad_b_up = jnp.sum(d_up, axis=0, dtype=F)
    d_normed = dot("rtf,tdf->rd", d_up, w_up_t) + d_res_second
    d_res_first, grad_gain_one, grad_shift_one = layer_back(
        normal_first, inverse_first, gain_first, d_normed
    )
    grad_b_out = jnp.sum(d_res_first, axis=0)
    d_attn = d_res_first.astype(B)
    grad_out = dot("rd,rtk->tdk", d_attn, mixed_t).astype(B)
    own_mid = links.collect(jnp.concatenate([grad_out, grad_up], axis=2))
    d_mixed = dot("rd,tdk->rtk", d_attn, w_out_t).astype(B).astype(F).reshape(span, heads, hd)
    d_num = d_mixed / denominator[..., None]
    d_den = -jnp.sum(d_mixed * ratio, axis=-1) / denominator
    d_state = dot("rhm,rhk->hmk", query_feat, d_num)
    d_total = dot("rhm,rh->hm", query_feat, d_den)
    d_state = lax.psum(d_state.astype(B), "context").astype(F)
    d_total = lax.psum(d_total.astype(B), "context").astype(F)
    d_query_dash = (
        dot("rhk,hmk->rhm", d_num, state_low) + d_den[..., None] * total_low[None].astype(F)
    ) * query_exp
    d_key_dash = (dot("rhk,hmk->rhm", values, d_state) + d_total[None]) * key_exp
    d_values = dot("rhm,hmk->rhk", key_feat, d_state)
    d_queries = dot("rhm,hkm->rhk", d_query_dash.astype(B), feat) - query_wide * jnp.sum(
        d_query_dash, axis=-1, keepdims=True
    )
    d_keys = dot("rhm,hkm->rhk", d_key_dash.astype(B), feat) - key_wide * jnp.sum(
        d_key_dash, axis=-1, keepdims=True
    )
    d_qkv = (
        jnp.stack(
            [
                (d_queries * scale).reshape(span, n, heads_local, hd),
                (d_keys * scale).reshape(span, n, heads_local, hd),
                d_values.reshape(span, n, heads_local, hd),
            ],
            axis=2,
        )
        .astype(B)
        .reshape(span, n, qkv_cols)
    )
    grad_qkv = dot("rd,rtj->tdj", x, d_qkv).astype(B)
    grad_b_qkv = jnp.sum(d_qkv, axis=0, dtype=F)
    grad_x = dot("rtj,tdj->rd", d_qkv, wq) + d_res_first
    grad_tokens = links.undeal(grad_x.astype(B)).astype(F)
    vecs = jnp.stack(
        [grad_b_out, grad_gain_one, grad_shift_one, grad_b_down, grad_gain_two, grad_shift_two]
    )
    vecs = vecs.reshape(6, m, share).transpose(1, 0, 2).reshape(m, 6 * share)
    small_qkv = (
        grad_b_qkv.reshape(n, 3, heads_local, m, hd // m).transpose(0, 3, 1, 2, 4).reshape(n, m, -1)
    )
    small_up = (
        grad_b_up.reshape(n, b_up.shape[0], m, b_up.shape[1]).transpose(0, 2, 1, 3).reshape(n, m, -1)
    )
    packed = jnp.concatenate(
        [jnp.broadcast_to(vecs[None], (n, m, 6 * share)), small_qkv, small_up], axis=2
    )
    packed = jnp.pad(packed, ((0, 0), (0, 0), (0, 16 * qkv_cols - used))).reshape(
        n, m, 16, qkv_cols
    )
    grad_qkv = jnp.concatenate(
        [
            grad_qkv.reshape(n, m, 2, rows, qkv_cols),
            packed.astype(B).reshape(n, m, 2, 8, qkv_cols),
        ],
        axis=3,
    ).reshape(n, m * 2 * (rows + 8), qkv_cols)
    own_qkv = links.collect(grad_qkv)
    own_qkv = own_qkv.reshape(2, rows + 8, qkv_cols)
    own_small = own_qkv[:, rows:].reshape(-1)[:used].astype(F)
    own_w_qkv = own_qkv[:, :rows].reshape(share, 3, heads_local, hd).astype(F)
    v = own_small[: 6 * share].reshape(6, share)
    own_b_qkv = own_small[6 * share : 6 * share + bq].reshape(b_qkv.shape)
    own_b_up = own_small[6 * share + bq :].reshape(b_up.shape)
    return (
        result,
        grad_tokens,
        own_w_qkv,
        own_b_qkv,
        own_mid[:, :out_cols].T.astype(F),
        v[0],
        v[1],
        v[2],
        own_mid[:, out_cols:].astype(F),
        own_b_up,
        own_down.T.astype(F),
        v[3],
        v[4],
        v[5],
    )


def solution(mesh):
    sizes = dict(mesh.shape)
    in_specs = (
        P("shard", ("context", "tensor"), None),
        P("shard"),
        P("tensor", None, None),
        P("shard", None, "tensor", None),
        P(None, "tensor", "shard"),
        P("tensor", "shard"),
        P("shard"),
        P("shard"),
        P("shard"),
        P("shard", "tensor"),
        P("tensor", "shard"),
        P("tensor", "shard"),
        P("shard"),
        P("shard"),
        P("shard"),
        P("shard", ("context", "tensor"), None),
    )
    out_specs = (
        P("shard", ("context", "tensor"), None),
        P("shard", ("context", "tensor"), None),
        P("shard", None, "tensor", None),
        P(None, "tensor", "shard"),
        P("tensor", "shard"),
        P("shard"),
        P("shard"),
        P("shard"),
        P("shard", "tensor"),
        P("tensor", "shard"),
        P("tensor", "shard"),
        P("shard"),
        P("shard"),
        P("shard"),
    )
    return jax.shard_map(
        functools.partial(on_device, sizes),
        mesh=mesh,
        in_specs=in_specs,
        out_specs=out_specs,
        check_vma=False,
    )
```

```python
import functools

import jax
import jax.numpy as jnp
from jax import lax
from jax.experimental import pallas as pl
from jax.experimental.pallas import tpu as pltpu
from jax.sharding import PartitionSpec as P

F = jnp.float32
B = jnp.bfloat16


def wide_add(*terms):
    total = terms[0].astype(F)
    for term in terms[1:]:
        total = total + term.astype(F)
    return total


class Links:
    def __init__(self, sizes):
        self.sizes = sizes
        self.s = lax.axis_index("shard")
        self.c = lax.axis_index("context")
        self.t = lax.axis_index("tensor")
        self.core = self.c % 2

    def perm_t(self, value, step):
        n = self.sizes["tensor"]
        return lax.ppermute(value, "tensor", [(i, (i + step) % n) for i in range(n)])

    def perm_s(self, value, mask):
        n = self.sizes["shard"]
        return lax.ppermute(value, "shard", [(i, i ^ mask) for i in range(n)])

    def perm_c(self, value, mask=1):
        n = self.sizes["context"]
        return lax.ppermute(value, "context", [(i, i ^ mask) for i in range(n)])

    def deal(self, rows):
        n = self.sizes["tensor"]
        pieces = [lax.dynamic_index_in_dim(rows, self.t, 0, keepdims=False)]
        for d in range(1, n):
            piece = lax.dynamic_index_in_dim(rows, (self.t + d) % n, 0, keepdims=False)
            pieces.append(self.perm_t(piece, d))
        return jnp.concatenate(pieces, axis=0)

    def undeal(self, rows):
        n = self.sizes["tensor"]
        rows = rows.reshape(n, rows.shape[0] // n, rows.shape[1])
        result = jnp.zeros(rows.shape, rows.dtype)
        for d in range(n):
            piece = rows[d] if d == 0 else self.perm_t(rows[d], n - d)
            result = lax.dynamic_update_index_in_dim(result, piece, (self.t + d) % n, 0)
        return result

    def spread(self, local):
        n = self.sizes["tensor"]
        block = jnp.stack([local] + [self.perm_t(local, d) for d in range(1, n)])
        over_x = self.perm_s(block, 1)
        over_y = self.perm_s(block, 2)
        far = (self.perm_s(over_x[: n // 2], 2), self.perm_s(over_y[n // 2 :], 1))
        mine = [block, over_x, over_y, far[0], far[1]]
        other = [self.perm_c(piece) for piece in mine]
        return mine + other

    def half(self, local):
        rows = local.shape[0] // 2
        return lax.dynamic_slice_in_dim(local, self.core * rows, rows, 0)

    def collect(self, keep, give):
        n = self.sizes["tensor"]
        parts = wide_add(keep, self.perm_c(give)).astype(B)
        near, beside, above, far = parts[0], parts[1], parts[2], parts[3]
        h = n // 2
        via_y = self.perm_s(far[:h], 2)
        via_x = self.perm_s(far[h:], 1)
        beside = jnp.concatenate([wide_add(beside[:h], via_y).astype(B), beside[h:]])
        above = jnp.concatenate([above[:h], wide_add(above[h:], via_x).astype(B)])
        parts = wide_add(near, self.perm_s(beside, 1), self.perm_s(above, 2)).astype(B)
        total = wide_add(parts[0], *[self.perm_t(parts[d], n - d) for d in range(1, n)])
        mask = 2
        while mask < self.sizes["context"]:
            low = total.astype(B)
            total = wide_add(low, self.perm_c(low, mask))
            mask *= 2
        low = total.astype(B)
        other = self.perm_c(low)
        first = jnp.where(self.core == 0, low, other)
        second = jnp.where(self.core == 0, other, low)
        return jnp.concatenate([first, second])


def dot(a, b, ca=1, cb=0):
    return lax.dot_general(a, b, (((ca,), (cb,)), ((), ())), preferred_element_type=F)


def iota(shape, axis):
    return lax.broadcasted_iota(jnp.int32, shape, axis)


def block_diagonal(compact, heads):
    k, m = compact.shape[0], compact.shape[1] // heads
    zero = jnp.zeros((k, m), compact.dtype)
    rows = []
    for h in range(heads):
        row = [zero] * heads
        row[h] = compact[:, h * m : (h + 1) * m]
        rows.append(jnp.concatenate(row, axis=1))
    return jnp.concatenate(rows, axis=0)


def diagonal_blocks(full, heads):
    k, m = full.shape[0] // heads, full.shape[1] // heads
    return jnp.concatenate(
        [full[h * k : (h + 1) * k, h * m : (h + 1) * m] for h in range(heads)], axis=1
    )


def stacked(upper, lower, heads):
    a, b = block_diagonal(upper, heads), block_diagonal(lower, heads)
    gap = jnp.zeros((second_start(a.shape[0]) - a.shape[0], a.shape[1]), a.dtype)
    return jnp.concatenate([a, gap, b], axis=0)


def second_start(width):
    return -(-width // 128) * 128


def beside(left, right):
    gap = jnp.zeros((left.shape[0], second_start(left.shape[1]) - left.shape[1]), left.dtype)
    return jnp.concatenate([left, gap, right], axis=1)


def rows_to_lanes(rows, lanes):
    k = rows.shape[1]
    tile = (iota((k, lanes), 1) % k == iota((k, lanes), 0)).astype(F).astype(B)
    spread = dot(rows, tile)
    hit = iota(spread.shape, 1) // k == iota(spread.shape, 0)
    return jnp.sum(jnp.where(hit, spread, 0.0), axis=0, keepdims=True)


class Pieces:
    def __init__(self, n, m, where, refs, dest, sems, start, cols):
        self.n, self.m, self.where, self.refs = n, m, where, refs
        self.dest, self.sems, self.start_col, self.cols = dest, sems, start, cols
        self.rows = refs[0].shape[1]

    def copies(self, t):
        s, c = self.where[0], self.where[1]
        made = []
        for i in range(2):
            half = c if i == 0 else 1 - c
            for j in range(self.m):
                row = pl.multiple_of((s ^ j) * (2 * self.rows) + half * self.rows, 8)
                if j < 3:
                    src = self.refs[i * 5 + j].at[t]
                elif t < self.n // 2:
                    src = self.refs[i * 5 + 3].at[t]
                else:
                    src = self.refs[i * 5 + 4].at[t - self.n // 2]
                src = src.at[:, pl.ds(self.start_col, self.cols)]
                target = self.dest.at[t, pl.ds(row, self.rows)]
                made.append(pltpu.make_async_copy(src, target, self.sems.at[t, i * self.m + j]))
        return made

    def start(self):
        for t in range(self.n):
            for copy in self.copies(t):
                copy.start()

    def wait(self, t):
        for u in range(self.n):

            @pl.when(t == u)
            def _():
                for copy in self.copies(u):
                    copy.wait()


ANY = pl.BlockSpec(memory_space=pl.ANY)
SCALARS = pl.BlockSpec(memory_space=pltpu.SMEM)


def slot(*shape):
    zeros = (0,) * len(shape)
    return pl.BlockSpec((1,) + shape, lambda t: (t,) + zeros)


def fixed(*shape):
    zeros = (0,) * len(shape)
    return pl.BlockSpec(shape, lambda *_: zeros)


def call(body, grid, in_specs, out_specs, outs, scratch, name, flops=0):
    return pl.pallas_call(
        body,
        grid=grid,
        in_specs=in_specs,
        out_specs=out_specs,
        out_shape=[jax.ShapeDtypeStruct(s, d) for s, d in outs],
        scratch_shapes=scratch,
        compiler_params=pltpu.CompilerParams(
            dimension_semantics=("arbitrary",) * len(grid), vmem_limit_bytes=60 * 1024 * 1024
        ),
        name=name,
    )


def norm_stats(res):
    mean = jnp.mean(res, axis=-1, keepdims=True)
    centered = res - mean
    var = jnp.mean(centered * centered, axis=-1, keepdims=True)
    inverse = lax.rsqrt(var + 1e-05)
    return centered * inverse, inverse


def norm_back(normal, inverse, gain, upstream):
    scaled = upstream * gain
    inner = (
        scaled
        - jnp.mean(scaled, axis=-1, keepdims=True)
        - normal * jnp.mean(scaled * normal, axis=-1, keepdims=True)
    )
    return inner * inverse


def as_rows(vectors, first):
    width = vectors[0].shape[1]
    row = iota((8, width), 0)
    total = jnp.zeros((8, width), F)
    for i, vector in enumerate(vectors):
        total = jnp.where(row == first + i, vector, total)
    return total


def store_split(value, where, keep, give, m):
    rows = value.shape[0] // (2 * m)
    s, c = where[0], where[1]
    for half in range(2):
        parts = [value[(2 * i + half) * rows : (2 * i + half + 1) * rows].astype(B) for i in range(m)]

        @pl.when(c == half)
        def _():
            for i in range(m):
                keep[s ^ i, 0] = parts[i]

        @pl.when(c != half)
        def _():
            for i in range(m):
                give[s ^ i, 0] = parts[i]


class Shape:
    def __init__(self, sizes, features, tokens, b_up):
        self.n, self.m = sizes["tensor"], sizes["shard"]
        self.hl, self.feats, self.hd = features.shape
        self.chunk, self.width = tokens.shape[1], tokens.shape[2]
        self.span = self.chunk * self.n
        self.share = self.width // self.m
        self.rows = self.share // 2
        self.oc = self.hl * self.hd
        self.qc = 3 * self.oc
        self.hm = self.hl * self.feats
        self.ff = b_up.size * self.m
        self.q_cols = self.qc + 64
        self.mid_cols = self.ff + self.oc + 64
        self.scale = self.hd ** (-0.25)


def project(z, where, pieces, x, feat, valid):
    n, span, hl, feats, hd = z.n, z.span, z.hl, z.feats, z.hd

    def body(where, *refs):
        pcs, refs = refs[:10], refs[10:]
        x, feat, valid, q_out, k_out, v_out, qf_out, kf_out, st_out, top_out, w, sems = refs
        t = pl.program_id(0)
        fetch = Pieces(n, z.m, where, pcs, w, sems, 0, z.q_cols)
        pl.when(t == 0)(fetch.start)
        fetch.wait(t)
        bias = jnp.zeros((16, 64), F)
        for s in range(z.m):
            bias = bias + w[t, s * z.share : s * z.share + 16, z.qc :].astype(F)
        qkv = dot(x[...], w[t, :, : z.qc]) + rows_to_lanes(bias.astype(B), z.qc)
        q = (qkv[:, : z.oc] * z.scale).astype(B)
        k = (qkv[:, z.oc : 2 * z.oc] * z.scale).astype(B)
        v = qkv[:, 2 * z.oc :].astype(B)
        q_out[0], k_out[0], v_out[0] = q, k, v
        table = block_diagonal(feat[0], hl)
        qd, kd = dot(q, table), dot(k, table)
        qs, ks = q.astype(F), k.astype(F)
        qs, ks = qs * qs, ks * ks
        live = valid[...] > 0
        kfs, tops = [], []
        for h in range(hl):
            seg, cols = slice(h * hd, (h + 1) * hd), slice(h * feats, (h + 1) * feats)
            dash = qd[:, cols] - 0.5 * jnp.sum(qs[:, seg], axis=-1, keepdims=True)
            qf_out[0, :, cols] = jnp.exp(
                dash - jnp.floor(jnp.max(dash, axis=-1, keepdims=True))
            ).astype(B)
            dash = kd[:, cols] - 0.5 * jnp.sum(ks[:, seg], axis=-1, keepdims=True)
            top = jnp.max(jnp.where(live, dash, -1e30), axis=0, keepdims=True)
            top = jnp.floor(jnp.max(top, axis=1, keepdims=True))
            kf = jnp.where(live, jnp.exp(dash - top), 0.0).astype(B)
            kf_out[0, :, cols] = kf
            kfs.append(kf)
            tops.append(jnp.broadcast_to(top, (8, feats)))
        top_out[0] = jnp.concatenate(tops, axis=1)
        vx = jnp.concatenate([v, jnp.ones((span, 64), B)], axis=1)
        state = dot(vx, jnp.concatenate(kfs, axis=1), 0, 0)
        st_out[0] = jnp.concatenate(
            [diagonal_blocks(state[: z.oc], hl), state[z.oc : z.oc + 8]], axis=0
        ).astype(B)

    return call(
        body,
        (n,),
        [SCALARS] + [ANY] * 10 + [fixed(span, z.width), slot(hd, z.hm), fixed(span, 1)],
        [slot(span, z.oc)] * 3 + [slot(span, z.hm)] * 2 + [slot(hd + 8, z.hm), slot(8, z.hm)],
        [((n, span, z.oc), B)] * 3
        + [((n, span, z.hm), B)] * 2
        + [((n, hd + 8, z.hm), B), ((n, 8, z.hm), F)],
        [pltpu.VMEM((n, z.width, z.q_cols), B), pltpu.SemaphoreType.DMA((n, 2 * z.m))],
        "project",
    )(where, *pieces, x, feat, valid)


def attend(z, where, pieces, x, qf, state):
    n, span, hl, hd = z.n, z.span, z.hl, z.hd

    def body(where, *refs):
        pcs, refs = refs[:10], refs[10:]
        x, qf, state, mixed_out, den_out, normal_out, inverse_out, vec_out, bup_out, w, acc, sems = refs
        t = pl.program_id(0)
        fetch = Pieces(n, z.m, where, pcs, w, sems, z.ff, z.oc + 64)
        pl.when(t == 0)(fetch.start)
        compact = state[0, :hd]
        total = jnp.broadcast_to(state[0, hd : hd + 1], (hd, z.hm))
        table = stacked(compact, total, hl)
        both = dot(qf[0], table, 1, 1)
        den = both[:, second_start(z.oc) :]
        mixed = (both[:, : z.oc] / den).astype(B)
        mixed_out[0] = mixed
        den_out[0] = den
        fetch.wait(t)
        part = dot(mixed, w[t, :, : z.oc], 1, 1)

        @pl.when(t == 0)
        def _():
            acc[...] = part

        @pl.when(t > 0)
        def _():
            acc[...] += part

        bias = jnp.zeros((16, 64), F)
        for s in range(z.m):
            bias = bias + w[t, s * z.share + 24 : s * z.share + 40, z.oc :].astype(F)
        bup_out[0] = jnp.broadcast_to(rows_to_lanes(bias.astype(B), z.ff), (8, z.ff))

        @pl.when(t == n - 1)
        def _():
            lanes = z.width
            per = z.share // 64
            tile = (iota((64, lanes), 1) % 64 == iota((64, lanes), 0)).astype(F).astype(B)
            found = jnp.zeros((24, lanes), F)
            for s in range(z.m):
                spread = dot(w[0, s * z.share : s * z.share + 24, z.oc :], tile)
                hit = iota((24, lanes), 1) // 64 == per * s + iota((24, lanes), 0) % per
                found = found + jnp.where(hit, spread, 0.0)
            pick = (iota((8, 24), 1) // per == iota((8, 24), 0)).astype(F).astype(B)
            vec = dot(pick, found.astype(B))
            vec_out[...] = vec
            res = acc[...] + vec[0:1] + x[...].astype(F)
            normal, inverse = norm_stats(res)
            normal_out[...] = normal
            inverse_out[...] = inverse

    return call(
        body,
        (n,),
        [SCALARS] + [ANY] * 10 + [fixed(span, z.width), slot(span, z.hm), slot(hd + 8, z.hm)],
        [
            slot(span, z.oc),
            slot(span, z.oc),
            fixed(span, z.width),
            fixed(span, 1),
            fixed(8, z.width),
            slot(8, z.ff),
        ],
        [
            ((n, span, z.oc), B),
            ((n, span, z.oc), F),
            ((span, z.width), F),
            ((span, 1), F),
            ((8, z.width), F),
            ((n, 8, z.ff), F),
        ],
        [
            pltpu.VMEM((n, z.width, z.oc + 64), B),
            pltpu.VMEM((span, z.width), F),
            pltpu.SemaphoreType.DMA((n, 2 * z.m)),
        ],
        "attend",
    )(where, *pieces, x, qf, state)


def widen(z, where, pieces, normal, vec, bup):
    n, span = z.n, z.span

    def body(where, *refs):
        pcs, refs = refs[:10], refs[10:]
        normal, vec, bup, act_out, slope_out, w, low, sems = refs
        t = pl.program_id(0)
        fetch = Pieces(n, z.m, where, pcs, w, sems, 0, z.ff)

        @pl.when(t == 0)
        def _():
            fetch.start()
            low[...] = (normal[...] * vec[1:2] + vec[2:3]).astype(B)

        fetch.wait(t)
        up = dot(low[...], w[t]) + bup[0, 0:1]
        share = 0.5 * (1.0 + lax.erf(up * 0.7071067811865476))
        act_out[0] = (up * share).astype(B)
        slope_out[0] = (share + up * jnp.exp(-0.5 * up * up) * 0.3989422804014327).astype(B)

    return call(
        body,
        (n,),
        [SCALARS] + [ANY] * 10 + [fixed(span, z.width), fixed(8, z.width), slot(8, z.ff)],
        [slot(span, z.ff)] * 2,
        [((n, span, z.ff), B)] * 2,
        [
            pltpu.VMEM((n, z.width, z.ff), B),
            pltpu.VMEM((span, z.width), B),
            pltpu.SemaphoreType.DMA((n, 2 * z.m)),
        ],
        "widen",
    )(where, *pieces, normal, vec, bup)


def narrow(z, where, pieces, normal, vec, cot, act, slope):
    n, span, rows, m = z.n, z.span, z.rows, z.m

    def body(where, *refs):
        pcs, refs = refs[:10], refs[10:]
        normal, vec, cot, act, slope = refs[:5]
        out, dres_out, keep, give, dup_out, small_out = refs[5:11]
        w, acc, low, low_t, sems = refs[11:]
        p, t = pl.program_id(0), pl.program_id(1)
        fetch = Pieces(n, m, where, pcs, w, sems, 0, z.ff)

        @pl.when((p == 0) & (t == 0))
        def _():
            fetch.start()

        @pl.when(p == 0)
        def _():
            fetch.wait(t)
            part = dot(act[0], w[t], 1, 1)

            @pl.when(t == 0)
            def _():
                acc[...] = part

            @pl.when(t > 0)
            def _():
                acc[...] += part

        @pl.when((p == 0) & (t == n - 1))
        def _():
            normed = normal[...] * vec[1:2] + vec[2:3]
            second, inverse = norm_stats(acc[...] + vec[3:4] + normed)
            out[...] = (second * vec[4:5] + vec[5:6]).astype(B)
            up = cot[...].astype(F)
            dres = norm_back(second, inverse, vec[4:5], up)
            dres_out[...] = dres
            low[...] = dres.astype(B)
            low_t[...] = dres.T.astype(B)
            small_out[...] = as_rows(
                [
                    jnp.sum(dres, axis=0, keepdims=True),
                    jnp.sum(up * second, axis=0, keepdims=True),
                    jnp.sum(up, axis=0, keepdims=True),
                ],
                3,
            )

        @pl.when(p == 1)
        def _():
            dup_out[0] = (dot(low[...], w[t]) * slope[0].astype(F)).astype(B)
            store_split(dot(low_t[...], act[0]), where, keep, give, m)

    second = lambda *shape: pl.BlockSpec((1,) + shape, lambda p, t: (p * t,) + (0,) * len(shape))
    grads = pl.BlockSpec((m, 1, rows, z.ff), lambda p, t: (0, p * t, 0, 0))
    return call(
        body,
        (2, n),
        [SCALARS]
        + [ANY] * 10
        + [
            fixed(span, z.width),
            fixed(8, z.width),
            fixed(span, z.width),
            pl.BlockSpec((1, span, z.ff), lambda p, t: (t, 0, 0)),
            second(span, z.ff),
        ],
        [fixed(span, z.width), fixed(span, z.width), grads, grads, second(span, z.ff), fixed(8, z.width)],
        [
            ((span, z.width), B),
            ((span, z.width), F),
            ((m, n, rows, z.ff), B),
            ((m, n, rows, z.ff), B),
            ((n, span, z.ff), B),
            ((8, z.width), F),
        ],
        [
            pltpu.VMEM((n, z.width, z.ff), B),
            pltpu.VMEM((span, z.width), F),
            pltpu.VMEM((span, z.width), B),
            pltpu.VMEM((z.width, span), B),
            pltpu.SemaphoreType.DMA((n, 2 * m)),
        ],
        "narrow",
    )(where, *pieces, normal, vec, cot, act, slope)


def widen_back(z, where, pieces, normal, inverse, vec, dup, dres):
    n, span = z.n, z.span

    def body(where, *refs):
        pcs, refs = refs[:10], refs[10:]
        normal, inverse, vec, dup, dres, out, small_out, w, acc, sems = refs
        t = pl.program_id(0)
        fetch = Pieces(n, z.m, where, pcs, w, sems, 0, z.ff)
        pl.when(t == 0)(fetch.start)
        fetch.wait(t)
        part = dot(dup[0], w[t], 1, 1)

        @pl.when(t == 0)
        def _():
            acc[...] = part + dres[...]

        @pl.when(t > 0)
        def _():
            acc[...] += part

        @pl.when(t == n - 1)
        def _():
            up = acc[...]
            back = norm_back(normal[...], inverse[...], vec[1:2], up)
            out[...] = back
            small_out[...] = as_rows(
                [
                    jnp.sum(back, axis=0, keepdims=True),
                    jnp.sum(up * normal[...], axis=0, keepdims=True),
                    jnp.sum(up, axis=0, keepdims=True),
                ],
                0,
            )

    return call(
        body,
        (n,),
        [SCALARS]
        + [ANY] * 10
        + [
            fixed(span, z.width),
            fixed(span, 1),
            fixed(8, z.width),
            slot(span, z.ff),
            fixed(span, z.width),
        ],
        [fixed(span, z.width), fixed(8, z.width)],
        [((span, z.width), F), ((8, z.width), F)],
        [
            pltpu.VMEM((n, z.width, z.ff), B),
            pltpu.VMEM((span, z.width), F),
            pltpu.SemaphoreType.DMA((n, 2 * z.m)),
        ],
        "widen_back",
    )(where, *pieces, normal, inverse, vec, dup, dres)


def attend_back(z, where, pieces, dres, normal, vec, small_a, small_b, dup, mixed, den, qf, q, state, feat):
    n, span, hl, hd, m, rows = z.n, z.span, z.hl, z.hd, z.m, z.rows

    def body(where, *refs):
        pcs, refs = refs[:10], refs[10:]
        dres, normal, vec, small_a, small_b, dup, mixed, den, qf, q, state, feat = refs[:12]
        keep, give, dq_out, dstate_out, w, low, low_t, normed_t, sems = refs[12:]
        t = pl.program_id(0)
        fetch = Pieces(n, m, where, pcs, w, sems, z.ff, z.oc + 64)

        @pl.when(t == 0)
        def _():
            fetch.start()
            low[...] = dres[...].astype(B)
            low_t[...] = dres[...].T.astype(B)
            normed_t[...] = (normal[...] * vec[1:2] + vec[2:3]).T.astype(B)

        fetch.wait(t)
        start = second_start(z.oc)
        d_mixed = dot(low[...], w[t, :, : z.oc]).astype(B).astype(F)
        d_num = d_mixed / den[0]
        d_den = -(d_num * mixed[0].astype(F))
        pair = beside(d_num.astype(B), d_den.astype(B))
        full = dot(pair, qf[0], 0, 0)
        row = jnp.concatenate(
            [
                jnp.sum(
                    full[start + h * hd : start + (h + 1) * hd, h * z.feats : (h + 1) * z.feats],
                    axis=0,
                    keepdims=True,
                )
                for h in range(hl)
            ],
            axis=1,
        )
        dstate_out[0] = jnp.concatenate(
            [diagonal_blocks(full[: z.oc], hl), jnp.broadcast_to(row, (8, z.hm))], axis=0
        ).astype(B)
        compact = state[0, :hd]
        total = jnp.broadcast_to(state[0, hd : hd + 1], (hd, z.hm))
        dash = (dot(pair, stacked(compact, total, hl)) * qf[0].astype(F)).astype(B)
        back = dot(dash, stacked(feat[0], jnp.ones((hd, z.hm), B), hl), 1, 1)
        dq = (back[:, : z.oc] - q[0].astype(F) * back[:, start:]) * z.scale
        dq_out[0] = dq.astype(B)
        grad_up = dot(normed_t[...], dup[0])
        grad_out = dot(low_t[...], mixed[0])
        b_up = jnp.sum(dup[0].astype(F), axis=0, keepdims=True)
        packed = small_a[...] + small_b[...] + as_rows([b_up], 6)
        per = z.width // 64
        one = (iota((rows, 8), 0) // per == iota((rows, 8), 1)).astype(F).astype(B)
        laid = dot(one, packed.astype(B))
        laid = jnp.where(iota(laid.shape, 1) // 64 == iota(laid.shape, 0) % per, laid, 0.0)
        fold = (iota((z.width, 64), 0) % 64 == iota((z.width, 64), 1)).astype(F).astype(B)
        tail = dot(laid.astype(B), fold)
        tail = jnp.concatenate([tail] * (2 * m), axis=0)
        store_split(
            jnp.concatenate([grad_up, jnp.concatenate([grad_out, tail], axis=1)], axis=1),
            where,
            keep,
            give,
            m,
        )

    grads = pl.BlockSpec((m, 1, rows, z.mid_cols), lambda t: (0, t, 0, 0))
    return call(
        body,
        (n,),
        [SCALARS]
        + [ANY] * 10
        + [
            fixed(span, z.width),
            fixed(span, z.width),
            fixed(8, z.width),
            fixed(8, z.width),
            fixed(8, z.width),
            slot(span, z.ff),
            slot(span, z.oc),
            slot(span, z.oc),
            slot(span, z.hm),
            slot(span, z.oc),
            slot(hd + 8, z.hm),
            slot(hd, z.hm),
        ],
        [grads, grads, slot(span, z.oc), slot(hd + 8, z.hm)],
        [
            ((m, n, rows, z.mid_cols), B),
            ((m, n, rows, z.mid_cols), B),
            ((n, span, z.oc), B),
            ((n, hd + 8, z.hm), B),
        ],
        [
            pltpu.VMEM((n, z.width, z.oc + 64), B),
            pltpu.VMEM((span, z.width), B),
            pltpu.VMEM((z.width, span), B),
            pltpu.VMEM((z.width, span), B),
            pltpu.SemaphoreType.DMA((n, 2 * m)),
        ],
        "attend_back",
    )(where, *pieces, dres, normal, vec, small_a, small_b, dup, mixed, den, qf, q, state, feat)


def project_back(z, where, pieces, x, dres, dq, k, v, kf, dstate, feat):
    n, span, hl, hd, m, rows = z.n, z.span, z.hl, z.hd, z.m, z.rows

    def body(where, *refs):
        pcs, refs = refs[:10], refs[10:]
        x, dres, dq, k, v, kf, dstate, feat = refs[:8]
        keep, give, out, w, x_t, acc, sems = refs[8:]
        t = pl.program_id(0)
        fetch = Pieces(n, m, where, pcs, w, sems, 0, z.q_cols)

        @pl.when(t == 0)
        def _():
            fetch.start()
            x_t[...] = x[...].astype(F).T.astype(B)

        start = second_start(z.oc)
        table = block_diagonal(dstate[0, :hd], hl)
        total = dstate[0, hd : hd + 1].astype(F)
        dash = ((dot(v[0], table) + total) * kf[0].astype(F)).astype(B)
        dv = dot(kf[0], table, 1, 1)
        back = dot(dash, stacked(feat[0], jnp.ones((hd, z.hm), B), hl), 1, 1)
        dk = (back[:, : z.oc] - k[0].astype(F) * back[:, start:]) * z.scale
        dqkv = jnp.concatenate(
            [dq[0], dk.astype(B), dv.astype(B), jnp.zeros((span, 64), B)], axis=1
        )
        bias = jnp.sum(dqkv.astype(F), axis=0, keepdims=True)
        laid = jnp.broadcast_to(bias, (rows, z.q_cols))
        laid = jnp.where(iota(laid.shape, 1) // 64 == iota(laid.shape, 0), laid, 0.0)
        a, b = iota((z.q_cols, z.q_cols), 0), iota((z.q_cols, z.q_cols), 1)
        fold = ((b >= z.qc) & (a % 64 == b - z.qc)).astype(F).astype(B)
        tail = dot(laid.astype(B), fold)
        grad = dot(x_t[...], dqkv)
        store_split(grad + jnp.concatenate([tail] * (2 * m), axis=0), where, keep, give, m)
        fetch.wait(t)
        part = dot(dqkv, w[t], 1, 1)

        @pl.when(t == 0)
        def _():
            acc[...] = part + dres[...]

        @pl.when(t > 0)
        def _():
            acc[...] += part

        @pl.when(t == n - 1)
        def _():
            out[...] = acc[...].astype(B)

    grads = pl.BlockSpec((m, 1, rows, z.q_cols), lambda t: (0, t, 0, 0))
    return call(
        body,
        (n,),
        [SCALARS]
        + [ANY] * 10
        + [
            fixed(span, z.width),
            fixed(span, z.width),
            slot(span, z.oc),
            slot(span, z.oc),
            slot(span, z.oc),
            slot(span, z.hm),
            slot(hd + 8, z.hm),
            slot(hd, z.hm),
        ],
        [grads, grads, fixed(span, z.width)],
        [
            ((m, n, rows, z.q_cols), B),
            ((m, n, rows, z.q_cols), B),
            ((span, z.width), B),
        ],
        [
            pltpu.VMEM((n, z.width, z.q_cols), B),
            pltpu.VMEM((z.width, span), B),
            pltpu.VMEM((span, z.width), F),
            pltpu.SemaphoreType.DMA((n, 2 * m)),
        ],
        "project_back",
    )(where, *pieces, x, dres, dq, k, v, kf, dstate, feat)


def place(part, axis, index, count):
    shape = list(part.shape)
    shape[axis] *= count
    return lax.dynamic_update_slice_in_dim(
        jnp.zeros(shape, part.dtype), part, index * part.shape[axis], axis
    )


def on_device(
    sizes,
    tokens,
    lengths,
    features,
    w_qkv,
    b_qkv,
    w_out,
    b_out,
    gain_one,
    shift_one,
    w_up,
    b_up,
    w_down,
    b_down,
    gain_two,
    shift_two,
    cotangent,
):
    links = Links(sizes)
    z = Shape(sizes, features, tokens, b_up)
    n, m, share = z.n, z.m, z.share
    where = jnp.stack([links.s, links.core]).astype(jnp.int32)
    spare = place(b_qkv, 2, links.s, m).reshape(3 * z.hl, z.hd)
    spare = jnp.pad(spare, ((0, share - 3 * z.hl), (0, 0)))
    local = jnp.concatenate([w_qkv.reshape(share, z.qc), spare], axis=1)
    pieces_qkv = links.spread(links.half(local))
    x = links.deal(tokens)
    feat_t = features.transpose(2, 0, 1).reshape(z.hd, z.hm)
    feat_half = links.half(feat_t)
    feat_mine = jnp.stack([feat_half] + [links.perm_t(feat_half, d) for d in range(1, n)])
    feat_other = links.perm_c(feat_mine)
    feat_low = jnp.where(links.core == 0, feat_mine, feat_other)
    feat_high = jnp.where(links.core == 0, feat_other, feat_mine)
    feat = jnp.concatenate([feat_low, feat_high], axis=1)
    vectors = jnp.stack([b_out, gain_one, shift_one, b_down, gain_two, shift_two])
    vectors = jnp.pad(vectors.reshape(6 * share // 64, 64), ((0, 24 - 6 * share // 64), (0, 0)))
    up_bias = place(b_up, 1, links.s, m).reshape(-1, 64)
    spare = jnp.concatenate([vectors, up_bias])
    spare = jnp.pad(spare, ((0, share - spare.shape[0]), (0, 0)))
    local = jnp.concatenate([w_up, w_out.T, spare], axis=1)
    pieces_mid = links.spread(links.half(local))
    pieces_down = links.spread(links.half(w_down.T))
    cot = links.deal(cotangent)
    length = lax.dynamic_index_in_dim(lengths, links.t, 0, keepdims=False)
    order = (links.t - jnp.arange(n)) % n
    position = links.c * z.span + order[:, None] * z.chunk + jnp.arange(z.chunk)[None]
    valid = (position.reshape(-1, 1) < length).astype(F)
    q, k, v, qf, kf, state, top = project(z, where, pieces_qkv, x, feat, valid)
    own_top = top[:, :1]
    most, mask = own_top, 1
    while mask < sizes["context"]:
        other, other_top = links.perm_c(state, mask), links.perm_c(top, mask)[:, :1]
        joint = jnp.maximum(most, other_top)
        state = (
            state.astype(F) * jnp.exp(most - joint) + other.astype(F) * jnp.exp(other_top - joint)
        ).astype(B)
        most, mask = joint, 2 * mask
        top = jnp.broadcast_to(most, top.shape)
    mixed, den, normal, inverse, vec, bup = attend(z, where, pieces_mid, x, qf, state)
    act, slope = widen(z, where, pieces_mid, normal, vec, bup)
    out, d_res_two, keep, give, dup, small_b = narrow(
        z, where, pieces_down, normal, vec, cot, act, slope
    )
    result = links.undeal(out)
    own_down = links.collect(keep, give)
    d_res_one, small_a = widen_back(z, where, pieces_mid, normal, inverse, vec, dup, d_res_two)
    keep, give, dq, d_state = attend_back(
        z, where, pieces_mid, d_res_one, normal, vec, small_a, small_b, dup, mixed, den, qf, q, state, feat
    )
    mask = 1
    while mask < sizes["context"]:
        d_state = wide_add(d_state, links.perm_c(d_state, mask)).astype(B)
        mask *= 2
    d_state = (d_state.astype(F) * jnp.exp(own_top - most)).astype(B)
    own_mid = links.collect(keep, give)
    keep, give, grad_x = project_back(z, where, pieces_qkv, x, d_res_one, dq, k, v, kf, d_state, feat)
    own_qkv = links.collect(keep, give)
    grad_tokens = links.undeal(grad_x).astype(F)
    def mine(value, axis):
        size = value.shape[axis] // m
        return lax.dynamic_slice_in_dim(value, links.s * size, size, axis).astype(F)

    own_b_qkv = mine(own_qkv[: 3 * z.hl, z.qc :].reshape(3, z.hl, z.hd), 2)
    tail = own_mid[: z.rows, z.ff + z.oc :]
    vecs = mine(tail[: 6 * z.width // 64].reshape(6, z.width), 1)
    first = 6 * z.width // 64
    own_b_up = mine(tail[first : first + z.ff // 64].reshape(b_up.shape[0], -1), 1)
    return (
        result,
        grad_tokens,
        own_qkv[:, : z.qc].reshape(w_qkv.shape).astype(F),
        own_b_qkv,
        own_mid[:, z.ff : z.ff + z.oc].T.astype(F),
        vecs[0],
        vecs[1],
        vecs[2],
        own_mid[:, : z.ff].astype(F),
        own_b_up,
        own_down.T.astype(F),
        vecs[3],
        vecs[4],
        vecs[5],
    )


def solution(mesh):
    sizes = dict(mesh.shape)
    in_specs = (
        P("shard", ("context", "tensor"), None),
        P("shard"),
        P("tensor", None, None),
        P("shard", None, "tensor", None),
        P(None, "tensor", "shard"),
        P("tensor", "shard"),
        P("shard"),
        P("shard"),
        P("shard"),
        P("shard", "tensor"),
        P("tensor", "shard"),
        P("tensor", "shard"),
        P("shard"),
        P("shard"),
        P("shard"),
        P("shard", ("context", "tensor"), None),
    )
    out_specs = (
        P("shard", ("context", "tensor"), None),
        P("shard", ("context", "tensor"), None),
        P("shard", None, "tensor", None),
        P(None, "tensor", "shard"),
        P("tensor", "shard"),
        P("shard"),
        P("shard"),
        P("shard"),
        P("shard", "tensor"),
        P("tensor", "shard"),
        P("tensor", "shard"),
        P("shard"),
        P("shard"),
        P("shard"),
    )
    return jax.shard_map(
        functools.partial(on_device, sizes),
        mesh=mesh,
        in_specs=in_specs,
        out_specs=out_specs,
        check_vma=False,
    )
```

```python
import functools

import jax
import jax.numpy as jnp
from jax import lax
from jax.experimental import pallas as pl
from jax.experimental.pallas import tpu as pltpu
from jax.sharding import PartitionSpec as P

F = jnp.float32
B = jnp.bfloat16


def wide_add(*terms):
    total = terms[0].astype(F)
    for term in terms[1:]:
        total = total + term.astype(F)
    return total


def together(*values):
    return lax.optimization_barrier(values)


class Links:
    def __init__(self, sizes):
        self.sizes = sizes
        self.s = lax.axis_index("shard")
        self.c = lax.axis_index("context")
        self.t = lax.axis_index("tensor")
        self.core = self.c % 2

    def perm_t(self, value, step):
        n = self.sizes["tensor"]
        return lax.ppermute(value, "tensor", [(i, (i + step) % n) for i in range(n)])

    def perm_s(self, value, mask):
        n = self.sizes["shard"]
        return lax.ppermute(value, "shard", [(i, i ^ mask) for i in range(n)])

    def perm_c(self, value, mask=1):
        n = self.sizes["context"]
        return lax.ppermute(value, "context", [(i, i ^ mask) for i in range(n)])

    def undeal_some(self, rows, steps):
        n = self.sizes["tensor"]
        rows = rows.reshape(n, rows.shape[0] // n, rows.shape[1])
        return {d: self.perm_t(rows[d], n - d) for d in steps if d < n}

    def undealt(self, rows, moved, dtype):
        n = self.sizes["tensor"]
        rows = rows.reshape(n, rows.shape[0] // n, rows.shape[1])
        return lay(self.t, [rows[0]] + [moved[d] for d in range(1, n)], dtype)

    def half(self, local):
        rows = local.shape[0] // 2
        return lax.dynamic_slice_in_dim(local, self.core * rows, rows, 0)

    def spread_t(self, local):
        n = self.sizes["tensor"]
        return jnp.stack([local] + [self.perm_t(local, d) for d in range(1, n)])

    def spread_near(self, block):
        return self.perm_s(block, 1), self.perm_s(block, 2)

    def spread_far(self, near):
        h = self.sizes["tensor"] // 2
        over_x, over_y = near
        return self.perm_s(over_x[:h], 2), self.perm_s(over_y[h:], 1)

    def carry(self, rows, extra, steps):
        n = self.sizes["tensor"]
        take = lambda d: lax.dynamic_index_in_dim(rows, (self.t + d) % n, 0, keepdims=False)
        return {d: self.perm_t(jnp.concatenate([take(d), extra]), d) for d in steps if d < n}

    def unload(self, rows, extra, moved):
        length = rows.shape[1]
        own = lax.dynamic_index_in_dim(rows, self.t, 0, keepdims=False)
        steps = sorted(moved)
        return (
            jnp.concatenate([own] + [moved[d][:length] for d in steps]),
            jnp.stack([extra] + [moved[d][length:] for d in steps]),
        )

    def swap(self, values):
        return tuple(self.perm_c(value) for value in values)

    def collect_one(self, parts):
        h = parts.shape[1] // 2
        return (
            self.perm_s(jnp.stack([parts[3, h:], parts[1, h:]]), 1),
            self.perm_s(jnp.stack([parts[3, :h], parts[2, :h]]), 2),
        )

    def collect_two(self, parts, one):
        h = parts.shape[1] // 2
        return (
            self.perm_s(wide_add(parts[1, :h], one[1][0]).astype(B), 1),
            self.perm_s(wide_add(parts[2, h:], one[0][0]).astype(B), 2),
        )

    def sums(self, parts, one, two):
        h = parts.shape[1] // 2
        return jnp.concatenate(
            [
                wide_add(parts[0, :h], two[0], one[1][1]).astype(B),
                wide_add(parts[0, h:], one[0][1], two[1]).astype(B),
            ]
        )

    def collect_t(self, total, slots):
        n = self.sizes["tensor"]
        return [self.perm_t(total[i], n - i) for i in slots if i < n]

    def collect_end(self, terms):
        total = wide_add(*terms)
        mask = 2
        while mask < self.sizes["context"]:
            low = total.astype(B)
            total = wide_add(low, self.perm_c(low, mask))
            mask *= 2
        low = total.astype(B)
        other = self.perm_c(low)
        first = jnp.where(self.core == 0, low, other)
        second = jnp.where(self.core == 0, other, low)
        return jnp.concatenate([first, second])


def dot(a, b, ca=1, cb=0):
    return lax.dot_general(a, b, (((ca,), (cb,)), ((), ())), preferred_element_type=F)


def iota(shape, axis):
    return lax.broadcasted_iota(jnp.int32, shape, axis)


def block_diagonal(compact, heads):
    k, m = compact.shape[0], compact.shape[1] // heads
    zero = jnp.zeros((k, m), compact.dtype)
    rows = []
    for h in range(heads):
        row = [zero] * heads
        row[h] = compact[:, h * m : (h + 1) * m]
        rows.append(jnp.concatenate(row, axis=1))
    return jnp.concatenate(rows, axis=0)


def diagonal_blocks(full, heads):
    k, m = full.shape[0] // heads, full.shape[1] // heads
    return jnp.concatenate(
        [full[h * k : (h + 1) * k, h * m : (h + 1) * m] for h in range(heads)], axis=1
    )


def stacked(upper, lower, heads):
    a, b = block_diagonal(upper, heads), block_diagonal(lower, heads)
    gap = jnp.zeros((second_start(a.shape[0]) - a.shape[0], a.shape[1]), a.dtype)
    return jnp.concatenate([a, gap, b], axis=0)


def second_start(width):
    return -(-width // 128) * 128


def beside(left, right):
    gap = jnp.zeros((left.shape[0], second_start(left.shape[1]) - left.shape[1]), left.dtype)
    return jnp.concatenate([left, gap, right], axis=1)


def rows_to_lanes(rows, lanes):
    k = rows.shape[1]
    tile = (iota((k, lanes), 1) % k == iota((k, lanes), 0)).astype(F).astype(B)
    spread = dot(rows, tile)
    hit = iota(spread.shape, 1) // k == iota(spread.shape, 0)
    return jnp.sum(jnp.where(hit, spread, 0.0), axis=0, keepdims=True)


class Pieces:
    def __init__(self, n, m, where, refs, dest, sems, start, cols, slots=None):
        self.n, self.m, self.where, self.refs = n, m, where, refs
        self.slots = slots or range(n)
        self.dest, self.sems, self.start_col, self.cols = dest, sems, start, cols
        self.rows = refs[0].shape[1]

    def copies(self, t):
        s, c = self.where[0], self.where[1]
        made = []
        for i in range(2):
            half = c if i == 0 else 1 - c
            for j in range(self.m):
                row = pl.multiple_of((s ^ j) * (2 * self.rows) + half * self.rows, 8)
                src = self.refs[i * self.m + j].at[t]
                src = src.at[:, pl.ds(self.start_col, self.cols)]
                u = t - self.slots[0]
                target = self.dest.at[u, pl.ds(row, self.rows)]
                made.append(pltpu.make_async_copy(src, target, self.sems.at[u, i * self.m + j]))
        return made

    def start(self):
        for t in self.slots:
            for copy in self.copies(t):
                copy.start()

    def wait(self, t):
        for u in self.slots:

            @pl.when(t == u - self.slots[0])
            def _():
                for copy in self.copies(u):
                    copy.wait()


ANY = pl.BlockSpec(memory_space=pl.ANY)
SCALARS = pl.BlockSpec(memory_space=pltpu.SMEM)


def slot(*shape, first=0):
    zeros = (0,) * len(shape)
    return pl.BlockSpec((1,) + shape, lambda t: (t + first,) + zeros)


def fixed(*shape):
    zeros = (0,) * len(shape)
    return pl.BlockSpec(shape, lambda *_: zeros)


COST = {
    "project": 11,
    "attend": 6,
    "widen": 10,
    "narrow": 13,
    "ffn_grad": 9,
    "widen_back": 10,
    "attend_back": 7,
    "project_back": 11,
}


def call(body, grid, in_specs, out_specs, outs, scratch, name, flops=0):
    return pl.pallas_call(
        body,
        grid=grid,
        in_specs=in_specs,
        out_specs=out_specs,
        out_shape=[jax.ShapeDtypeStruct(s, d) for s, d in outs],
        scratch_shapes=scratch,
        compiler_params=pltpu.CompilerParams(
            dimension_semantics=("arbitrary",) * len(grid), vmem_limit_bytes=60 * 1024 * 1024
        ),
        cost_estimate=pl.CostEstimate(
            flops=COST[name] * 300_000_000, transcendentals=0, bytes_accessed=COST[name] * 800_000
        ),
        name=name,
    )


def lay(t, chunks, dtype):
    n, shape = len(chunks), chunks[0].shape

    def body(t, *refs):
        for d in range(n):

            @pl.when(pl.program_id(0) == d)
            def _():
                refs[n][0] = refs[d][...].astype(dtype)

    return pl.pallas_call(
        body,
        grid_spec=pltpu.PrefetchScalarGridSpec(
            num_scalar_prefetch=1,
            grid=(n,),
            in_specs=[pl.BlockSpec(shape, lambda d, t: (0, 0))] * n,
            out_specs=pl.BlockSpec((1,) + shape, lambda d, t: ((t[0] + d) % n, 0, 0)),
        ),
        out_shape=jax.ShapeDtypeStruct((n,) + shape, dtype),
        cost_estimate=pl.CostEstimate(flops=0, transcendentals=0, bytes_accessed=800_000),
        compiler_params=pltpu.CompilerParams(dimension_semantics=("arbitrary",)),
        name="lay",
    )(t[None].astype(jnp.int32), *chunks)


def norm_stats(res):
    mean = jnp.mean(res, axis=-1, keepdims=True)
    centered = res - mean
    var = jnp.mean(centered * centered, axis=-1, keepdims=True)
    inverse = lax.rsqrt(var + 1e-05)
    return centered * inverse, inverse


def norm_back(normal, inverse, gain, upstream):
    scaled = upstream * gain
    inner = (
        scaled
        - jnp.mean(scaled, axis=-1, keepdims=True)
        - normal * jnp.mean(scaled * normal, axis=-1, keepdims=True)
    )
    return inner * inverse


def as_rows(vectors, first):
    width = vectors[0].shape[1]
    row = iota((8, width), 0)
    total = jnp.zeros((8, width), F)
    for i, vector in enumerate(vectors):
        total = jnp.where(row == first + i, vector, total)
    return total


def store_split(value, where, keep, give, m):
    rows = value.shape[0] // (2 * m)
    s, c = where[0], where[1]
    for half in range(2):
        parts = [value[(2 * i + half) * rows : (2 * i + half + 1) * rows].astype(B) for i in range(m)]

        @pl.when(c == half)
        def _():
            for i in range(m):
                keep[s ^ i, 0] = parts[i]

        @pl.when(c != half)
        def _():
            for i in range(m):
                give[s ^ i, 0] = parts[i]


class Shape:
    def __init__(self, sizes, features, tokens, b_up):
        self.n, self.m = sizes["tensor"], sizes["shard"]
        self.hl, self.feats, self.hd = features.shape
        self.chunk, self.width = tokens.shape[1], tokens.shape[2]
        self.span = self.chunk * self.n
        self.share = self.width // self.m
        self.rows = self.share // 2
        self.oc = self.hl * self.hd
        self.qc = 3 * self.oc
        self.hm = self.hl * self.feats
        self.ff = b_up.size * self.m
        self.q_cols = self.qc + 64
        self.a_cols = self.q_cols + self.oc + 64
        self.scale = self.hd ** (-0.25)


def project(z, where, pieces, x, feat, valid, slots):
    cnt, first = len(slots), slots[0]
    n, span, hl, feats, hd = z.n, z.span, z.hl, z.feats, z.hd

    def body(where, *refs):
        pcs, refs = refs[:8], refs[8:]
        x, feat, valid, q_out, k_out, v_out, qf_out, kf_out, st_out, top_out, w, sems = refs
        t = pl.program_id(0)
        fetch = Pieces(n, z.m, where, pcs, w, sems, 0, z.q_cols, slots)
        pl.when(t == 0)(fetch.start)
        fetch.wait(t)
        bias = jnp.zeros((16, 64), F)
        for s in range(z.m):
            bias = bias + w[t, s * z.share : s * z.share + 16, z.qc :].astype(F)
        qkv = dot(x[...], w[t, :, : z.qc]) + rows_to_lanes(bias.astype(B), z.qc)
        q = (qkv[:, : z.oc] * z.scale).astype(B)
        k = (qkv[:, z.oc : 2 * z.oc] * z.scale).astype(B)
        v = qkv[:, 2 * z.oc :].astype(B)
        q_out[0], k_out[0], v_out[0] = q, k, v
        table = block_diagonal(feat[0], hl)
        qd, kd = dot(q, table), dot(k, table)
        qs, ks = q.astype(F), k.astype(F)
        qs, ks = qs * qs, ks * ks
        live = valid[...] > 0
        kfs, tops = [], []
        for h in range(hl):
            seg, cols = slice(h * hd, (h + 1) * hd), slice(h * feats, (h + 1) * feats)
            dash = qd[:, cols] - 0.5 * jnp.sum(qs[:, seg], axis=-1, keepdims=True)
            qf_out[0, :, cols] = jnp.exp(
                dash - jnp.floor(jnp.max(dash, axis=-1, keepdims=True))
            ).astype(B)
            dash = kd[:, cols] - 0.5 * jnp.sum(ks[:, seg], axis=-1, keepdims=True)
            top = jnp.max(jnp.where(live, dash, -1e30), axis=0, keepdims=True)
            top = jnp.floor(jnp.max(top, axis=1, keepdims=True))
            kf = jnp.where(live, jnp.exp(dash - top), 0.0).astype(B)
            kf_out[0, :, cols] = kf
            kfs.append(kf)
            tops.append(jnp.broadcast_to(top, (8, feats)))
        top = jnp.concatenate(tops, axis=1)
        top_out[0] = top
        vx = jnp.concatenate([v, jnp.ones((span, 64), B)], axis=1)
        state = dot(vx, jnp.concatenate(kfs, axis=1), 0, 0)
        high = top.astype(B).astype(F)
        mid = (top - high).astype(B).astype(F)
        row, last = iota((8, z.hm), 0), state[z.oc : z.oc + 8]
        for i, term in enumerate((high, mid, top - high - mid)):
            last = jnp.where(row == i + 1, term, last)
        st_out[0] = jnp.concatenate([diagonal_blocks(state[: z.oc], hl), last], axis=0).astype(B)

    return call(
        body,
        (cnt,),
        [SCALARS] + [ANY] * 8 + [fixed(span, z.width), slot(hd, z.hm, first=first), fixed(span, 1)],
        [slot(span, z.oc)] * 3 + [slot(span, z.hm)] * 2 + [slot(hd + 8, z.hm), slot(8, z.hm)],
        [((cnt, span, z.oc), B)] * 3
        + [((cnt, span, z.hm), B)] * 2
        + [((cnt, hd + 8, z.hm), B), ((cnt, 8, z.hm), F)],
        [pltpu.VMEM((cnt, z.width, z.q_cols), B), pltpu.SemaphoreType.DMA((cnt, 2 * z.m))],
        "project",
    )(where, *pieces, x, feat, valid)


def attend(z, where, pieces, qf, state, slots, x=None, before=None):
    cnt, first, last = len(slots), slots[0], x is not None
    n, span, hl, hd = z.n, z.span, z.hl, z.hd

    def body(where, *refs):
        pcs, refs = refs[:8], refs[8:]
        qf, state, refs = refs[0], refs[1], refs[2:]
        if last:
            x, before, refs = refs[0], refs[1], refs[2:]
        mixed_out, den_out, bup_out, refs = refs[0], refs[1], refs[2], refs[3:]
        if last:
            normal_out, inverse_out, vec_out, w, acc, sems = refs
        else:
            acc, w, sems = refs
        t = pl.program_id(0)
        fetch = Pieces(n, z.m, where, pcs, w, sems, z.q_cols, z.oc + 64, slots)
        pl.when(t == 0)(fetch.start)
        compact = state[0, :hd]
        total = jnp.broadcast_to(state[0, hd : hd + 1], (hd, z.hm))
        table = stacked(compact, total, hl)
        both = dot(qf[0], table, 1, 1)
        den = both[:, second_start(z.oc) :]
        mixed = (both[:, : z.oc] / den).astype(B)
        mixed_out[0] = mixed
        den_out[0] = den
        fetch.wait(t)
        part = dot(mixed, w[t, :, : z.oc], 1, 1)

        @pl.when(t == 0)
        def _():
            acc[...] = part + before[...] if last else part

        @pl.when(t > 0)
        def _():
            acc[...] += part

        bias = jnp.zeros((16, 64), F)
        for s in range(z.m):
            bias = bias + w[t, s * z.share + 24 : s * z.share + 40, z.oc :].astype(F)
        bup_out[0] = jnp.broadcast_to(rows_to_lanes(bias.astype(B), z.ff), (8, z.ff))
        if not last:
            return

        @pl.when(t == cnt - 1)
        def _():
            lanes = z.width
            per = z.share // 64
            tile = (iota((64, lanes), 1) % 64 == iota((64, lanes), 0)).astype(F).astype(B)
            found = jnp.zeros((24, lanes), F)
            for s in range(z.m):
                spread = dot(w[0, s * z.share : s * z.share + 24, z.oc :], tile)
                hit = iota((24, lanes), 1) // 64 == per * s + iota((24, lanes), 0) % per
                found = found + jnp.where(hit, spread, 0.0)
            pick = (iota((8, 24), 1) // per == iota((8, 24), 0)).astype(F).astype(B)
            vec = dot(pick, found.astype(B))
            vec_out[...] = vec
            res = acc[...] + vec[0:1] + x[...].astype(F)
            normal, inverse = norm_stats(res)
            normal_out[...] = normal
            inverse_out[...] = inverse

    wide = fixed(span, z.width)
    ins, extra = [slot(span, z.hm), slot(hd + 8, z.hm)], []
    outs = [slot(span, z.oc), slot(span, z.oc), slot(8, z.ff)]
    shapes = [((cnt, span, z.oc), B), ((cnt, span, z.oc), F), ((cnt, 8, z.ff), F)]
    scratch = [pltpu.VMEM((cnt, z.width, z.oc + 64), B)]
    if last:
        ins, extra = ins + [wide, wide], [x, before]
        outs += [wide, fixed(span, 1), fixed(8, z.width)]
        shapes += [((span, z.width), F), ((span, 1), F), ((8, z.width), F)]
        scratch += [pltpu.VMEM((span, z.width), F)]
    else:
        outs, shapes = outs + [wide], shapes + [((span, z.width), F)]
    return call(
        body,
        (cnt,),
        [SCALARS] + [ANY] * 8 + ins,
        outs,
        shapes,
        scratch + [pltpu.SemaphoreType.DMA((cnt, 2 * z.m))],
        "attend",
    )(where, *pieces, qf, state, *extra)


def widen(z, where, pieces, normal, vec, bup):
    n, span = z.n, z.span

    def body(where, *refs):
        pcs, refs = refs[:8], refs[8:]
        normal, vec, bup, act_out, slope_out, w, low, sems = refs
        t = pl.program_id(0)
        fetch = Pieces(n, z.m, where, pcs, w, sems, 0, z.ff)

        @pl.when(t == 0)
        def _():
            fetch.start()
            low[...] = (normal[...] * vec[1:2] + vec[2:3]).astype(B)

        fetch.wait(t)
        up = dot(low[...], w[t]) + bup[0, 0:1]
        share = 0.5 * (1.0 + lax.erf(up * 0.7071067811865476))
        act_out[0] = (up * share).astype(B)
        slope_out[0] = (share + up * jnp.exp(-0.5 * up * up) * 0.3989422804014327).astype(B)

    return call(
        body,
        (n,),
        [SCALARS] + [ANY] * 8 + [fixed(span, z.width), fixed(8, z.width), slot(8, z.ff)],
        [slot(span, z.ff)] * 2,
        [((n, span, z.ff), B)] * 2,
        [
            pltpu.VMEM((n, z.width, z.ff), B),
            pltpu.VMEM((span, z.width), B),
            pltpu.SemaphoreType.DMA((n, 2 * z.m)),
        ],
        "widen",
    )(where, *pieces, normal, vec, bup)


def narrow(z, where, pieces, normal, vec, cot, act, slope):
    n, span, rows, m = z.n, z.span, z.rows, z.m

    def body(where, *refs):
        pcs, refs = refs[:8], refs[8:]
        normal, vec, cot, act, slope = refs[:5]
        out, dres_out, low, dup_out, small_out = refs[5:10]
        w, acc, sems = refs[10:]
        p, t = pl.program_id(0), pl.program_id(1)
        fetch = Pieces(n, m, where, pcs, w, sems, 0, z.ff)

        @pl.when((p == 0) & (t == 0))
        def _():
            fetch.start()

        @pl.when(p == 0)
        def _():
            fetch.wait(t)
            part = dot(act[0], w[t], 1, 1)

            @pl.when(t == 0)
            def _():
                acc[...] = part

            @pl.when(t > 0)
            def _():
                acc[...] += part

        @pl.when((p == 0) & (t == n - 1))
        def _():
            normed = normal[...] * vec[1:2] + vec[2:3]
            second, inverse = norm_stats(acc[...] + vec[3:4] + normed)
            out[...] = (second * vec[4:5] + vec[5:6]).astype(B)
            up = cot[...].astype(F)
            dres = norm_back(second, inverse, vec[4:5], up)
            dres_out[...] = dres
            low[...] = dres.astype(B)
            small_out[...] = as_rows(
                [
                    jnp.sum(dres, axis=0, keepdims=True),
                    jnp.sum(up * second, axis=0, keepdims=True),
                    jnp.sum(up, axis=0, keepdims=True),
                ],
                3,
            )

        @pl.when(p == 1)
        def _():
            dup_out[0] = (dot(low[...], w[t]) * slope[0].astype(F)).astype(B)

    second = lambda *shape: pl.BlockSpec((1,) + shape, lambda p, t: (p * t,) + (0,) * len(shape))
    return call(
        body,
        (2, n),
        [SCALARS]
        + [ANY] * 8
        + [
            fixed(span, z.width),
            fixed(8, z.width),
            fixed(span, z.width),
            pl.BlockSpec((1, span, z.ff), lambda p, t: (t * (1 - p) + (n - 1) * p, 0, 0)),
            second(span, z.ff),
        ],
        [fixed(span, z.width)] * 3 + [second(span, z.ff), fixed(8, z.width)],
        [
            ((span, z.width), B),
            ((span, z.width), F),
            ((span, z.width), B),
            ((n, span, z.ff), B),
            ((8, z.width), F),
        ],
        [
            pltpu.VMEM((n, z.width, z.ff), B),
            pltpu.VMEM((span, z.width), F),
            pltpu.SemaphoreType.DMA((n, 2 * m)),
        ],
        "narrow",
    )(where, *pieces, normal, vec, cot, act, slope)


def ffn_grad(z, where, normal, vec, d_ffn, act, dup):
    n, span, rows, m = z.n, z.span, z.rows, z.m

    def body(where, normal, vec, d_ffn, act, dup, keep, give, bup_out, low_t, normed_t):
        t = pl.program_id(0)

        @pl.when(t == 0)
        def _():
            low_t[...] = d_ffn[...].astype(F).T.astype(B)
            normed_t[...] = (normal[...] * vec[1:2] + vec[2:3]).T.astype(B)

        down, up = dot(low_t[...], act[0]), dot(normed_t[...], dup[0])
        store_split(jnp.concatenate([down, up], axis=1), where, keep, give, m)
        bup_out[0] = jnp.broadcast_to(
            jnp.sum(dup[0].astype(F), axis=0, keepdims=True), (8, z.ff)
        )

    wide, grads = fixed(span, z.width), pl.BlockSpec((m, 1, rows, 2 * z.ff), lambda t: (0, t, 0, 0))
    return call(
        body,
        (n,),
        [SCALARS, wide, fixed(8, z.width), wide, slot(span, z.ff), slot(span, z.ff)],
        [grads, grads, slot(8, z.ff)],
        [((m, n, rows, 2 * z.ff), B)] * 2 + [((n, 8, z.ff), F)],
        [pltpu.VMEM((z.width, span), B)] * 2,
        "ffn_grad",
    )(where, normal, vec, d_ffn, act, dup)


def widen_back(z, where, pieces, normal, inverse, vec, dup, dres):
    n, span = z.n, z.span

    def body(where, *refs):
        pcs, refs = refs[:8], refs[8:]
        normal, inverse, vec, dup, dres, out, small_out, w, acc, sems = refs
        t = pl.program_id(0)
        fetch = Pieces(n, z.m, where, pcs, w, sems, 0, z.ff)
        pl.when(t == 0)(fetch.start)
        fetch.wait(t)
        part = dot(dup[0], w[t], 1, 1)

        @pl.when(t == 0)
        def _():
            acc[...] = part + dres[...]

        @pl.when(t > 0)
        def _():
            acc[...] += part

        @pl.when(t == n - 1)
        def _():
            up = acc[...]
            back = norm_back(normal[...], inverse[...], vec[1:2], up)
            out[...] = back
            small_out[...] = as_rows(
                [
                    jnp.sum(back, axis=0, keepdims=True),
                    jnp.sum(up * normal[...], axis=0, keepdims=True),
                    jnp.sum(up, axis=0, keepdims=True),
                ],
                0,
            )

    return call(
        body,
        (n,),
        [SCALARS]
        + [ANY] * 8
        + [
            fixed(span, z.width),
            fixed(span, 1),
            fixed(8, z.width),
            slot(span, z.ff),
            fixed(span, z.width),
        ],
        [fixed(span, z.width), fixed(8, z.width)],
        [((span, z.width), F), ((8, z.width), F)],
        [
            pltpu.VMEM((n, z.width, z.ff), B),
            pltpu.VMEM((span, z.width), F),
            pltpu.SemaphoreType.DMA((n, 2 * z.m)),
        ],
        "widen_back",
    )(where, *pieces, normal, inverse, vec, dup, dres)


def attend_back(z, where, pieces, dres, mixed, den, qf, q, state, feat, slots):
    cnt, first = len(slots), slots[0]
    n, span, hl, hd, m = z.n, z.span, z.hl, z.hd, z.m

    def body(where, *refs):
        pcs, refs = refs[:8], refs[8:]
        dres, mixed, den, qf, q, state, feat, dq_out, dstate_out, w, low, sems = refs
        t = pl.program_id(0)
        fetch = Pieces(n, m, where, pcs, w, sems, z.q_cols, z.oc + 64, slots)

        @pl.when(t == 0)
        def _():
            fetch.start()
            low[...] = dres[...].astype(B)

        fetch.wait(t)
        start = second_start(z.oc)
        d_mixed = dot(low[...], w[t, :, : z.oc]).astype(B).astype(F)
        d_num = d_mixed / den[0]
        d_den = -(d_num * mixed[0].astype(F))
        pair = beside(d_num.astype(B), d_den.astype(B))
        full = dot(pair, qf[0], 0, 0)
        row = jnp.concatenate(
            [
                jnp.sum(
                    full[start + h * hd : start + (h + 1) * hd, h * z.feats : (h + 1) * z.feats],
                    axis=0,
                    keepdims=True,
                )
                for h in range(hl)
            ],
            axis=1,
        )
        dstate_out[0] = jnp.concatenate(
            [diagonal_blocks(full[: z.oc], hl), jnp.broadcast_to(row, (8, z.hm))], axis=0
        ).astype(B)
        compact = state[0, :hd]
        total = jnp.broadcast_to(state[0, hd : hd + 1], (hd, z.hm))
        dash = (dot(pair, stacked(compact, total, hl)) * qf[0].astype(F)).astype(B)
        back = dot(dash, stacked(feat[0], jnp.ones((hd, z.hm), B), hl), 1, 1)
        dq = (back[:, : z.oc] - q[0].astype(F) * back[:, start:]) * z.scale
        dq_out[0] = dq.astype(B)

    return call(
        body,
        (cnt,),
        [SCALARS]
        + [ANY] * 8
        + [
            fixed(span, z.width),
            slot(span, z.oc),
            slot(span, z.oc),
            slot(span, z.hm),
            slot(span, z.oc),
            slot(hd + 8, z.hm),
            slot(hd, z.hm, first=first),
        ],
        [slot(span, z.oc), slot(hd + 8, z.hm)],
        [((cnt, span, z.oc), B), ((cnt, hd + 8, z.hm), B)],
        [
            pltpu.VMEM((cnt, z.width, z.oc + 64), B),
            pltpu.VMEM((span, z.width), B),
            pltpu.SemaphoreType.DMA((cnt, 2 * m)),
        ],
        "attend_back",
    )(where, *pieces, dres, mixed, den, qf, q, state, feat)


def project_back(z, where, pieces, x, dres, dq, k, v, kf, dstate, feat, mixed, small_a, small_b, dbup, slots, before=None):
    cnt, first, last = len(slots), slots[0], before is not None
    n, span, hl, hd, m, rows = z.n, z.span, z.hl, z.hd, z.m, z.rows
    cols = z.a_cols

    def body(where, *refs):
        pcs, refs = refs[:8], refs[8:]
        x, dres, dq, k, v, kf, dstate, feat, mixed, small_a, small_b, dbup = refs[:12]
        refs = refs[12:]
        if last:
            before, refs = refs[0], refs[1:]
            keep, give, out, w, x_t, low_t, acc, sems = refs
        else:
            keep, give, acc, w, x_t, low_t, sems = refs
        t = pl.program_id(0)
        fetch = Pieces(n, m, where, pcs, w, sems, 0, z.q_cols, slots)

        @pl.when(t == 0)
        def _():
            fetch.start()
            x_t[...] = x[...].astype(F).T.astype(B)
            low_t[...] = dres[...].T.astype(B)

        start = second_start(z.oc)
        table = block_diagonal(dstate[0, :hd], hl)
        total = dstate[0, hd : hd + 1].astype(F)
        dash = ((dot(v[0], table) + total) * kf[0].astype(F)).astype(B)
        dv = dot(kf[0], table, 1, 1)
        back = dot(dash, stacked(feat[0], jnp.ones((hd, z.hm), B), hl), 1, 1)
        dk = (back[:, : z.oc] - k[0].astype(F) * back[:, start:]) * z.scale
        dqkv = jnp.concatenate(
            [dq[0], dk.astype(B), dv.astype(B), jnp.zeros((span, 64), B)], axis=1
        )
        bias = jnp.sum(dqkv.astype(F), axis=0, keepdims=True)
        laid = jnp.broadcast_to(bias, (rows, z.q_cols))
        laid = jnp.where(iota(laid.shape, 1) // 64 == iota(laid.shape, 0), laid, 0.0)
        a, b = iota((z.q_cols, z.q_cols), 0), iota((z.q_cols, z.q_cols), 1)
        fold = ((b >= z.qc) & (a % 64 == b - z.qc)).astype(F).astype(B)
        tail = dot(laid.astype(B), fold)
        grad = dot(x_t[...], dqkv) + jnp.concatenate([tail] * (2 * m), axis=0)
        grad_out = dot(low_t[...], mixed[0])
        packed = small_a[...] + small_b[...] + as_rows([dbup[0, 0:1]], 6)
        per = z.width // 64
        one = (iota((rows, 8), 0) // per == iota((rows, 8), 1)).astype(F).astype(B)
        laid = dot(one, packed.astype(B))
        laid = jnp.where(iota(laid.shape, 1) // 64 == iota(laid.shape, 0) % per, laid, 0.0)
        fold = (iota((z.width, 64), 0) % 64 == iota((z.width, 64), 1)).astype(F).astype(B)
        tail = dot(laid.astype(B), fold)
        tail = jnp.concatenate([tail] * (2 * m), axis=0)
        store_split(
            jnp.concatenate([grad, jnp.concatenate([grad_out, tail], axis=1)], axis=1),
            where,
            keep,
            give,
            m,
        )
        fetch.wait(t)
        part = dot(dqkv, w[t], 1, 1)

        @pl.when(t == 0)
        def _():
            acc[...] = part + (before[...] if last else dres[...])

        @pl.when(t > 0)
        def _():
            acc[...] += part

        if last:

            @pl.when(t == cnt - 1)
            def _():
                out[...] = acc[...].astype(B)

    grads = pl.BlockSpec((m, 1, rows, cols), lambda t: (0, t, 0, 0))
    wide, scratch = fixed(span, z.width), [pltpu.VMEM((cnt, z.width, z.q_cols), B)]
    scratch += [pltpu.VMEM((z.width, span), B)] * 2
    if last:
        scratch += [pltpu.VMEM((span, z.width), F)]
    return call(
        body,
        (cnt,),
        [SCALARS]
        + [ANY] * 8
        + [
            wide,
            wide,
            slot(span, z.oc),
            slot(span, z.oc),
            slot(span, z.oc),
            slot(span, z.hm),
            slot(hd + 8, z.hm),
            slot(hd, z.hm, first=first),
            slot(span, z.oc),
            fixed(8, z.width),
            fixed(8, z.width),
            slot(8, z.ff, first=first),
        ]
        + ([wide] if last else []),
        [grads, grads, wide],
        [((m, cnt, rows, cols), B)] * 2 + [((span, z.width), B if last else F)],
        scratch + [pltpu.SemaphoreType.DMA((cnt, 2 * m))],
        "project_back",
    )(
        where, *pieces, x, dres, dq, k, v, kf, dstate, feat, mixed, small_a, small_b, dbup,
        *([before] if last else []),
    )


def place(part, axis, index, count):
    shape = list(part.shape)
    shape[axis] *= count
    return lax.dynamic_update_slice_in_dim(
        jnp.zeros(shape, part.dtype), part, index * part.shape[axis], axis
    )


def on_device(
    sizes,
    tokens,
    lengths,
    features,
    w_qkv,
    b_qkv,
    w_out,
    b_out,
    gain_one,
    shift_one,
    w_up,
    b_up,
    w_down,
    b_down,
    gain_two,
    shift_two,
    cotangent,
):
    links = Links(sizes)
    z = Shape(sizes, features, tokens, b_up)
    n, m, share = z.n, z.m, z.share
    where = jnp.stack([links.s, links.core]).astype(jnp.int32)
    def tall(value):
        return jnp.pad(value, ((0, share - value.shape[0]), (0, 0)))

    biases = place(b_qkv, 2, links.s, m).reshape(3 * z.hl, z.hd)
    vectors = b_out[None]
    for i, vector in enumerate((gain_one, shift_one, b_down, gain_two, shift_two)):
        vectors = jnp.where(jnp.arange(6)[:, None] == i + 1, vector[None], vectors)
    vectors = jnp.pad(vectors.reshape(6 * share // 64, 64), ((0, 24 - 6 * share // 64), (0, 0)))
    vectors = jnp.concatenate([vectors, place(b_up, 1, links.s, m).reshape(-1, 64)])
    local_a = links.half(
        jnp.concatenate([w_qkv.reshape(share, z.qc), tall(biases), w_out.T, tall(vectors)], axis=1)
    )
    feat_half = links.half(features.transpose(2, 0, 1).reshape(z.hd, z.hm))
    local_u, local_d = links.half(w_up), links.half(w_down.T)
    length = lax.dynamic_index_in_dim(lengths, links.t, 0, keepdims=False)
    order = (links.t - jnp.arange(n)) % n
    position = links.c * z.span + order[:, None] * z.chunk + jnp.arange(z.chunk)[None]
    valid = (position.reshape(-1, 1) < length).astype(F)
    halves = (range(n // 2), range(n // 2, n))
    lo, hi = halves

    def join_states(state, top, came):
        row, mask = z.hd + 1, 1
        own = most = top[:, :1]
        while mask < sizes["context"]:
            if mask > 1:
                came = links.perm_c(state, mask), links.perm_c(top, mask)
                other, other_top = came[0], came[1][:, :1]
            else:
                other = came
                other_top = wide_add(*[other[:, row + i : row + i + 1] for i in range(3)])
            joint = jnp.maximum(most, other_top)
            state = (
                state.astype(F) * jnp.exp(most - joint) + other.astype(F) * jnp.exp(other_top - joint)
            ).astype(B)
            most, mask = joint, 2 * mask
            top = jnp.broadcast_to(most, top.shape)
        return state, jnp.exp(own - most)

    def join_grads(state, came, fall):
        mask = 1
        while mask < sizes["context"]:
            other = came if mask == 1 else links.perm_c(state, mask)
            state = wide_add(state, other).astype(B)
            mask *= 2
        return (state.astype(F) * fall).astype(B)

    block_a = links.spread_t(local_a)
    block_a, tokens, feat_half = together(block_a, tokens, feat_half)
    near_a = links.spread_near(block_a)
    moved = links.carry(tokens, feat_half, range(1, n))
    block_a, near_a, moved, local_u, tokens, feat_half = together(
        block_a, near_a, moved, local_u, tokens, feat_half
    )
    far_a = links.spread_far(near_a)
    other_a = links.swap((block_a,) + near_a)
    x, feat_mine = links.unload(tokens, feat_half, moved)
    far_a, feat_mine, other_a, local_u, valid, x = together(far_a, feat_mine, other_a, local_u, valid, x)
    far_a = (jnp.concatenate(far_a),)
    other_a += links.swap(far_a)
    feat_other = links.perm_c(feat_mine)
    feat_low = jnp.where(links.core == 0, feat_mine, feat_other)
    feat_high = jnp.where(links.core == 0, feat_other, feat_mine)
    feat = jnp.concatenate([feat_low, feat_high], axis=1)
    feat, other_a, local_u = together(feat, other_a, local_u)
    pieces_a = (block_a,) + near_a + far_a + other_a
    block_u = links.spread_t(local_u)
    first = project(z, where, pieces_a, x, feat, valid, lo)
    first, block_u, local_d, valid, cot = together(first, block_u, local_d, valid, cotangent)
    near_u = links.spread_near(block_u)
    moved = links.carry(cot, local_d, (2,))
    other_u = links.swap((block_u,))
    came = links.perm_c(first[5])
    second = project(z, where, pieces_a, x, feat, valid, hi)
    first, second, near_u, block_u, other_u, moved, came, cot, local_d = together(
        first, second, near_u, block_u, other_u, moved, came, cot, local_d
    )
    made = (first, second)
    far_u = links.spread_far(near_u)
    moved.update(links.carry(cot, local_d, (1, 3)))
    came_b = links.perm_c(second[5])
    state_a, fall_a = join_states(first[5], first[6], came)
    one = attend(z, where, pieces_a, first[3], state_a, lo)
    one, far_u, near_u, other_u, moved, came_b, cot, local_d = together(
        one, far_u, near_u, other_u, moved, came_b, cot, local_d
    )
    mixed_a, den_a, bup_a, acc = one
    far_u = (jnp.concatenate(far_u),)
    cot, block_d = links.unload(cot, local_d, moved)
    near_d = links.spread_near(block_d)
    other_u += links.swap(near_u + far_u)
    state_b, fall_b = join_states(second[5], second[6], came_b)
    two = attend(z, where, pieces_a, second[3], state_b, hi, x, acc)
    two, near_d, block_d, other_u, cot = together(two, near_d, block_d, other_u, cot)
    mixed_b, den_b, bup_b, normal, inverse, vec = two
    states, falls = (state_a, state_b), (fall_a, fall_b)
    bup = jnp.concatenate([bup_a, bup_b])
    mixed, den = (mixed_a, mixed_b), (den_a, den_b)
    pieces_u = (block_u,) + near_u + far_u + other_u
    far_d = links.spread_far(near_d)
    other_d = links.swap((block_d,) + near_d)
    act, slope = widen(z, where, pieces_u, normal, vec, bup)
    act, slope, far_d, other_d = together(act, slope, far_d, other_d)
    far_d = (jnp.concatenate(far_d),)
    other_d += links.swap(far_d)
    pieces_d = (block_d,) + near_d + far_d + other_d
    out, d_res_two, d_ffn, dup, small_b = narrow(
        z, where, pieces_d, normal, vec, cot, act, slope
    )
    sent = links.undeal_some(out, (2,))
    keep, give, dbup = ffn_grad(z, where, normal, vec, d_ffn, act, dup)
    keep, give, out, dup, sent = together(keep, give, out, dup, sent)
    other = links.perm_c(give)
    sent.update(links.undeal_some(out, (1, 3)))
    d_res_one, small_a = widen_back(z, where, pieces_u, normal, inverse, vec, dup, d_res_two)
    d_res_one, keep, other, sent = together(d_res_one, keep, other, sent)
    result = links.undealt(out, sent, B)
    parts_f = wide_add(keep, other).astype(B)
    one_f = links.collect_one(parts_f)
    dq_a, d_state_a = attend_back(
        z, where, pieces_a, d_res_one, mixed[0], den[0], made[0][3], made[0][0], states[0], feat, lo
    )
    dq_a, d_state_a, d_res_one, parts_f = together(dq_a, d_state_a, d_res_one, parts_f)
    came = links.perm_c(d_state_a)
    dq_b, d_state_b = attend_back(
        z, where, pieces_a, d_res_one, mixed[1], den[1], made[1][3], made[1][0], states[1], feat, hi
    )
    dq_b, d_state_b, came, one_f, parts_f, x = together(dq_b, d_state_b, came, one_f, parts_f, x)
    two_f = links.collect_two(parts_f, one_f)
    came_b = links.perm_c(d_state_b)
    d_state_a = join_grads(d_state_a, came, falls[0])
    dq = (dq_a, dq_b)

    def run_back(i, d_state, x, before):
        return project_back(
            z, where, pieces_a, x, d_res_one, dq[i], made[i][1], made[i][2], made[i][4],
            d_state, feat, mixed[i], small_a, small_b, dbup, halves[i], before,
        )

    keep, give, acc = run_back(0, d_state_a, x, None)
    keep, give, acc, two_f, came_b, parts_f, x = together(keep, give, acc, two_f, came_b, parts_f, x)
    sums_f = links.sums(parts_f, one_f, two_f)
    terms_f = links.collect_t(sums_f, (1, 2))
    other = links.perm_c(give)
    d_state_b = join_grads(d_state_b, came_b, falls[1])
    keep_b, give_b, grad_x = run_back(1, d_state_b, x, acc)
    keep_b, give_b, grad_x, keep, other, terms_f, sums_f = together(
        keep_b, give_b, grad_x, keep, other, terms_f, sums_f
    )
    other_b = links.perm_c(give_b)
    terms_f += links.collect_t(sums_f, range(3, n))
    parts = wide_add(keep, other).astype(B)
    parts_b = wide_add(keep_b, other_b).astype(B)
    parts, grad_x = together(jnp.concatenate([parts, parts_b], axis=1), grad_x)
    one = links.collect_one(parts)
    sent = links.undeal_some(grad_x, (2,))
    one, parts, sent, grad_x, terms_f = together(one, parts, sent, grad_x, terms_f)
    two = links.collect_two(parts, one)
    sent.update(links.undeal_some(grad_x, (1, 3)))
    two, one, parts, sent, grad_x = together(two, one, parts, sent, grad_x)
    grad_tokens = links.undealt(grad_x, sent, F)
    sums = links.sums(parts, one, two)
    terms = [sums[0]] + links.collect_t(sums, range(1, n))
    terms_f = [sums_f[0]] + terms_f
    own_ffn = links.collect_end(terms_f)
    own_qkv = links.collect_end(terms)
    def mine(value, axis):
        size = value.shape[axis] // m
        return lax.dynamic_slice_in_dim(value, links.s * size, size, axis).astype(F)

    own_b_qkv = mine(own_qkv[: 3 * z.hl, z.qc : z.q_cols].reshape(3, z.hl, z.hd), 2)
    own_out = own_qkv[:, z.q_cols : z.q_cols + z.oc]
    tail = own_qkv[: z.rows, z.q_cols + z.oc :]
    vecs = mine(tail[: 6 * z.width // 64].reshape(6, z.width), 1)
    start = 6 * z.width // 64
    own_b_up = mine(tail[start : start + z.ff // 64].reshape(b_up.shape[0], -1), 1)
    return (
        result,
        grad_tokens,
        own_qkv[:, : z.qc].reshape(w_qkv.shape).astype(F),
        own_b_qkv,
        own_out.T.astype(F),
        vecs[0],
        vecs[1],
        vecs[2],
        own_ffn[:, z.ff :].astype(F),
        own_b_up,
        own_ffn[:, : z.ff].T.astype(F),
        vecs[3],
        vecs[4],
        vecs[5],
    )


def solution(mesh):
    sizes = dict(mesh.shape)
    in_specs = (
        P("shard", ("context", "tensor"), None),
        P("shard"),
        P("tensor", None, None),
        P("shard", None, "tensor", None),
        P(None, "tensor", "shard"),
        P("tensor", "shard"),
        P("shard"),
        P("shard"),
        P("shard"),
        P("shard", "tensor"),
        P("tensor", "shard"),
        P("tensor", "shard"),
        P("shard"),
        P("shard"),
        P("shard"),
        P("shard", ("context", "tensor"), None),
    )
    out_specs = (
        P("shard", ("context", "tensor"), None),
        P("shard", ("context", "tensor"), None),
        P("shard", None, "tensor", None),
        P(None, "tensor", "shard"),
        P("tensor", "shard"),
        P("shard"),
        P("shard"),
        P("shard"),
        P("shard", "tensor"),
        P("tensor", "shard"),
        P("tensor", "shard"),
        P("shard"),
        P("shard"),
        P("shard"),
    )
    return jax.shard_map(
        functools.partial(on_device, sizes),
        mesh=mesh,
        in_specs=in_specs,
        out_specs=out_specs,
        check_vma=False,
    )
```

```python
import functools

import jax
import jax.numpy as jnp
from jax import lax
from jax.experimental import pallas as pl
from jax.experimental.pallas import tpu as pltpu
from jax.sharding import PartitionSpec as P

F = jnp.float32
B = jnp.bfloat16


def wide_add(*terms):
    total = terms[0].astype(F)
    for term in terms[1:]:
        total = total + term.astype(F)
    return total


def together(*values):
    return lax.optimization_barrier(values)


class Links:
    def __init__(self, sizes):
        self.sizes = sizes
        self.s = lax.axis_index("shard")
        self.c = lax.axis_index("context")
        self.t = lax.axis_index("tensor")
        self.core = self.c % 2

    def perm_t(self, value, step):
        n = self.sizes["tensor"]
        return lax.ppermute(value, "tensor", [(i, (i + step) % n) for i in range(n)])

    def perm_s(self, value, mask):
        n = self.sizes["shard"]
        return lax.ppermute(value, "shard", [(i, i ^ mask) for i in range(n)])

    def perm_c(self, value, mask=1):
        n = self.sizes["context"]
        return lax.ppermute(value, "context", [(i, i ^ mask) for i in range(n)])

    def undeal_some(self, rows, steps):
        n = self.sizes["tensor"]
        rows = rows.reshape(n, rows.shape[0] // n, rows.shape[1])
        return {d: self.perm_t(rows[d], n - d) for d in steps if d < n}

    def undealt(self, rows, moved, dtype):
        n = self.sizes["tensor"]
        rows = rows.reshape(n, rows.shape[0] // n, rows.shape[1])
        return lay(self.t, [rows[0]] + [moved[d] for d in range(1, n)], dtype)

    def half(self, local):
        rows = local.shape[0] // 2
        return lax.dynamic_slice_in_dim(local, self.core * rows, rows, 0)

    def spread_t(self, local):
        n = self.sizes["tensor"]
        return jnp.stack([local] + [self.perm_t(local, d) for d in range(1, n)])

    def spread_near(self, block):
        return self.perm_s(block, 1), self.perm_s(block, 2)

    def spread_far(self, near):
        h = self.sizes["tensor"] // 2
        over_x, over_y = near
        return self.perm_s(over_x[:h], 2), self.perm_s(over_y[h:], 1)

    def carry(self, rows, extra, steps):
        n = self.sizes["tensor"]
        take = lambda d: lax.dynamic_index_in_dim(rows, (self.t + d) % n, 0, keepdims=False)
        return {d: self.perm_t(jnp.concatenate([take(d), extra]), d) for d in steps if d < n}

    def unload(self, rows, extra, moved):
        length = rows.shape[1]
        own = lax.dynamic_index_in_dim(rows, self.t, 0, keepdims=False)
        steps = sorted(moved)
        return (
            jnp.concatenate([own] + [moved[d][:length] for d in steps]),
            jnp.stack([extra] + [moved[d][length:] for d in steps]),
        )

    def swap(self, values):
        return tuple(self.perm_c(value) for value in values)

    def collect_one(self, parts):
        h = parts.shape[1] // 2
        return (
            self.perm_s(jnp.stack([parts[3, h:], parts[1, h:]]), 1),
            self.perm_s(jnp.stack([parts[3, :h], parts[2, :h]]), 2),
        )

    def collect_two(self, parts, one):
        h = parts.shape[1] // 2
        return (
            self.perm_s(wide_add(parts[1, :h], one[1][0]).astype(B), 1),
            self.perm_s(wide_add(parts[2, h:], one[0][0]).astype(B), 2),
        )

    def sums(self, parts, one, two):
        h = parts.shape[1] // 2
        return jnp.concatenate(
            [
                wide_add(parts[0, :h], two[0], one[1][1]).astype(B),
                wide_add(parts[0, h:], one[0][1], two[1]).astype(B),
            ]
        )

    def collect_t(self, total, slots):
        n = self.sizes["tensor"]
        return [self.perm_t(total[i], n - i) for i in slots if i < n]

    def collect_end(self, terms):
        total = wide_add(*terms)
        mask = 2
        while mask < self.sizes["context"]:
            low = total.astype(B)
            total = wide_add(low, self.perm_c(low, mask))
            mask *= 2
        low = total.astype(B)
        other = self.perm_c(low)
        first = jnp.where(self.core == 0, low, other)
        second = jnp.where(self.core == 0, other, low)
        return jnp.concatenate([first, second])


def dot(a, b, ca=1, cb=0):
    return lax.dot_general(a, b, (((ca,), (cb,)), ((), ())), preferred_element_type=F)


def iota(shape, axis):
    return lax.broadcasted_iota(jnp.int32, shape, axis)


def block_diagonal(compact, heads):
    k, m = compact.shape[0], compact.shape[1] // heads
    zero = jnp.zeros((k, m), compact.dtype)
    rows = []
    for h in range(heads):
        row = [zero] * heads
        row[h] = compact[:, h * m : (h + 1) * m]
        rows.append(jnp.concatenate(row, axis=1))
    return jnp.concatenate(rows, axis=0)


def diagonal_blocks(full, heads):
    k, m = full.shape[0] // heads, full.shape[1] // heads
    return jnp.concatenate(
        [full[h * k : (h + 1) * k, h * m : (h + 1) * m] for h in range(heads)], axis=1
    )


def stacked(upper, lower, heads):
    a, b = block_diagonal(upper, heads), block_diagonal(lower, heads)
    gap = jnp.zeros((second_start(a.shape[0]) - a.shape[0], a.shape[1]), a.dtype)
    return jnp.concatenate([a, gap, b], axis=0)


def second_start(width):
    return -(-width // 128) * 128


def beside(left, right):
    gap = jnp.zeros((left.shape[0], second_start(left.shape[1]) - left.shape[1]), left.dtype)
    return jnp.concatenate([left, gap, right], axis=1)


def rows_to_lanes(rows, lanes):
    k = rows.shape[1]
    tile = (iota((k, lanes), 1) % k == iota((k, lanes), 0)).astype(F).astype(B)
    spread = dot(rows, tile)
    hit = iota(spread.shape, 1) // k == iota(spread.shape, 0)
    return jnp.sum(jnp.where(hit, spread, 0.0), axis=0, keepdims=True)


class Pieces:
    def __init__(self, n, m, where, refs, dest, sems, start, cols, slots=None):
        self.n, self.m, self.where, self.refs = n, m, where, refs
        self.slots = slots or range(n)
        self.dest, self.sems, self.start_col, self.cols = dest, sems, start, cols
        self.rows = refs[0].shape[1]

    def copies(self, t):
        s, c = self.where[0], self.where[1]
        made = []
        for i in range(2):
            half = c if i == 0 else 1 - c
            for j in range(self.m):
                row = pl.multiple_of((s ^ j) * (2 * self.rows) + half * self.rows, 8)
                src = self.refs[i * self.m + j].at[t]
                src = src.at[:, pl.ds(self.start_col, self.cols)]
                u = t - self.slots[0]
                target = self.dest.at[u, pl.ds(row, self.rows)]
                made.append(pltpu.make_async_copy(src, target, self.sems.at[u, i * self.m + j]))
        return made

    def start(self):
        for t in self.slots:
            for copy in self.copies(t):
                copy.start()

    def wait(self, t):
        for u in self.slots:

            @pl.when(t == u - self.slots[0])
            def _():
                for copy in self.copies(u):
                    copy.wait()


ANY = pl.BlockSpec(memory_space=pl.ANY)
SCALARS = pl.BlockSpec(memory_space=pltpu.SMEM)


def slot(*shape, first=0):
    zeros = (0,) * len(shape)
    return pl.BlockSpec((1,) + shape, lambda t: (t + first,) + zeros)


def fixed(*shape):
    zeros = (0,) * len(shape)
    return pl.BlockSpec(shape, lambda *_: zeros)


COST = {
    "project": 11,
    "attend": 6,
    "widen": 10,
    "narrow": 13,
    "ffn_grad": 9,
    "widen_back": 10,
    "attend_back": 7,
    "project_back": 11,
}


def call(body, grid, in_specs, out_specs, outs, scratch, name, flops=0):
    return pl.pallas_call(
        body,
        grid=grid,
        in_specs=in_specs,
        out_specs=out_specs,
        out_shape=[jax.ShapeDtypeStruct(s, d) for s, d in outs],
        scratch_shapes=scratch,
        compiler_params=pltpu.CompilerParams(
            dimension_semantics=("arbitrary",) * len(grid), vmem_limit_bytes=60 * 1024 * 1024
        ),
        cost_estimate=pl.CostEstimate(
            flops=COST[name] * 300_000_000, transcendentals=0, bytes_accessed=COST[name] * 800_000
        ),
        name=name,
    )


def lay(t, chunks, dtype):
    n, shape = len(chunks), chunks[0].shape

    def body(t, *refs):
        for d in range(n):

            @pl.when(pl.program_id(0) == d)
            def _():
                refs[n][0] = refs[d][...].astype(dtype)

    return pl.pallas_call(
        body,
        grid_spec=pltpu.PrefetchScalarGridSpec(
            num_scalar_prefetch=1,
            grid=(n,),
            in_specs=[pl.BlockSpec(shape, lambda d, t: (0, 0))] * n,
            out_specs=pl.BlockSpec((1,) + shape, lambda d, t: ((t[0] + d) % n, 0, 0)),
        ),
        out_shape=jax.ShapeDtypeStruct((n,) + shape, dtype),
        cost_estimate=pl.CostEstimate(flops=0, transcendentals=0, bytes_accessed=800_000),
        compiler_params=pltpu.CompilerParams(dimension_semantics=("arbitrary",)),
        name="lay",
    )(t[None].astype(jnp.int32), *chunks)


def gather_rows(vectors, count):
    def body(*refs):
        row, k = iota((count, 64), 0), 0
        total = jnp.zeros((count, 64), F)
        for ref in refs[:-1]:
            value = ref[...].astype(F).reshape(1, ref.shape[0])
            for start in range(0, ref.shape[0], 64):
                total = jnp.where(row == k, value[:, start : start + 64], total)
                k += 1
        refs[-1][...] = total.astype(B)

    return pl.pallas_call(
        body,
        out_shape=jax.ShapeDtypeStruct((count, 64), B),
        cost_estimate=pl.CostEstimate(flops=0, transcendentals=0, bytes_accessed=8_000),
        name="gather_rows",
    )(*vectors)


def norm_stats(res):
    mean = jnp.mean(res, axis=-1, keepdims=True)
    centered = res - mean
    var = jnp.mean(centered * centered, axis=-1, keepdims=True)
    inverse = lax.rsqrt(var + 1e-05)
    return centered * inverse, inverse


def norm_back(normal, inverse, gain, upstream):
    scaled = upstream * gain
    inner = (
        scaled
        - jnp.mean(scaled, axis=-1, keepdims=True)
        - normal * jnp.mean(scaled * normal, axis=-1, keepdims=True)
    )
    return inner * inverse


def as_rows(vectors, first):
    width = vectors[0].shape[1]
    row = iota((8, width), 0)
    total = jnp.zeros((8, width), F)
    for i, vector in enumerate(vectors):
        total = jnp.where(row == first + i, vector, total)
    return total


def turn(dest, spare, value, where, m):
    spare[...] = value
    rows = value.shape[0] // (2 * m)
    s, c = where[0], where[1]
    for part in range(2):
        half = c if part == 0 else 1 - c
        for i in range(m):
            src = pl.multiple_of(((s ^ i) * 2 + half) * rows, 16)
            row = (part * m + i) * rows
            dest[row : row + rows] = spare[pl.ds(src, rows)]


def store_turned(value, col, keep, give, m):
    rows, cols = value.shape[0] // (2 * m), value.shape[1]
    for i in range(m):
        keep[i, 0, :, col : col + cols] = value[i * rows : (i + 1) * rows].astype(B)
        give[i, 0, :, col : col + cols] = value[(m + i) * rows : (m + i + 1) * rows].astype(B)


def folded(laid):
    pair = laid[:, :128]
    for k in range(128, laid.shape[1], 128):
        pair = pair + laid[:, k : k + 128]
    return jnp.concatenate([jnp.zeros((laid.shape[0], 64), F), pair[:, :64] + pair[:, 64:]], axis=1)


def over_rows(span, step_rows):
    step = 256 if span % 256 == 0 else span

    def one(i, carry):
        step_rows(pl.ds(pl.multiple_of(i * step, step), step))
        return carry

    lax.fori_loop(0, span // step, one, 0)


class Shape:
    def __init__(self, sizes, features, tokens, b_up):
        self.n, self.m = sizes["tensor"], sizes["shard"]
        self.hl, self.feats, self.hd = features.shape
        self.chunk, self.width = tokens.shape[1], tokens.shape[2]
        self.span = self.chunk * self.n
        self.share = self.width // self.m
        self.rows = self.share // 2
        self.oc = self.hl * self.hd
        self.qc = 3 * self.oc
        self.hm = self.hl * self.feats
        self.ff = b_up.size * self.m
        self.q_cols = self.qc + 64
        self.a_cols = self.q_cols + self.oc + 64
        self.scale = self.hd ** (-0.25)


def project(z, where, pieces, x, feat, valid, slots):
    cnt, first = len(slots), slots[0]
    n, span, hl, feats, hd = z.n, z.span, z.hl, z.feats, z.hd

    def body(where, *refs):
        pcs, refs = refs[:8], refs[8:]
        x, feat, valid, q_out, k_out, v_out, qf_out, kf_out, st_out, top_out, w, k_dash, peak, sems = refs
        t = pl.program_id(0)
        fetch = Pieces(n, z.m, where, pcs, w, sems, 0, z.q_cols, slots)
        pl.when(t == 0)(fetch.start)
        fetch.wait(t)
        bias = jnp.zeros((16, 64), F)
        for s in range(z.m):
            bias = bias + w[t, s * z.share : s * z.share + 16, z.qc :].astype(F)
        bias = rows_to_lanes(bias.astype(B), z.qc)
        table = block_diagonal(feat[0], hl)
        peak[...] = jnp.full((8, z.hm), -1e30, F)

        def queries_keys(r):
            qkv = dot(x[r], w[t, :, : z.qc]) + bias
            q = (qkv[:, : z.oc] * z.scale).astype(B)
            k = (qkv[:, z.oc : 2 * z.oc] * z.scale).astype(B)
            q_out[0, r], k_out[0, r], v_out[0, r] = q, k, qkv[:, 2 * z.oc :].astype(B)
            qd, kd = dot(q, table), dot(k, table)
            qs, ks = q.astype(F), k.astype(F)
            qs, ks = qs * qs, ks * ks
            live = valid[r] > 0
            for h in range(hl):
                seg, cols = slice(h * hd, (h + 1) * hd), slice(h * feats, (h + 1) * feats)
                dash = qd[:, cols] - 0.5 * jnp.sum(qs[:, seg], axis=-1, keepdims=True)
                qf_out[0, r, cols] = jnp.exp(
                    dash - jnp.floor(jnp.max(dash, axis=-1, keepdims=True))
                ).astype(B)
                dash = kd[:, cols] - 0.5 * jnp.sum(ks[:, seg], axis=-1, keepdims=True)
                k_dash[r, cols] = dash
                top = jnp.max(jnp.where(live, dash, -1e30), axis=0, keepdims=True)
                peak[:, cols] = jnp.maximum(peak[:, cols], top)

        over_rows(span, queries_keys)
        tops = []
        for h in range(hl):
            top = jnp.max(peak[0:1, h * feats : (h + 1) * feats], axis=1, keepdims=True)
            tops.append(jnp.broadcast_to(jnp.floor(top), (8, feats)))
        top = jnp.concatenate(tops, axis=1)
        top_out[0] = top

        def keys(r):
            live = valid[r] > 0
            kf_out[0, r] = jnp.where(live, jnp.exp(k_dash[r] - top[0:1]), 0.0).astype(B)

        over_rows(span, keys)
        vx = jnp.concatenate([v_out[0], jnp.ones((span, 64), B)], axis=1)
        state = dot(vx, kf_out[0], 0, 0)
        high = top.astype(B).astype(F)
        mid = (top - high).astype(B).astype(F)
        row, last = iota((8, z.hm), 0), state[z.oc : z.oc + 8]
        for i, term in enumerate((high, mid, top - high - mid)):
            last = jnp.where(row == i + 1, term, last)
        st_out[0] = jnp.concatenate([diagonal_blocks(state[: z.oc], hl), last], axis=0).astype(B)

    return call(
        body,
        (cnt,),
        [SCALARS] + [ANY] * 8 + [fixed(span, z.width), slot(hd, z.hm, first=first), fixed(span, 1)],
        [slot(span, z.oc)] * 3 + [slot(span, z.hm)] * 2 + [slot(hd + 8, z.hm), slot(8, z.hm)],
        [((cnt, span, z.oc), B)] * 3
        + [((cnt, span, z.hm), B)] * 2
        + [((cnt, hd + 8, z.hm), B), ((cnt, 8, z.hm), F)],
        [
            pltpu.VMEM((cnt, z.width, z.q_cols), B),
            pltpu.VMEM((span, z.hm), F),
            pltpu.VMEM((8, z.hm), F),
            pltpu.SemaphoreType.DMA((cnt, 2 * z.m)),
        ],
        "project",
    )(where, *pieces, x, feat, valid)


def attend(z, where, pieces, qf, state, slots, x=None, before=None):
    cnt, first, last = len(slots), slots[0], x is not None
    n, span, hl, hd = z.n, z.span, z.hl, z.hd

    def body(where, *refs):
        pcs, refs = refs[:8], refs[8:]
        qf, state, refs = refs[0], refs[1], refs[2:]
        if last:
            x, before, refs = refs[0], refs[1], refs[2:]
        mixed_out, den_out, bup_out, refs = refs[0], refs[1], refs[2], refs[3:]
        if last:
            normal_out, inverse_out, vec_out, w, acc, sems = refs
        else:
            acc, w, sems = refs
        t = pl.program_id(0)
        fetch = Pieces(n, z.m, where, pcs, w, sems, z.q_cols, z.oc + 64, slots)
        pl.when(t == 0)(fetch.start)
        compact = state[0, :hd]
        total = jnp.broadcast_to(state[0, hd : hd + 1], (hd, z.hm))
        table = stacked(compact, total, hl)
        fetch.wait(t)

        def ratios(r):
            both = dot(qf[0, r], table, 1, 1)
            den = both[:, second_start(z.oc) :]
            mixed = (both[:, : z.oc] / den).astype(B)
            mixed_out[0, r] = mixed
            den_out[0, r] = den
            so_far = jnp.where(t == 0, before[r] if last else 0.0, acc[r])
            acc[r] = dot(mixed, w[t, :, : z.oc], 1, 1) + so_far

        over_rows(span, ratios)
        bias = jnp.zeros((16, 64), F)
        for s in range(z.m):
            bias = bias + w[t, s * z.share + 24 : s * z.share + 40, z.oc :].astype(F)
        bup_out[0] = jnp.broadcast_to(rows_to_lanes(bias.astype(B), z.ff), (8, z.ff))
        if not last:
            return

        @pl.when(t == cnt - 1)
        def _():
            lanes = z.width
            per = z.share // 64
            tile = (iota((64, lanes), 1) % 64 == iota((64, lanes), 0)).astype(F).astype(B)
            found = jnp.zeros((24, lanes), F)
            for s in range(z.m):
                spread = dot(w[0, s * z.share : s * z.share + 24, z.oc :], tile)
                hit = iota((24, lanes), 1) // 64 == per * s + iota((24, lanes), 0) % per
                found = found + jnp.where(hit, spread, 0.0)
            pick = (iota((8, 24), 1) // per == iota((8, 24), 0)).astype(F).astype(B)
            vec = dot(pick, found.astype(B))
            vec_out[...] = vec

            def norm(r):
                res = acc[r] + vec[0:1] + x[r].astype(F)
                normal_out[r], inverse_out[r] = norm_stats(res)

            over_rows(span, norm)

    wide = fixed(span, z.width)
    ins, extra = [slot(span, z.hm), slot(hd + 8, z.hm)], []
    outs = [slot(span, z.oc), slot(span, z.oc), slot(8, z.ff)]
    shapes = [((cnt, span, z.oc), B), ((cnt, span, z.oc), F), ((cnt, 8, z.ff), F)]
    scratch = [pltpu.VMEM((cnt, z.width, z.oc + 64), B)]
    if last:
        ins, extra = ins + [wide, wide], [x, before]
        outs += [wide, fixed(span, 1), fixed(8, z.width)]
        shapes += [((span, z.width), F), ((span, 1), F), ((8, z.width), F)]
        scratch += [pltpu.VMEM((span, z.width), F)]
    else:
        outs, shapes = outs + [wide], shapes + [((span, z.width), F)]
    return call(
        body,
        (cnt,),
        [SCALARS] + [ANY] * 8 + ins,
        outs,
        shapes,
        scratch + [pltpu.SemaphoreType.DMA((cnt, 2 * z.m))],
        "attend",
    )(where, *pieces, qf, state, *extra)


def widen(z, where, pieces, normal, vec, bup):
    n, span = z.n, z.span

    def body(where, *refs):
        pcs, refs = refs[:8], refs[8:]
        normal, vec, bup, act_out, slope_out, w, low, sems = refs
        t = pl.program_id(0)
        fetch = Pieces(n, z.m, where, pcs, w, sems, 0, z.ff)

        @pl.when(t == 0)
        def _():
            fetch.start()
            low[...] = (normal[...] * vec[1:2] + vec[2:3]).astype(B)

        fetch.wait(t)

        def hidden(r):
            up = dot(low[r], w[t]) + bup[0, 0:1]
            share = 0.5 * (1.0 + lax.erf(up * 0.7071067811865476))
            act_out[0, r] = (up * share).astype(B)
            slope_out[0, r] = (share + up * jnp.exp(-0.5 * up * up) * 0.3989422804014327).astype(B)

        over_rows(span, hidden)

    return call(
        body,
        (n,),
        [SCALARS] + [ANY] * 8 + [fixed(span, z.width), fixed(8, z.width), slot(8, z.ff)],
        [slot(span, z.ff)] * 2,
        [((n, span, z.ff), B)] * 2,
        [
            pltpu.VMEM((n, z.width, z.ff), B),
            pltpu.VMEM((span, z.width), B),
            pltpu.SemaphoreType.DMA((n, 2 * z.m)),
        ],
        "widen",
    )(where, *pieces, normal, vec, bup)


def narrow(z, where, pieces, normal, vec, cot, act, slope):
    n, span, rows, m = z.n, z.span, z.rows, z.m

    def body(where, *refs):
        pcs, refs = refs[:8], refs[8:]
        normal, vec, cot, act, slope = refs[:5]
        out, dres_out, low, dup_out, small_out = refs[5:10]
        w, acc, sems = refs[10:]
        p, t = pl.program_id(0), pl.program_id(1)
        fetch = Pieces(n, m, where, pcs, w, sems, 0, z.ff)

        @pl.when((p == 0) & (t == 0))
        def _():
            fetch.start()

        @pl.when(p == 0)
        def _():
            fetch.wait(t)

            def down(r):
                acc[r] = dot(act[0, r], w[t], 1, 1) + jnp.where(t == 0, 0.0, acc[r])

            over_rows(span, down)

        @pl.when((p == 0) & (t == n - 1))
        def _():
            small_out[...] = jnp.zeros((8, z.width), F)

            def norm(r):
                normed = normal[r] * vec[1:2] + vec[2:3]
                second, inverse = norm_stats(acc[r] + vec[3:4] + normed)
                out[r] = (second * vec[4:5] + vec[5:6]).astype(B)
                up = cot[r].astype(F)
                dres = norm_back(second, inverse, vec[4:5], up)
                dres_out[r] = dres
                low[r] = dres.astype(B)
                small_out[...] += as_rows(
                    [
                        jnp.sum(dres, axis=0, keepdims=True),
                        jnp.sum(up * second, axis=0, keepdims=True),
                        jnp.sum(up, axis=0, keepdims=True),
                    ],
                    3,
                )

            over_rows(span, norm)

        @pl.when(p == 1)
        def _():
            def up_back(r):
                dup_out[0, r] = (dot(low[r], w[t]) * slope[0, r].astype(F)).astype(B)

            over_rows(span, up_back)

    second = lambda *shape: pl.BlockSpec((1,) + shape, lambda p, t: (p * t,) + (0,) * len(shape))
    return call(
        body,
        (2, n),
        [SCALARS]
        + [ANY] * 8
        + [
            fixed(span, z.width),
            fixed(8, z.width),
            fixed(span, z.width),
            pl.BlockSpec((1, span, z.ff), lambda p, t: (t * (1 - p) + (n - 1) * p, 0, 0)),
            second(span, z.ff),
        ],
        [fixed(span, z.width)] * 3 + [second(span, z.ff), fixed(8, z.width)],
        [
            ((span, z.width), B),
            ((span, z.width), F),
            ((span, z.width), B),
            ((n, span, z.ff), B),
            ((8, z.width), F),
        ],
        [
            pltpu.VMEM((n, z.width, z.ff), B),
            pltpu.VMEM((span, z.width), F),
            pltpu.SemaphoreType.DMA((n, 2 * m)),
        ],
        "narrow",
    )(where, *pieces, normal, vec, cot, act, slope)


def ffn_grad(z, where, normal, vec, d_ffn, act, dup):
    n, span, rows, m = z.n, z.span, z.rows, z.m

    def body(where, normal, vec, d_ffn, act, dup, keep, give, bup_out, low_t, normed_t, spare):
        t = pl.program_id(0)

        @pl.when(t == 0)
        def _():
            turn(low_t, spare, d_ffn[...].astype(F).T.astype(B), where, m)
            turn(normed_t, spare, (normal[...] * vec[1:2] + vec[2:3]).T.astype(B), where, m)

        store_turned(dot(low_t[...], act[0]), 0, keep, give, m)
        store_turned(dot(normed_t[...], dup[0]), z.ff, keep, give, m)
        bup_out[0] = jnp.broadcast_to(
            jnp.sum(dup[0].astype(F), axis=0, keepdims=True), (8, z.ff)
        )

    wide, grads = fixed(span, z.width), pl.BlockSpec((m, 1, rows, 2 * z.ff), lambda t: (0, t, 0, 0))
    return call(
        body,
        (n,),
        [SCALARS, wide, fixed(8, z.width), wide, slot(span, z.ff), slot(span, z.ff)],
        [grads, grads, slot(8, z.ff)],
        [((m, n, rows, 2 * z.ff), B)] * 2 + [((n, 8, z.ff), F)],
        [pltpu.VMEM((z.width, span), B)] * 3,
        "ffn_grad",
    )(where, normal, vec, d_ffn, act, dup)


def widen_back(z, where, pieces, normal, inverse, vec, dup, dres):
    n, span = z.n, z.span

    def body(where, *refs):
        pcs, refs = refs[:8], refs[8:]
        normal, inverse, vec, dup, dres, out, small_out, w, acc, sems = refs
        t = pl.program_id(0)
        fetch = Pieces(n, z.m, where, pcs, w, sems, 0, z.ff)
        pl.when(t == 0)(fetch.start)
        fetch.wait(t)

        def back(r):
            acc[r] = dot(dup[0, r], w[t], 1, 1) + jnp.where(t == 0, dres[r], acc[r])

        over_rows(span, back)

        @pl.when(t == n - 1)
        def _():
            small_out[...] = jnp.zeros((8, z.width), F)

            def norm(r):
                up = acc[r]
                back = norm_back(normal[r], inverse[r], vec[1:2], up)
                out[r] = back
                small_out[...] += as_rows(
                    [
                        jnp.sum(back, axis=0, keepdims=True),
                        jnp.sum(up * normal[r], axis=0, keepdims=True),
                        jnp.sum(up, axis=0, keepdims=True),
                    ],
                    0,
                )

            over_rows(span, norm)

    return call(
        body,
        (n,),
        [SCALARS]
        + [ANY] * 8
        + [
            fixed(span, z.width),
            fixed(span, 1),
            fixed(8, z.width),
            slot(span, z.ff),
            fixed(span, z.width),
        ],
        [fixed(span, z.width), fixed(8, z.width)],
        [((span, z.width), F), ((8, z.width), F)],
        [
            pltpu.VMEM((n, z.width, z.ff), B),
            pltpu.VMEM((span, z.width), F),
            pltpu.SemaphoreType.DMA((n, 2 * z.m)),
        ],
        "widen_back",
    )(where, *pieces, normal, inverse, vec, dup, dres)


def attend_back(z, where, pieces, dres, mixed, den, qf, q, state, feat, slots):
    cnt, first = len(slots), slots[0]
    n, span, hl, hd, m = z.n, z.span, z.hl, z.hd, z.m

    def body(where, *refs):
        pcs, refs = refs[:8], refs[8:]
        dres, mixed, den, qf, q, state, feat, dq_out, dstate_out, w, low, pair, sems = refs
        t = pl.program_id(0)
        fetch = Pieces(n, m, where, pcs, w, sems, z.q_cols, z.oc + 64, slots)

        @pl.when(t == 0)
        def _():
            fetch.start()
            low[...] = dres[...].astype(B)

        fetch.wait(t)
        start = second_start(z.oc)
        compact = state[0, :hd]
        total = jnp.broadcast_to(state[0, hd : hd + 1], (hd, z.hm))
        states, tables = stacked(compact, total, hl), stacked(feat[0], jnp.ones((hd, z.hm), B), hl)

        def back(r):
            d_mixed = dot(low[r], w[t, :, : z.oc]).astype(B).astype(F)
            d_num = d_mixed / den[0, r]
            d_den = -(d_num * mixed[0, r].astype(F))
            both = beside(d_num.astype(B), d_den.astype(B))
            pair[r] = both
            dash = (dot(both, states) * qf[0, r].astype(F)).astype(B)
            back = dot(dash, tables, 1, 1)
            dq_out[0, r] = ((back[:, : z.oc] - q[0, r].astype(F) * back[:, start:]) * z.scale).astype(B)

        over_rows(span, back)
        full = dot(pair[...], qf[0], 0, 0)
        row = jnp.concatenate(
            [
                jnp.sum(
                    full[start + h * hd : start + (h + 1) * hd, h * z.feats : (h + 1) * z.feats],
                    axis=0,
                    keepdims=True,
                )
                for h in range(hl)
            ],
            axis=1,
        )
        dstate_out[0] = jnp.concatenate(
            [diagonal_blocks(full[: z.oc], hl), jnp.broadcast_to(row, (8, z.hm))], axis=0
        ).astype(B)

    return call(
        body,
        (cnt,),
        [SCALARS]
        + [ANY] * 8
        + [
            fixed(span, z.width),
            slot(span, z.oc),
            slot(span, z.oc),
            slot(span, z.hm),
            slot(span, z.oc),
            slot(hd + 8, z.hm),
            slot(hd, z.hm, first=first),
        ],
        [slot(span, z.oc), slot(hd + 8, z.hm)],
        [((cnt, span, z.oc), B), ((cnt, hd + 8, z.hm), B)],
        [
            pltpu.VMEM((cnt, z.width, z.oc + 64), B),
            pltpu.VMEM((span, z.width), B),
            pltpu.VMEM((span, second_start(z.oc) + z.oc), B),
            pltpu.SemaphoreType.DMA((cnt, 2 * m)),
        ],
        "attend_back",
    )(where, *pieces, dres, mixed, den, qf, q, state, feat)


def project_back(z, where, pieces, x, dres, dq, k, v, kf, dstate, feat, mixed, small_a, small_b, dbup, slots, before=None):
    cnt, first, last = len(slots), slots[0], before is not None
    n, span, hl, hd, m, rows = z.n, z.span, z.hl, z.hd, z.m, z.rows
    cols = z.a_cols

    def body(where, *refs):
        pcs, refs = refs[:8], refs[8:]
        x, dres, dq, k, v, kf, dstate, feat, mixed, small_a, small_b, dbup = refs[:12]
        refs = refs[12:]
        if last:
            before, refs = refs[0], refs[1:]
            keep, give, out, w, x_t, low_t, spare, dqkv_low, acc, sems = refs
        else:
            keep, give, acc, w, x_t, low_t, spare, dqkv_low, sems = refs
        t = pl.program_id(0)
        fetch = Pieces(n, m, where, pcs, w, sems, 0, z.q_cols, slots)

        @pl.when(t == 0)
        def _():
            fetch.start()
            turn(x_t, spare, x[...].astype(F).T.astype(B), where, m)
            turn(low_t, spare, dres[...].T.astype(B), where, m)

        start = second_start(z.oc)
        table = block_diagonal(dstate[0, :hd], hl)
        total = dstate[0, hd : hd + 1].astype(F)
        dash = ((dot(v[0], table) + total) * kf[0].astype(F)).astype(B)
        dv = dot(kf[0], table, 1, 1)
        back = dot(dash, stacked(feat[0], jnp.ones((hd, z.hm), B), hl), 1, 1)
        dk = (back[:, : z.oc] - k[0].astype(F) * back[:, start:]) * z.scale
        dqkv = jnp.concatenate(
            [dq[0], dk.astype(B), dv.astype(B), jnp.zeros((span, 64), B)], axis=1
        )
        dqkv_low[...] = dqkv
        bias = jnp.sum(dqkv.astype(F), axis=0, keepdims=True)
        laid = jnp.broadcast_to(bias, (rows, z.q_cols))
        laid = jnp.where(iota(laid.shape, 1) // 64 == iota(laid.shape, 0), laid, 0.0)
        grad = dot(x_t[...], dqkv)
        edge = z.q_cols - 128
        store_turned(grad[:, :edge], 0, keep, give, m)
        store_turned(
            grad[:, edge:] + jnp.concatenate([folded(laid)] * (2 * m), axis=0), edge, keep, give, m
        )
        grad = dot(low_t[...], jnp.concatenate([mixed[0], jnp.zeros((span, 64), B)], axis=1))
        packed = small_a[...] + small_b[...] + as_rows([dbup[0, 0:1]], 6)
        per = z.width // 64
        one = (iota((rows, 8), 0) // per == iota((rows, 8), 1)).astype(F).astype(B)
        laid = dot(one, packed.astype(B))
        laid = jnp.where(iota(laid.shape, 1) // 64 == iota(laid.shape, 0) % per, laid, 0.0)
        edge = z.oc + 64 - 128
        store_turned(grad[:, :edge], z.q_cols, keep, give, m)
        store_turned(
            grad[:, edge:] + jnp.concatenate([folded(laid)] * (2 * m), axis=0),
            z.q_cols + edge,
            keep,
            give,
            m,
        )
        fetch.wait(t)

        def tokens_back(r):
            so_far = jnp.where(t == 0, before[r] if last else dres[r], acc[r])
            acc[r] = dot(dqkv_low[r], w[t], 1, 1) + so_far

        over_rows(span, tokens_back)

        if last:

            @pl.when(t == cnt - 1)
            def _():
                out[...] = acc[...].astype(B)

    grads = pl.BlockSpec((m, 1, rows, cols), lambda t: (0, t, 0, 0))
    wide, scratch = fixed(span, z.width), [pltpu.VMEM((cnt, z.width, z.q_cols), B)]
    scratch += [pltpu.VMEM((z.width, span), B)] * 3 + [pltpu.VMEM((span, z.q_cols), B)]
    if last:
        scratch += [pltpu.VMEM((span, z.width), F)]
    return call(
        body,
        (cnt,),
        [SCALARS]
        + [ANY] * 8
        + [
            wide,
            wide,
            slot(span, z.oc),
            slot(span, z.oc),
            slot(span, z.oc),
            slot(span, z.hm),
            slot(hd + 8, z.hm),
            slot(hd, z.hm, first=first),
            slot(span, z.oc),
            fixed(8, z.width),
            fixed(8, z.width),
            slot(8, z.ff, first=first),
        ]
        + ([wide] if last else []),
        [grads, grads, wide],
        [((m, cnt, rows, cols), B)] * 2 + [((span, z.width), B if last else F)],
        scratch + [pltpu.SemaphoreType.DMA((cnt, 2 * m))],
        "project_back",
    )(
        where, *pieces, x, dres, dq, k, v, kf, dstate, feat, mixed, small_a, small_b, dbup,
        *([before] if last else []),
    )


def place(part, axis, index, count):
    shape = list(part.shape)
    shape[axis] *= count
    return lax.dynamic_update_slice_in_dim(
        jnp.zeros(shape, part.dtype), part, index * part.shape[axis], axis
    )


def on_device(
    sizes,
    tokens,
    lengths,
    features,
    w_qkv,
    b_qkv,
    w_out,
    b_out,
    gain_one,
    shift_one,
    w_up,
    b_up,
    w_down,
    b_down,
    gain_two,
    shift_two,
    cotangent,
):
    links = Links(sizes)
    z = Shape(sizes, features, tokens, b_up)
    n, m, share = z.n, z.m, z.share
    where = jnp.stack([links.s, links.core]).astype(jnp.int32)
    def tall(value):
        return jnp.pad(value, ((0, share - value.shape[0]), (0, 0)))

    biases = place(b_qkv, 2, links.s, m).reshape(3 * z.hl, z.hd)
    vectors = gather_rows([b_out, gain_one, shift_one, b_down, gain_two, shift_two], 24)
    vectors = jnp.concatenate([vectors, place(b_up, 1, links.s, m).reshape(-1, 64)])
    local_a = links.half(
        jnp.concatenate([w_qkv.reshape(share, z.qc), tall(biases), w_out.T, tall(vectors)], axis=1)
    )
    feat_half = links.half(features.transpose(2, 0, 1).reshape(z.hd, z.hm))
    local_u, local_d = links.half(w_up), links.half(w_down.T)
    length = lax.dynamic_index_in_dim(lengths, links.t, 0, keepdims=False)
    order = (links.t - jnp.arange(n)) % n
    position = links.c * z.span + order[:, None] * z.chunk + jnp.arange(z.chunk)[None]
    valid = (position.reshape(-1, 1) < length).astype(F)
    halves = (range(n // 2), range(n // 2, n))
    lo, hi = halves

    def join_states(state, top, came):
        row, mask = z.hd + 1, 1
        own = most = top[:, :1]
        while mask < sizes["context"]:
            if mask > 1:
                came = links.perm_c(state, mask), links.perm_c(top, mask)
                other, other_top = came[0], came[1][:, :1]
            else:
                other = came
                other_top = wide_add(*[other[:, row + i : row + i + 1] for i in range(3)])
            joint = jnp.maximum(most, other_top)
            state = (
                state.astype(F) * jnp.exp(most - joint) + other.astype(F) * jnp.exp(other_top - joint)
            ).astype(B)
            most, mask = joint, 2 * mask
            top = jnp.broadcast_to(most, top.shape)
        return state, jnp.exp(own - most)

    def join_grads(state, came, fall):
        mask = 1
        while mask < sizes["context"]:
            other = came if mask == 1 else links.perm_c(state, mask)
            state = wide_add(state, other).astype(B)
            mask *= 2
        return (state.astype(F) * fall).astype(B)

    block_a = links.spread_t(local_a)
    block_a, tokens, feat_half = together(block_a, tokens, feat_half)
    near_a = links.spread_near(block_a)
    moved = links.carry(tokens, feat_half, range(1, n))
    block_a, near_a, moved, local_u, tokens, feat_half = together(
        block_a, near_a, moved, local_u, tokens, feat_half
    )
    far_a = links.spread_far(near_a)
    other_a = links.swap((block_a,) + near_a)
    x, feat_mine = links.unload(tokens, feat_half, moved)
    far_a, feat_mine, other_a, local_u, valid, x = together(far_a, feat_mine, other_a, local_u, valid, x)
    far_a = (jnp.concatenate(far_a),)
    other_a += links.swap(far_a)
    feat_other = links.perm_c(feat_mine)
    feat_low = jnp.where(links.core == 0, feat_mine, feat_other)
    feat_high = jnp.where(links.core == 0, feat_other, feat_mine)
    feat = jnp.concatenate([feat_low, feat_high], axis=1)
    feat, other_a, local_u = together(feat, other_a, local_u)
    pieces_a = (block_a,) + near_a + far_a + other_a
    block_u = links.spread_t(local_u)
    first = project(z, where, pieces_a, x, feat, valid, lo)
    first, block_u, local_d, valid, cot = together(first, block_u, local_d, valid, cotangent)
    near_u = links.spread_near(block_u)
    moved = links.carry(cot, local_d, (2,))
    other_u = links.swap((block_u,))
    came = links.perm_c(first[5])
    second = project(z, where, pieces_a, x, feat, valid, hi)
    first, second, near_u, block_u, other_u, moved, came, cot, local_d = together(
        first, second, near_u, block_u, other_u, moved, came, cot, local_d
    )
    made = (first, second)
    far_u = links.spread_far(near_u)
    moved.update(links.carry(cot, local_d, (1, 3)))
    came_b = links.perm_c(second[5])
    state_a, fall_a = join_states(first[5], first[6], came)
    one = attend(z, where, pieces_a, first[3], state_a, lo)
    one, far_u, near_u, other_u, moved, came_b, cot, local_d = together(
        one, far_u, near_u, other_u, moved, came_b, cot, local_d
    )
    mixed_a, den_a, bup_a, acc = one
    far_u = (jnp.concatenate(far_u),)
    cot, block_d = links.unload(cot, local_d, moved)
    near_d = links.spread_near(block_d)
    other_u += links.swap(near_u + far_u)
    state_b, fall_b = join_states(second[5], second[6], came_b)
    two = attend(z, where, pieces_a, second[3], state_b, hi, x, acc)
    two, near_d, block_d, other_u, cot = together(two, near_d, block_d, other_u, cot)
    mixed_b, den_b, bup_b, normal, inverse, vec = two
    states, falls = (state_a, state_b), (fall_a, fall_b)
    bup = jnp.concatenate([bup_a, bup_b])
    mixed, den = (mixed_a, mixed_b), (den_a, den_b)
    pieces_u = (block_u,) + near_u + far_u + other_u
    far_d = links.spread_far(near_d)
    other_d = links.swap((block_d,) + near_d)
    act, slope = widen(z, where, pieces_u, normal, vec, bup)
    act, slope, far_d, other_d = together(act, slope, far_d, other_d)
    far_d = (jnp.concatenate(far_d),)
    other_d += links.swap(far_d)
    pieces_d = (block_d,) + near_d + far_d + other_d
    out, d_res_two, d_ffn, dup, small_b = narrow(
        z, where, pieces_d, normal, vec, cot, act, slope
    )
    sent = links.undeal_some(out, (2,))
    keep, give, dbup = ffn_grad(z, where, normal, vec, d_ffn, act, dup)
    keep, give, out, dup, sent = together(keep, give, out, dup, sent)
    other = links.perm_c(give)
    sent.update(links.undeal_some(out, (1, 3)))
    d_res_one, small_a = widen_back(z, where, pieces_u, normal, inverse, vec, dup, d_res_two)
    d_res_one, keep, other, sent = together(d_res_one, keep, other, sent)
    result = links.undealt(out, sent, B)
    parts_f = wide_add(keep, other).astype(B)
    one_f = links.collect_one(parts_f)
    dq_a, d_state_a = attend_back(
        z, where, pieces_a, d_res_one, mixed[0], den[0], made[0][3], made[0][0], states[0], feat, lo
    )
    dq_a, d_state_a, d_res_one, parts_f = together(dq_a, d_state_a, d_res_one, parts_f)
    came = links.perm_c(d_state_a)
    dq_b, d_state_b = attend_back(
        z, where, pieces_a, d_res_one, mixed[1], den[1], made[1][3], made[1][0], states[1], feat, hi
    )
    dq_b, d_state_b, came, one_f, parts_f, x = together(dq_b, d_state_b, came, one_f, parts_f, x)
    two_f = links.collect_two(parts_f, one_f)
    came_b = links.perm_c(d_state_b)
    d_state_a = join_grads(d_state_a, came, falls[0])
    dq = (dq_a, dq_b)

    def run_back(i, d_state, x, before):
        return project_back(
            z, where, pieces_a, x, d_res_one, dq[i], made[i][1], made[i][2], made[i][4],
            d_state, feat, mixed[i], small_a, small_b, dbup, halves[i], before,
        )

    keep, give, acc = run_back(0, d_state_a, x, None)
    keep, give, acc, two_f, came_b, parts_f, x = together(keep, give, acc, two_f, came_b, parts_f, x)
    sums_f = links.sums(parts_f, one_f, two_f)
    terms_f = links.collect_t(sums_f, (1, 2))
    other = links.perm_c(give)
    d_state_b = join_grads(d_state_b, came_b, falls[1])
    keep_b, give_b, grad_x = run_back(1, d_state_b, x, acc)
    keep_b, give_b, grad_x, keep, other, terms_f, sums_f = together(
        keep_b, give_b, grad_x, keep, other, terms_f, sums_f
    )
    other_b = links.perm_c(give_b)
    terms_f += links.collect_t(sums_f, range(3, n))
    parts = wide_add(keep, other).astype(B)
    parts_b = wide_add(keep_b, other_b).astype(B)
    parts, grad_x = together(jnp.concatenate([parts, parts_b], axis=1), grad_x)
    one = links.collect_one(parts)
    sent = links.undeal_some(grad_x, (2,))
    one, parts, sent, grad_x, terms_f = together(one, parts, sent, grad_x, terms_f)
    two = links.collect_two(parts, one)
    sent.update(links.undeal_some(grad_x, (1, 3)))
    two, one, parts, sent, grad_x = together(two, one, parts, sent, grad_x)
    grad_tokens = links.undealt(grad_x, sent, F)
    sums = links.sums(parts, one, two)
    terms = [sums[0]] + links.collect_t(sums, range(1, n))
    terms_f = [sums_f[0]] + terms_f
    own_ffn = links.collect_end(terms_f)
    grad_up, grad_down = own_ffn[:, z.ff :].astype(F), own_ffn[:, : z.ff].T.astype(F)
    terms, grad_tokens, result, grad_up, grad_down = together(
        terms, grad_tokens, result, grad_up, grad_down
    )
    own_qkv = links.collect_end(terms)
    def mine(value, axis):
        size = value.shape[axis] // m
        return lax.dynamic_slice_in_dim(value, links.s * size, size, axis).astype(F)

    own_b_qkv = mine(own_qkv[: 3 * z.hl, z.qc : z.q_cols].reshape(3, z.hl, z.hd), 2)
    own_out = own_qkv[:, z.q_cols : z.q_cols + z.oc]
    tail = own_qkv[: z.rows, z.q_cols + z.oc :]
    vecs = mine(tail[: 6 * z.width // 64].reshape(6, z.width), 1)
    start = 6 * z.width // 64
    own_b_up = mine(tail[start : start + z.ff // 64].reshape(b_up.shape[0], -1), 1)
    return (
        result,
        grad_tokens,
        own_qkv[:, : z.qc].reshape(w_qkv.shape).astype(F),
        own_b_qkv,
        own_out.T.astype(F),
        vecs[0],
        vecs[1],
        vecs[2],
        grad_up,
        own_b_up,
        grad_down,
        vecs[3],
        vecs[4],
        vecs[5],
    )


def solution(mesh):
    sizes = dict(mesh.shape)
    in_specs = (
        P("shard", ("context", "tensor"), None),
        P("shard"),
        P("tensor", None, None),
        P("shard", None, "tensor", None),
        P(None, "tensor", "shard"),
        P("tensor", "shard"),
        P("shard"),
        P("shard"),
        P("shard"),
        P("shard", "tensor"),
        P("tensor", "shard"),
        P("tensor", "shard"),
        P("shard"),
        P("shard"),
        P("shard"),
        P("shard", ("context", "tensor"), None),
    )
    out_specs = (
        P("shard", ("context", "tensor"), None),
        P("shard", ("context", "tensor"), None),
        P("shard", None, "tensor", None),
        P(None, "tensor", "shard"),
        P("tensor", "shard"),
        P("shard"),
        P("shard"),
        P("shard"),
        P("shard", "tensor"),
        P("tensor", "shard"),
        P("tensor", "shard"),
        P("shard"),
        P("shard"),
        P("shard"),
    )
    return jax.shard_map(
        functools.partial(on_device, sizes),
        mesh=mesh,
        in_specs=in_specs,
        out_specs=out_specs,
        check_vma=False,
    )
```

```python
import functools

import jax
import jax.numpy as jnp
from jax import lax
from jax.experimental import pallas as pl
from jax.experimental.pallas import tpu as pltpu
from jax.sharding import PartitionSpec as P

F = jnp.float32
B = jnp.bfloat16
ORDER = (0, 1, 3, 2)


def wide_add(*terms):
    total = terms[0].astype(F)
    for term in terms[1:]:
        total = total + term.astype(F)
    return total


def together(*values):
    return lax.optimization_barrier(values)


class Links:
    def __init__(self, sizes):
        self.sizes = sizes
        self.s = lax.axis_index("shard")
        self.c = lax.axis_index("context")
        self.t = lax.axis_index("tensor")
        self.core = self.c % 2

    def perm_t(self, value, step):
        n = self.sizes["tensor"]
        return lax.ppermute(value, "tensor", [(i, (i + step) % n) for i in range(n)])

    def perm_s(self, value, mask):
        n = self.sizes["shard"]
        return lax.ppermute(value, "shard", [(i, i ^ mask) for i in range(n)])

    def perm_c(self, value, mask=1):
        n = self.sizes["context"]
        return lax.ppermute(value, "context", [(i, i ^ mask) for i in range(n)])

    def undeal_some(self, rows, steps):
        n = self.sizes["tensor"]
        rows = rows.reshape(n, rows.shape[0] // n, rows.shape[1])
        return {d: self.perm_t(rows[d], n - d) for d in steps if d < n}

    def undealt(self, rows, moved, dtype):
        n = self.sizes["tensor"]
        rows = rows.reshape(n, rows.shape[0] // n, rows.shape[1])
        return lay(self.t, [rows[0]] + [moved[d] for d in range(1, n)], dtype)

    def half(self, local):
        rows = local.shape[0] // 2
        return lax.dynamic_slice_in_dim(local, self.core * rows, rows, 0)

    def spread_t(self, local):
        n = self.sizes["tensor"]
        return jnp.stack([local] + [self.perm_t(local, d) for d in range(1, n)])

    def spread_near(self, block):
        return self.perm_s(block, 1), self.perm_s(block, 2)

    def spread_far(self, near):
        h = self.sizes["tensor"] // 2
        over_x, over_y = near
        return self.perm_s(over_x[:h], 2), self.perm_s(over_y[h:], 1)

    def carry(self, rows, extra, steps):
        n = self.sizes["tensor"]
        take = lambda d: lax.dynamic_index_in_dim(rows, (self.t + d) % n, 0, keepdims=False)
        return {d: self.perm_t(jnp.concatenate([take(d), extra]), d) for d in steps if d < n}

    def unload(self, rows, extra, moved):
        length = rows.shape[1]
        own = lax.dynamic_index_in_dim(rows, self.t, 0, keepdims=False)
        steps = sorted(moved)
        return (
            jnp.concatenate([own] + [moved[d][:length] for d in steps]),
            jnp.stack([extra] + [moved[d][length:] for d in steps]),
        )

    def swap(self, values):
        return tuple(self.perm_c(value) for value in values)

    def collect_one(self, low, high):
        return (
            self.perm_s(wide_add(*[term[1:3] for term in high]).astype(B), 1),
            self.perm_s(wide_add(*[term[2:4] for term in low]).astype(B), 2),
        )

    def collect_two(self, low, high, one):
        return (
            self.perm_s(wide_add(*[term[1] for term in low], one[1][0]).astype(B), 1),
            self.perm_s(wide_add(*[term[3] for term in high], one[0][1]).astype(B), 2),
        )

    def sums(self, low, high, one, two):
        return jnp.concatenate(
            [
                wide_add(*[term[0] for term in low], two[0], one[1][1]).astype(B),
                wide_add(*[term[0] for term in high], one[0][0], two[1]).astype(B),
            ]
        )

    def collect_t(self, total, slots):
        n = self.sizes["tensor"]
        return [self.perm_t(total[i], n - i) for i in slots if i < n]

    def collect_end(self, terms):
        total = wide_add(*terms)
        mask = 2
        while mask < self.sizes["context"]:
            low = total.astype(B)
            total = wide_add(low, self.perm_c(low, mask))
            mask *= 2
        low = total.astype(B)
        other = self.perm_c(low)
        first = jnp.where(self.core == 0, low, other)
        second = jnp.where(self.core == 0, other, low)
        return jnp.concatenate([first, second])


def dot(a, b, ca=1, cb=0):
    return lax.dot_general(a, b, (((ca,), (cb,)), ((), ())), preferred_element_type=F)


def iota(shape, axis):
    return lax.broadcasted_iota(jnp.int32, shape, axis)


def block_diagonal(compact, heads):
    k, m = compact.shape[0], compact.shape[1] // heads
    zero = jnp.zeros((k, m), compact.dtype)
    rows = []
    for h in range(heads):
        row = [zero] * heads
        row[h] = compact[:, h * m : (h + 1) * m]
        rows.append(jnp.concatenate(row, axis=1))
    return jnp.concatenate(rows, axis=0)


def diagonal_blocks(full, heads):
    k, m = full.shape[0] // heads, full.shape[1] // heads
    return jnp.concatenate(
        [full[h * k : (h + 1) * k, h * m : (h + 1) * m] for h in range(heads)], axis=1
    )


def stacked(upper, lower, heads):
    a, b = block_diagonal(upper, heads), block_diagonal(lower, heads)
    gap = jnp.zeros((second_start(a.shape[0]) - a.shape[0], a.shape[1]), a.dtype)
    return jnp.concatenate([a, gap, b], axis=0)


def second_start(width):
    return -(-width // 128) * 128


def beside(left, right):
    gap = jnp.zeros((left.shape[0], second_start(left.shape[1]) - left.shape[1]), left.dtype)
    return jnp.concatenate([left, gap, right], axis=1)


def rows_to_lanes(rows, lanes):
    k = rows.shape[1]
    tile = (iota((k, lanes), 1) % k == iota((k, lanes), 0)).astype(F).astype(B)
    spread = dot(rows, tile)
    hit = iota(spread.shape, 1) // k == iota(spread.shape, 0)
    return jnp.sum(jnp.where(hit, spread, 0.0), axis=0, keepdims=True)


class Pieces:
    def __init__(self, n, m, where, refs, dest, sems, start, cols, slots=None):
        self.n, self.m, self.where, self.refs = n, m, where, refs
        self.slots = slots or range(n)
        self.dest, self.sems, self.start_col, self.cols = dest, sems, start, cols
        self.rows = refs[0].shape[1]

    def copies(self, t):
        s, c = self.where[0], self.where[1]
        made = []
        for i in range(2):
            half = c if i == 0 else 1 - c
            for j in range(self.m):
                row = pl.multiple_of((s ^ j) * (2 * self.rows) + half * self.rows, 8)
                src = self.refs[i * self.m + j].at[t]
                src = src.at[:, pl.ds(self.start_col, self.cols)]
                u = t - self.slots[0]
                target = self.dest.at[u, pl.ds(row, self.rows)]
                made.append(pltpu.make_async_copy(src, target, self.sems.at[u, i * self.m + j]))
        return made

    def start(self):
        for t in self.slots:
            for copy in self.copies(t):
                copy.start()

    def wait(self, t):
        for u in self.slots:

            @pl.when(t == u - self.slots[0])
            def _():
                for copy in self.copies(u):
                    copy.wait()


ANY = pl.BlockSpec(memory_space=pl.ANY)
SCALARS = pl.BlockSpec(memory_space=pltpu.SMEM)


def slot(*shape, first=0):
    zeros = (0,) * len(shape)
    return pl.BlockSpec((1,) + shape, lambda t: (t + first,) + zeros)


def fixed(*shape):
    zeros = (0,) * len(shape)
    return pl.BlockSpec(shape, lambda *_: zeros)


COST = {
    "project": 11,
    "attend": 6,
    "widen": 10,
    "narrow": 13,
    "ffn_grad": 9,
    "widen_back": 10,
    "attend_back": 7,
    "project_back": 11,
}


def call(body, grid, in_specs, out_specs, outs, scratch, name, flops=0):
    return pl.pallas_call(
        body,
        grid=grid,
        in_specs=in_specs,
        out_specs=out_specs,
        out_shape=[jax.ShapeDtypeStruct(s, d) for s, d in outs],
        scratch_shapes=scratch,
        compiler_params=pltpu.CompilerParams(
            dimension_semantics=("arbitrary",) * len(grid), vmem_limit_bytes=60 * 1024 * 1024
        ),
        cost_estimate=pl.CostEstimate(
            flops=COST[name] * 300_000_000, transcendentals=0, bytes_accessed=COST[name] * 800_000
        ),
        name=name,
    )


def lay(t, chunks, dtype):
    n, shape = len(chunks), chunks[0].shape

    def body(t, *refs):
        for d in range(n):

            @pl.when(pl.program_id(0) == d)
            def _():
                refs[n][0] = refs[d][...].astype(dtype)

    return pl.pallas_call(
        body,
        grid_spec=pltpu.PrefetchScalarGridSpec(
            num_scalar_prefetch=1,
            grid=(n,),
            in_specs=[pl.BlockSpec(shape, lambda d, t: (0, 0))] * n,
            out_specs=pl.BlockSpec((1,) + shape, lambda d, t: ((t[0] + d) % n, 0, 0)),
        ),
        out_shape=jax.ShapeDtypeStruct((n,) + shape, dtype),
        cost_estimate=pl.CostEstimate(flops=0, transcendentals=0, bytes_accessed=800_000),
        compiler_params=pltpu.CompilerParams(dimension_semantics=("arbitrary",)),
        name="lay",
    )(t[None].astype(jnp.int32), *chunks)


def gather_rows(vectors, count):
    def body(*refs):
        row, k = iota((count, 64), 0), 0
        total = jnp.zeros((count, 64), F)
        for ref in refs[:-1]:
            value = ref[...].astype(F).reshape(1, ref.shape[0])
            for start in range(0, ref.shape[0], 64):
                total = jnp.where(row == k, value[:, start : start + 64], total)
                k += 1
        refs[-1][...] = total.astype(B)

    return pl.pallas_call(
        body,
        out_shape=jax.ShapeDtypeStruct((count, 64), B),
        cost_estimate=pl.CostEstimate(flops=0, transcendentals=0, bytes_accessed=8_000),
        name="gather_rows",
    )(*vectors)


def norm_stats(res):
    mean = jnp.mean(res, axis=-1, keepdims=True)
    centered = res - mean
    var = jnp.mean(centered * centered, axis=-1, keepdims=True)
    inverse = lax.rsqrt(var + 1e-05)
    return centered * inverse, inverse


def norm_back(normal, inverse, gain, upstream):
    scaled = upstream * gain
    inner = (
        scaled
        - jnp.mean(scaled, axis=-1, keepdims=True)
        - normal * jnp.mean(scaled * normal, axis=-1, keepdims=True)
    )
    return inner * inverse


def as_rows(vectors, first):
    width = vectors[0].shape[1]
    row = iota((8, width), 0)
    total = jnp.zeros((8, width), F)
    for i, vector in enumerate(vectors):
        total = jnp.where(row == first + i, vector, total)
    return total


def turn(dest, spare, value, where, m):
    spare[...] = value
    rows = value.shape[0] // (2 * m)
    s, c = where[0], where[1]
    for part in range(2):
        half = c if part == 0 else 1 - c
        for i in range(m):
            src = pl.multiple_of(((s ^ ORDER[i]) * 2 + half) * rows, 16)
            row = (part * m + i) * rows
            dest[row : row + rows] = spare[pl.ds(src, rows)]


def store_turned(value, col, keep, give, m):
    rows, cols = value.shape[0] // (2 * m), value.shape[1]
    for i in range(m):
        keep[i, 0, :, col : col + cols] = value[i * rows : (i + 1) * rows].astype(B)
        give[i, 0, :, col : col + cols] = value[(m + i) * rows : (m + i + 1) * rows].astype(B)


def folded(laid):
    pair = laid[:, :128]
    for k in range(128, laid.shape[1], 128):
        pair = pair + laid[:, k : k + 128]
    return jnp.concatenate([jnp.zeros((laid.shape[0], 64), F), pair[:, :64] + pair[:, 64:]], axis=1)


def over_rows(span, step_rows):
    step = 256 if span % 256 == 0 else span

    def one(i, carry):
        step_rows(pl.ds(pl.multiple_of(i * step, step), step))
        return carry

    lax.fori_loop(0, span // step, one, 0)


class Shape:
    def __init__(self, sizes, features, tokens, b_up):
        self.n, self.m = sizes["tensor"], sizes["shard"]
        self.hl, self.feats, self.hd = features.shape
        self.chunk, self.width = tokens.shape[1], tokens.shape[2]
        self.span = self.chunk * self.n
        self.share = self.width // self.m
        self.rows = self.share // 2
        self.oc = self.hl * self.hd
        self.qc = 3 * self.oc
        self.hm = self.hl * self.feats
        self.ff = b_up.size * self.m
        self.q_cols = self.qc + 64
        self.a_cols = self.q_cols + self.oc + 64
        self.scale = self.hd ** (-0.25)


def project(z, where, pieces, x, feat, valid, slots):
    cnt, first = len(slots), slots[0]
    n, span, hl, feats, hd = z.n, z.span, z.hl, z.feats, z.hd

    def body(where, *refs):
        pcs, refs = refs[:8], refs[8:]
        x, feat, valid, q_out, k_out, v_out, qf_out, kf_out, st_out, top_out, w, k_dash, peak, sems = refs
        t = pl.program_id(0)
        fetch = Pieces(n, z.m, where, pcs, w, sems, 0, z.q_cols, slots)
        pl.when(t == 0)(fetch.start)
        fetch.wait(t)
        bias = jnp.zeros((16, 64), F)
        for s in range(z.m):
            bias = bias + w[t, s * z.share : s * z.share + 16, z.qc :].astype(F)
        bias = rows_to_lanes(bias.astype(B), z.qc)
        table = block_diagonal(feat[0], hl)
        peak[...] = jnp.full((8, z.hm), -1e30, F)

        def queries_keys(r):
            qkv = dot(x[r], w[t, :, : z.qc]) + bias
            q = (qkv[:, : z.oc] * z.scale).astype(B)
            k = (qkv[:, z.oc : 2 * z.oc] * z.scale).astype(B)
            q_out[0, r], k_out[0, r], v_out[0, r] = q, k, qkv[:, 2 * z.oc :].astype(B)
            qd, kd = dot(q, table), dot(k, table)
            qs, ks = q.astype(F), k.astype(F)
            qs, ks = qs * qs, ks * ks
            live = valid[r] > 0
            for h in range(hl):
                seg, cols = slice(h * hd, (h + 1) * hd), slice(h * feats, (h + 1) * feats)
                dash = qd[:, cols] - 0.5 * jnp.sum(qs[:, seg], axis=-1, keepdims=True)
                qf_out[0, r, cols] = jnp.exp(
                    dash - jnp.floor(jnp.max(dash, axis=-1, keepdims=True))
                ).astype(B)
                dash = kd[:, cols] - 0.5 * jnp.sum(ks[:, seg], axis=-1, keepdims=True)
                k_dash[r, cols] = dash
                top = jnp.max(jnp.where(live, dash, -1e30), axis=0, keepdims=True)
                peak[:, cols] = jnp.maximum(peak[:, cols], top)

        over_rows(span, queries_keys)
        tops = []
        for h in range(hl):
            top = jnp.max(peak[0:1, h * feats : (h + 1) * feats], axis=1, keepdims=True)
            tops.append(jnp.broadcast_to(jnp.floor(top), (8, feats)))
        top = jnp.concatenate(tops, axis=1)
        top_out[0] = top

        def keys(r):
            live = valid[r] > 0
            kf_out[0, r] = jnp.where(live, jnp.exp(k_dash[r] - top[0:1]), 0.0).astype(B)

        over_rows(span, keys)
        vx = jnp.concatenate([v_out[0], jnp.ones((span, 64), B)], axis=1)
        state = dot(vx, kf_out[0], 0, 0)
        high = top.astype(B).astype(F)
        mid = (top - high).astype(B).astype(F)
        row, last = iota((8, z.hm), 0), state[z.oc : z.oc + 8]
        for i, term in enumerate((high, mid, top - high - mid)):
            last = jnp.where(row == i + 1, term, last)
        st_out[0] = jnp.concatenate([diagonal_blocks(state[: z.oc], hl), last], axis=0).astype(B)

    return call(
        body,
        (cnt,),
        [SCALARS] + [ANY] * 8 + [fixed(span, z.width), slot(hd, z.hm, first=first), fixed(span, 1)],
        [slot(span, z.oc)] * 3 + [slot(span, z.hm)] * 2 + [slot(hd + 8, z.hm), slot(8, z.hm)],
        [((cnt, span, z.oc), B)] * 3
        + [((cnt, span, z.hm), B)] * 2
        + [((cnt, hd + 8, z.hm), B), ((cnt, 8, z.hm), F)],
        [
            pltpu.VMEM((cnt, z.width, z.q_cols), B),
            pltpu.VMEM((span, z.hm), F),
            pltpu.VMEM((8, z.hm), F),
            pltpu.SemaphoreType.DMA((cnt, 2 * z.m)),
        ],
        "project",
    )(where, *pieces, x, feat, valid)


def attend(z, where, pieces, qf, state, slots, x=None, before=None):
    cnt, first, last = len(slots), slots[0], x is not None
    n, span, hl, hd = z.n, z.span, z.hl, z.hd

    def body(where, *refs):
        pcs, refs = refs[:8], refs[8:]
        qf, state, refs = refs[0], refs[1], refs[2:]
        if last:
            x, before, refs = refs[0], refs[1], refs[2:]
        mixed_out, den_out, bup_out, refs = refs[0], refs[1], refs[2], refs[3:]
        if last:
            normal_out, inverse_out, vec_out, w, acc, sems = refs
        else:
            acc, w, sems = refs
        t = pl.program_id(0)
        fetch = Pieces(n, z.m, where, pcs, w, sems, z.q_cols, z.oc + 64, slots)
        pl.when(t == 0)(fetch.start)
        compact = state[0, :hd]
        total = jnp.broadcast_to(state[0, hd : hd + 1], (hd, z.hm))
        table = stacked(compact, total, hl)
        fetch.wait(t)

        def ratios(r):
            both = dot(qf[0, r], table, 1, 1)
            den = both[:, second_start(z.oc) :]
            mixed = (both[:, : z.oc] / den).astype(B)
            mixed_out[0, r] = mixed
            den_out[0, r] = den
            so_far = jnp.where(t == 0, before[r] if last else 0.0, acc[r])
            acc[r] = dot(mixed, w[t, :, : z.oc], 1, 1) + so_far

        over_rows(span, ratios)
        bias = jnp.zeros((16, 64), F)
        for s in range(z.m):
            bias = bias + w[t, s * z.share + 24 : s * z.share + 40, z.oc :].astype(F)
        bup_out[0] = jnp.broadcast_to(rows_to_lanes(bias.astype(B), z.ff), (8, z.ff))
        if not last:
            return

        @pl.when(t == cnt - 1)
        def _():
            lanes = z.width
            per = z.share // 64
            tile = (iota((64, lanes), 1) % 64 == iota((64, lanes), 0)).astype(F).astype(B)
            found = jnp.zeros((24, lanes), F)
            for s in range(z.m):
                spread = dot(w[0, s * z.share : s * z.share + 24, z.oc :], tile)
                hit = iota((24, lanes), 1) // 64 == per * s + iota((24, lanes), 0) % per
                found = found + jnp.where(hit, spread, 0.0)
            pick = (iota((8, 24), 1) // per == iota((8, 24), 0)).astype(F).astype(B)
            vec = dot(pick, found.astype(B))
            vec_out[...] = vec

            def norm(r):
                res = acc[r] + vec[0:1] + x[r].astype(F)
                normal_out[r], inverse_out[r] = norm_stats(res)

            over_rows(span, norm)

    wide = fixed(span, z.width)
    ins, extra = [slot(span, z.hm), slot(hd + 8, z.hm)], []
    outs = [slot(span, z.oc), slot(span, z.oc), slot(8, z.ff)]
    shapes = [((cnt, span, z.oc), B), ((cnt, span, z.oc), F), ((cnt, 8, z.ff), F)]
    scratch = [pltpu.VMEM((cnt, z.width, z.oc + 64), B)]
    if last:
        ins, extra = ins + [wide, wide], [x, before]
        outs += [wide, fixed(span, 1), fixed(8, z.width)]
        shapes += [((span, z.width), F), ((span, 1), F), ((8, z.width), F)]
        scratch += [pltpu.VMEM((span, z.width), F)]
    else:
        outs, shapes = outs + [wide], shapes + [((span, z.width), F)]
    return call(
        body,
        (cnt,),
        [SCALARS] + [ANY] * 8 + ins,
        outs,
        shapes,
        scratch + [pltpu.SemaphoreType.DMA((cnt, 2 * z.m))],
        "attend",
    )(where, *pieces, qf, state, *extra)


def widen(z, where, pieces, normal, vec, bup):
    n, span = z.n, z.span

    def body(where, *refs):
        pcs, refs = refs[:8], refs[8:]
        normal, vec, bup, act_out, slope_out, w, low, sems = refs
        t = pl.program_id(0)
        fetch = Pieces(n, z.m, where, pcs, w, sems, 0, z.ff)

        @pl.when(t == 0)
        def _():
            fetch.start()
            low[...] = (normal[...] * vec[1:2] + vec[2:3]).astype(B)

        fetch.wait(t)

        def hidden(r):
            up = dot(low[r], w[t]) + bup[0, 0:1]
            share = 0.5 * (1.0 + lax.erf(up * 0.7071067811865476))
            act_out[0, r] = (up * share).astype(B)
            slope_out[0, r] = (share + up * jnp.exp(-0.5 * up * up) * 0.3989422804014327).astype(B)

        over_rows(span, hidden)

    return call(
        body,
        (n,),
        [SCALARS] + [ANY] * 8 + [fixed(span, z.width), fixed(8, z.width), slot(8, z.ff)],
        [slot(span, z.ff)] * 2,
        [((n, span, z.ff), B)] * 2,
        [
            pltpu.VMEM((n, z.width, z.ff), B),
            pltpu.VMEM((span, z.width), B),
            pltpu.SemaphoreType.DMA((n, 2 * z.m)),
        ],
        "widen",
    )(where, *pieces, normal, vec, bup)


def narrow(z, where, pieces, normal, vec, cot, act, slope):
    n, span, rows, m = z.n, z.span, z.rows, z.m

    def body(where, *refs):
        pcs, refs = refs[:8], refs[8:]
        normal, vec, cot, act, slope = refs[:5]
        out, dres_out, low, dup_out, small_out = refs[5:10]
        w, acc, sems = refs[10:]
        p, t = pl.program_id(0), pl.program_id(1)
        fetch = Pieces(n, m, where, pcs, w, sems, 0, z.ff)

        @pl.when((p == 0) & (t == 0))
        def _():
            fetch.start()

        @pl.when(p == 0)
        def _():
            fetch.wait(t)

            def down(r):
                acc[r] = dot(act[0, r], w[t], 1, 1) + jnp.where(t == 0, 0.0, acc[r])

            over_rows(span, down)

        @pl.when((p == 0) & (t == n - 1))
        def _():
            small_out[...] = jnp.zeros((8, z.width), F)

            def norm(r):
                normed = normal[r] * vec[1:2] + vec[2:3]
                second, inverse = norm_stats(acc[r] + vec[3:4] + normed)
                out[r] = (second * vec[4:5] + vec[5:6]).astype(B)
                up = cot[r].astype(F)
                dres = norm_back(second, inverse, vec[4:5], up)
                dres_out[r] = dres
                low[r] = dres.astype(B)
                small_out[...] += as_rows(
                    [
                        jnp.sum(dres, axis=0, keepdims=True),
                        jnp.sum(up * second, axis=0, keepdims=True),
                        jnp.sum(up, axis=0, keepdims=True),
                    ],
                    3,
                )

            over_rows(span, norm)

        @pl.when(p == 1)
        def _():
            def up_back(r):
                dup_out[0, r] = (dot(low[r], w[t]) * slope[0, r].astype(F)).astype(B)

            over_rows(span, up_back)

    second = lambda *shape: pl.BlockSpec((1,) + shape, lambda p, t: (p * t,) + (0,) * len(shape))
    return call(
        body,
        (2, n),
        [SCALARS]
        + [ANY] * 8
        + [
            fixed(span, z.width),
            fixed(8, z.width),
            fixed(span, z.width),
            pl.BlockSpec((1, span, z.ff), lambda p, t: (t * (1 - p) + (n - 1) * p, 0, 0)),
            second(span, z.ff),
        ],
        [fixed(span, z.width)] * 3 + [second(span, z.ff), fixed(8, z.width)],
        [
            ((span, z.width), B),
            ((span, z.width), F),
            ((span, z.width), B),
            ((n, span, z.ff), B),
            ((8, z.width), F),
        ],
        [
            pltpu.VMEM((n, z.width, z.ff), B),
            pltpu.VMEM((span, z.width), F),
            pltpu.SemaphoreType.DMA((n, 2 * m)),
        ],
        "narrow",
    )(where, *pieces, normal, vec, cot, act, slope)


def ffn_grad(z, where, normal, vec, d_ffn, act, dup):
    n, span, rows, m = z.n, z.span, z.rows, z.m

    def body(where, normal, vec, d_ffn, act, dup, keep, give, bup_out, low_t, normed_t, spare):
        t = pl.program_id(0)

        @pl.when(t == 0)
        def _():
            turn(low_t, spare, d_ffn[...].astype(F).T.astype(B), where, m)
            turn(normed_t, spare, (normal[...] * vec[1:2] + vec[2:3]).T.astype(B), where, m)

        store_turned(dot(low_t[...], act[0]), 0, keep, give, m)
        store_turned(dot(normed_t[...], dup[0]), z.ff, keep, give, m)
        bup_out[0] = jnp.broadcast_to(
            jnp.sum(dup[0].astype(F), axis=0, keepdims=True), (8, z.ff)
        )

    wide, grads = fixed(span, z.width), pl.BlockSpec((m, 1, rows, 2 * z.ff), lambda t: (0, t, 0, 0))
    return call(
        body,
        (n,),
        [SCALARS, wide, fixed(8, z.width), wide, slot(span, z.ff), slot(span, z.ff)],
        [grads, grads, slot(8, z.ff)],
        [((m, n, rows, 2 * z.ff), B)] * 2 + [((n, 8, z.ff), F)],
        [pltpu.VMEM((z.width, span), B)] * 3,
        "ffn_grad",
    )(where, normal, vec, d_ffn, act, dup)


def widen_back(z, where, pieces, normal, inverse, vec, dup, dres):
    n, span = z.n, z.span

    def body(where, *refs):
        pcs, refs = refs[:8], refs[8:]
        normal, inverse, vec, dup, dres, out, small_out, w, acc, sems = refs
        t = pl.program_id(0)
        fetch = Pieces(n, z.m, where, pcs, w, sems, 0, z.ff)
        pl.when(t == 0)(fetch.start)
        fetch.wait(t)

        def back(r):
            acc[r] = dot(dup[0, r], w[t], 1, 1) + jnp.where(t == 0, dres[r], acc[r])

        over_rows(span, back)

        @pl.when(t == n - 1)
        def _():
            small_out[...] = jnp.zeros((8, z.width), F)

            def norm(r):
                up = acc[r]
                back = norm_back(normal[r], inverse[r], vec[1:2], up)
                out[r] = back
                small_out[...] += as_rows(
                    [
                        jnp.sum(back, axis=0, keepdims=True),
                        jnp.sum(up * normal[r], axis=0, keepdims=True),
                        jnp.sum(up, axis=0, keepdims=True),
                    ],
                    0,
                )

            over_rows(span, norm)

    return call(
        body,
        (n,),
        [SCALARS]
        + [ANY] * 8
        + [
            fixed(span, z.width),
            fixed(span, 1),
            fixed(8, z.width),
            slot(span, z.ff),
            fixed(span, z.width),
        ],
        [fixed(span, z.width), fixed(8, z.width)],
        [((span, z.width), F), ((8, z.width), F)],
        [
            pltpu.VMEM((n, z.width, z.ff), B),
            pltpu.VMEM((span, z.width), F),
            pltpu.SemaphoreType.DMA((n, 2 * z.m)),
        ],
        "widen_back",
    )(where, *pieces, normal, inverse, vec, dup, dres)


def attend_back(z, where, pieces, dres, mixed, den, qf, q, state, feat, slots):
    cnt, first = len(slots), slots[0]
    n, span, hl, hd, m = z.n, z.span, z.hl, z.hd, z.m

    def body(where, *refs):
        pcs, refs = refs[:8], refs[8:]
        dres, mixed, den, qf, q, state, feat, dq_out, dstate_out, w, low, pair, sems = refs
        t = pl.program_id(0)
        fetch = Pieces(n, m, where, pcs, w, sems, z.q_cols, z.oc + 64, slots)

        @pl.when(t == 0)
        def _():
            fetch.start()
            low[...] = dres[...].astype(B)

        fetch.wait(t)
        start = second_start(z.oc)
        compact = state[0, :hd]
        total = jnp.broadcast_to(state[0, hd : hd + 1], (hd, z.hm))
        states, tables = stacked(compact, total, hl), stacked(feat[0], jnp.ones((hd, z.hm), B), hl)

        def back(r):
            d_mixed = dot(low[r], w[t, :, : z.oc]).astype(B).astype(F)
            d_num = d_mixed / den[0, r]
            d_den = -(d_num * mixed[0, r].astype(F))
            both = beside(d_num.astype(B), d_den.astype(B))
            pair[r] = both
            dash = (dot(both, states) * qf[0, r].astype(F)).astype(B)
            back = dot(dash, tables, 1, 1)
            dq_out[0, r] = ((back[:, : z.oc] - q[0, r].astype(F) * back[:, start:]) * z.scale).astype(B)

        over_rows(span, back)
        full = dot(pair[...], qf[0], 0, 0)
        row = jnp.concatenate(
            [
                jnp.sum(
                    full[start + h * hd : start + (h + 1) * hd, h * z.feats : (h + 1) * z.feats],
                    axis=0,
                    keepdims=True,
                )
                for h in range(hl)
            ],
            axis=1,
        )
        dstate_out[0] = jnp.concatenate(
            [diagonal_blocks(full[: z.oc], hl), jnp.broadcast_to(row, (8, z.hm))], axis=0
        ).astype(B)

    return call(
        body,
        (cnt,),
        [SCALARS]
        + [ANY] * 8
        + [
            fixed(span, z.width),
            slot(span, z.oc),
            slot(span, z.oc),
            slot(span, z.hm),
            slot(span, z.oc),
            slot(hd + 8, z.hm),
            slot(hd, z.hm, first=first),
        ],
        [slot(span, z.oc), slot(hd + 8, z.hm)],
        [((cnt, span, z.oc), B), ((cnt, hd + 8, z.hm), B)],
        [
            pltpu.VMEM((cnt, z.width, z.oc + 64), B),
            pltpu.VMEM((span, z.width), B),
            pltpu.VMEM((span, second_start(z.oc) + z.oc), B),
            pltpu.SemaphoreType.DMA((cnt, 2 * m)),
        ],
        "attend_back",
    )(where, *pieces, dres, mixed, den, qf, q, state, feat)


def project_back(z, where, pieces, x, dres, dq, k, v, kf, dstate, feat, mixed, small_a, small_b, dbup, slots, before=None):
    cnt, first, last = len(slots), slots[0], before is not None
    n, span, hl, hd, m, rows = z.n, z.span, z.hl, z.hd, z.m, z.rows
    cols = z.a_cols

    def body(where, *refs):
        pcs, refs = refs[:8], refs[8:]
        x, dres, dq, k, v, kf, dstate, feat, mixed, small_a, small_b, dbup = refs[:12]
        refs = refs[12:]
        if last:
            before, refs = refs[0], refs[1:]
            keep, give, out, w, x_t, low_t, spare, dqkv_low, acc, sems = refs
        else:
            keep, give, acc, w, x_t, low_t, spare, dqkv_low, sems = refs
        t = pl.program_id(0)
        fetch = Pieces(n, m, where, pcs, w, sems, 0, z.q_cols, slots)

        @pl.when(t == 0)
        def _():
            fetch.start()
            turn(x_t, spare, x[...].astype(F).T.astype(B), where, m)
            turn(low_t, spare, dres[...].T.astype(B), where, m)

        start = second_start(z.oc)
        table = block_diagonal(dstate[0, :hd], hl)
        total = dstate[0, hd : hd + 1].astype(F)
        dash = ((dot(v[0], table) + total) * kf[0].astype(F)).astype(B)
        dv = dot(kf[0], table, 1, 1)
        back = dot(dash, stacked(feat[0], jnp.ones((hd, z.hm), B), hl), 1, 1)
        dk = (back[:, : z.oc] - k[0].astype(F) * back[:, start:]) * z.scale
        dqkv = jnp.concatenate(
            [dq[0], dk.astype(B), dv.astype(B), jnp.zeros((span, 64), B)], axis=1
        )
        dqkv_low[...] = dqkv
        bias = jnp.sum(dqkv.astype(F), axis=0, keepdims=True)
        laid = jnp.broadcast_to(bias, (rows, z.q_cols))
        laid = jnp.where(iota(laid.shape, 1) // 64 == iota(laid.shape, 0), laid, 0.0)
        grad = dot(x_t[...], dqkv)
        edge = z.q_cols - 128
        store_turned(grad[:, :edge], 0, keep, give, m)
        store_turned(
            grad[:, edge:] + jnp.concatenate([folded(laid)] * (2 * m), axis=0), edge, keep, give, m
        )
        grad = dot(low_t[...], jnp.concatenate([mixed[0], jnp.zeros((span, 64), B)], axis=1))
        packed = small_a[...] + small_b[...] + as_rows([dbup[0, 0:1]], 6)
        per = z.width // 64
        one = (iota((rows, 8), 0) // per == iota((rows, 8), 1)).astype(F).astype(B)
        laid = dot(one, packed.astype(B))
        laid = jnp.where(iota(laid.shape, 1) // 64 == iota(laid.shape, 0) % per, laid, 0.0)
        edge = z.oc + 64 - 128
        store_turned(grad[:, :edge], z.q_cols, keep, give, m)
        store_turned(
            grad[:, edge:] + jnp.concatenate([folded(laid)] * (2 * m), axis=0),
            z.q_cols + edge,
            keep,
            give,
            m,
        )
        fetch.wait(t)

        def tokens_back(r):
            so_far = jnp.where(t == 0, before[r] if last else dres[r], acc[r])
            acc[r] = dot(dqkv_low[r], w[t], 1, 1) + so_far

        over_rows(span, tokens_back)

        if last:

            @pl.when(t == cnt - 1)
            def _():
                out[...] = acc[...].astype(B)

    grads = pl.BlockSpec((m, 1, rows, cols), lambda t: (0, t, 0, 0))
    wide, scratch = fixed(span, z.width), [pltpu.VMEM((cnt, z.width, z.q_cols), B)]
    scratch += [pltpu.VMEM((z.width, span), B)] * 3 + [pltpu.VMEM((span, z.q_cols), B)]
    if last:
        scratch += [pltpu.VMEM((span, z.width), F)]
    return call(
        body,
        (cnt,),
        [SCALARS]
        + [ANY] * 8
        + [
            wide,
            wide,
            slot(span, z.oc),
            slot(span, z.oc),
            slot(span, z.oc),
            slot(span, z.hm),
            slot(hd + 8, z.hm),
            slot(hd, z.hm, first=first),
            slot(span, z.oc),
            fixed(8, z.width),
            fixed(8, z.width),
            slot(8, z.ff, first=first),
        ]
        + ([wide] if last else []),
        [grads, grads, wide],
        [((m, cnt, rows, cols), B)] * 2 + [((span, z.width), B if last else F)],
        scratch + [pltpu.SemaphoreType.DMA((cnt, 2 * m))],
        "project_back",
    )(
        where, *pieces, x, dres, dq, k, v, kf, dstate, feat, mixed, small_a, small_b, dbup,
        *([before] if last else []),
    )


def place(part, axis, index, count):
    shape = list(part.shape)
    shape[axis] *= count
    return lax.dynamic_update_slice_in_dim(
        jnp.zeros(shape, part.dtype), part, index * part.shape[axis], axis
    )


def on_device(
    sizes,
    tokens,
    lengths,
    features,
    w_qkv,
    b_qkv,
    w_out,
    b_out,
    gain_one,
    shift_one,
    w_up,
    b_up,
    w_down,
    b_down,
    gain_two,
    shift_two,
    cotangent,
):
    links = Links(sizes)
    z = Shape(sizes, features, tokens, b_up)
    n, m, share = z.n, z.m, z.share
    where = jnp.stack([links.s, links.core]).astype(jnp.int32)
    def tall(value):
        return jnp.pad(value, ((0, share - value.shape[0]), (0, 0)))

    biases = place(b_qkv, 2, links.s, m).reshape(3 * z.hl, z.hd)
    vectors = gather_rows([b_out, gain_one, shift_one, b_down, gain_two, shift_two], 24)
    vectors = jnp.concatenate([vectors, place(b_up, 1, links.s, m).reshape(-1, 64)])
    local_a = links.half(
        jnp.concatenate([w_qkv.reshape(share, z.qc), tall(biases), w_out.T, tall(vectors)], axis=1)
    )
    feat_half = links.half(features.transpose(2, 0, 1).reshape(z.hd, z.hm))
    local_u, local_d = links.half(w_up), links.half(w_down.T)
    length = lax.dynamic_index_in_dim(lengths, links.t, 0, keepdims=False)
    order = (links.t - jnp.arange(n)) % n
    position = links.c * z.span + order[:, None] * z.chunk + jnp.arange(z.chunk)[None]
    valid = (position.reshape(-1, 1) < length).astype(F)
    halves = (range(n // 2), range(n // 2, n))
    lo, hi = halves

    def join_states(state, top, came):
        row, mask = z.hd + 1, 1
        own = most = top[:, :1]
        while mask < sizes["context"]:
            if mask > 1:
                came = links.perm_c(state, mask), links.perm_c(top, mask)
                other, other_top = came[0], came[1][:, :1]
            else:
                other = came
                other_top = wide_add(*[other[:, row + i : row + i + 1] for i in range(3)])
            joint = jnp.maximum(most, other_top)
            state = (
                state.astype(F) * jnp.exp(most - joint) + other.astype(F) * jnp.exp(other_top - joint)
            ).astype(B)
            most, mask = joint, 2 * mask
            top = jnp.broadcast_to(most, top.shape)
        return state, jnp.exp(own - most)

    def join_grads(state, came, fall):
        mask = 1
        while mask < sizes["context"]:
            other = came if mask == 1 else links.perm_c(state, mask)
            state = wide_add(state, other).astype(B)
            mask *= 2
        return (state.astype(F) * fall).astype(B)

    block_a = links.spread_t(local_a)
    block_a, tokens, feat_half = together(block_a, tokens, feat_half)
    near_a = links.spread_near(block_a)
    moved = links.carry(tokens, feat_half, range(1, n))
    block_a, near_a, moved, local_u, tokens, feat_half = together(
        block_a, near_a, moved, local_u, tokens, feat_half
    )
    far_a = links.spread_far(near_a)
    other_a = links.swap((block_a,) + near_a)
    x, feat_mine = links.unload(tokens, feat_half, moved)
    far_a, feat_mine, other_a, local_u, valid, x = together(far_a, feat_mine, other_a, local_u, valid, x)
    far_a = (jnp.concatenate(far_a),)
    other_a += links.swap(far_a)
    feat_other = links.perm_c(feat_mine)
    feat_low = jnp.where(links.core == 0, feat_mine, feat_other)
    feat_high = jnp.where(links.core == 0, feat_other, feat_mine)
    feat = jnp.concatenate([feat_low, feat_high], axis=1)
    feat, other_a, local_u = together(feat, other_a, local_u)
    pieces_a = (block_a,) + near_a + far_a + other_a
    block_u = links.spread_t(local_u)
    first = project(z, where, pieces_a, x, feat, valid, lo)
    first, block_u, local_d, valid, cot = together(first, block_u, local_d, valid, cotangent)
    near_u = links.spread_near(block_u)
    moved = links.carry(cot, local_d, (2,))
    other_u = links.swap((block_u,))
    came = links.perm_c(first[5])
    second = project(z, where, pieces_a, x, feat, valid, hi)
    first, second, near_u, block_u, other_u, moved, came, cot, local_d = together(
        first, second, near_u, block_u, other_u, moved, came, cot, local_d
    )
    made = (first, second)
    far_u = links.spread_far(near_u)
    moved.update(links.carry(cot, local_d, (1, 3)))
    came_b = links.perm_c(second[5])
    state_a, fall_a = join_states(first[5], first[6], came)
    one = attend(z, where, pieces_a, first[3], state_a, lo)
    one, far_u, near_u, other_u, moved, came_b, cot, local_d = together(
        one, far_u, near_u, other_u, moved, came_b, cot, local_d
    )
    mixed_a, den_a, bup_a, acc = one
    far_u = (jnp.concatenate(far_u),)
    cot, block_d = links.unload(cot, local_d, moved)
    near_d = links.spread_near(block_d)
    other_u += links.swap(near_u + far_u)
    state_b, fall_b = join_states(second[5], second[6], came_b)
    two = attend(z, where, pieces_a, second[3], state_b, hi, x, acc)
    two, near_d, block_d, other_u, cot = together(two, near_d, block_d, other_u, cot)
    mixed_b, den_b, bup_b, normal, inverse, vec = two
    states, falls = (state_a, state_b), (fall_a, fall_b)
    bup = jnp.concatenate([bup_a, bup_b])
    mixed, den = (mixed_a, mixed_b), (den_a, den_b)
    pieces_u = (block_u,) + near_u + far_u + other_u
    far_d = links.spread_far(near_d)
    other_d = links.swap((block_d,) + near_d)
    act, slope = widen(z, where, pieces_u, normal, vec, bup)
    act, slope, far_d, other_d = together(act, slope, far_d, other_d)
    far_d = (jnp.concatenate(far_d),)
    other_d += links.swap(far_d)
    pieces_d = (block_d,) + near_d + far_d + other_d
    out, d_res_two, d_ffn, dup, small_b = narrow(
        z, where, pieces_d, normal, vec, cot, act, slope
    )
    sent = links.undeal_some(out, (2,))
    keep, give, dbup = ffn_grad(z, where, normal, vec, d_ffn, act, dup)
    keep, give, out, dup, sent = together(keep, give, out, dup, sent)
    other = links.perm_c(give)
    sent.update(links.undeal_some(out, (1, 3)))
    d_res_one, small_a = widen_back(z, where, pieces_u, normal, inverse, vec, dup, d_res_two)
    d_res_one, keep, other, sent = together(d_res_one, keep, other, sent)
    result = links.undealt(out, sent, B)
    slots_f = keep, other
    split = lambda slots: ([term[:, : n // 2] for term in slots], [term[:, n // 2 :] for term in slots])
    one_f = links.collect_one(*split(slots_f))
    dq_a, d_state_a = attend_back(
        z, where, pieces_a, d_res_one, mixed[0], den[0], made[0][3], made[0][0], states[0], feat, lo
    )
    dq_a, d_state_a, d_res_one, slots_f = together(dq_a, d_state_a, d_res_one, slots_f)
    came = links.perm_c(d_state_a)
    dq_b, d_state_b = attend_back(
        z, where, pieces_a, d_res_one, mixed[1], den[1], made[1][3], made[1][0], states[1], feat, hi
    )
    dq_b, d_state_b, came, one_f, slots_f, x = together(dq_b, d_state_b, came, one_f, slots_f, x)
    two_f = links.collect_two(*split(slots_f), one_f)
    came_b = links.perm_c(d_state_b)
    d_state_a = join_grads(d_state_a, came, falls[0])
    dq = (dq_a, dq_b)

    def run_back(i, d_state, x, before):
        return project_back(
            z, where, pieces_a, x, d_res_one, dq[i], made[i][1], made[i][2], made[i][4],
            d_state, feat, mixed[i], small_a, small_b, dbup, halves[i], before,
        )

    keep, give, acc = run_back(0, d_state_a, x, None)
    keep, give, acc, two_f, came_b, slots_f, x = together(keep, give, acc, two_f, came_b, slots_f, x)
    sums_f = links.sums(*split(slots_f), one_f, two_f)
    terms_f = links.collect_t(sums_f, (1, 2))
    other = links.perm_c(give)
    d_state_b = join_grads(d_state_b, came_b, falls[1])
    keep_b, give_b, grad_x = run_back(1, d_state_b, x, acc)
    keep_b, give_b, grad_x, keep, other, terms_f, sums_f = together(
        keep_b, give_b, grad_x, keep, other, terms_f, sums_f
    )
    other_b = links.perm_c(give_b)
    terms_f += links.collect_t(sums_f, range(3, n))
    keep_b, other_b, grad_x = together(keep_b, other_b, grad_x)
    low, high = (keep, other), (keep_b, other_b)
    one = links.collect_one(low, high)
    sent = links.undeal_some(grad_x, (2,))
    one, low, high, sent, grad_x, terms_f = together(one, low, high, sent, grad_x, terms_f)
    two = links.collect_two(low, high, one)
    sent.update(links.undeal_some(grad_x, (1, 3)))
    two, one, low, high, sent, grad_x = together(two, one, low, high, sent, grad_x)
    grad_tokens = links.undealt(grad_x, sent, F)
    sums = links.sums(low, high, one, two)
    terms = [sums[0]] + links.collect_t(sums, range(1, n))
    terms_f = [sums_f[0]] + terms_f
    own_ffn = links.collect_end(terms_f)
    grad_up, grad_down = own_ffn[:, z.ff :].astype(F), own_ffn[:, : z.ff].T.astype(F)
    terms, grad_tokens, result, grad_up, grad_down = together(
        terms, grad_tokens, result, grad_up, grad_down
    )
    own_qkv = links.collect_end(terms)
    def mine(value, axis):
        size = value.shape[axis] // m
        return lax.dynamic_slice_in_dim(value, links.s * size, size, axis).astype(F)

    own_b_qkv = mine(own_qkv[: 3 * z.hl, z.qc : z.q_cols].reshape(3, z.hl, z.hd), 2)
    own_out = own_qkv[:, z.q_cols : z.q_cols + z.oc]
    tail = own_qkv[: z.rows, z.q_cols + z.oc :]
    vecs = mine(tail[: 6 * z.width // 64].reshape(6, z.width), 1)
    start = 6 * z.width // 64
    own_b_up = mine(tail[start : start + z.ff // 64].reshape(b_up.shape[0], -1), 1)
    return (
        result,
        grad_tokens,
        own_qkv[:, : z.qc].reshape(w_qkv.shape).astype(F),
        own_b_qkv,
        own_out.T.astype(F),
        vecs[0],
        vecs[1],
        vecs[2],
        grad_up,
        own_b_up,
        grad_down,
        vecs[3],
        vecs[4],
        vecs[5],
    )


def solution(mesh):
    sizes = dict(mesh.shape)
    in_specs = (
        P("shard", ("context", "tensor"), None),
        P("shard"),
        P("tensor", None, None),
        P("shard", None, "tensor", None),
        P(None, "tensor", "shard"),
        P("tensor", "shard"),
        P("shard"),
        P("shard"),
        P("shard"),
        P("shard", "tensor"),
        P("tensor", "shard"),
        P("tensor", "shard"),
        P("shard"),
        P("shard"),
        P("shard"),
        P("shard", ("context", "tensor"), None),
    )
    out_specs = (
        P("shard", ("context", "tensor"), None),
        P("shard", ("context", "tensor"), None),
        P("shard", None, "tensor", None),
        P(None, "tensor", "shard"),
        P("tensor", "shard"),
        P("shard"),
        P("shard"),
        P("shard"),
        P("shard", "tensor"),
        P("tensor", "shard"),
        P("tensor", "shard"),
        P("shard"),
        P("shard"),
        P("shard"),
    )
    return jax.shard_map(
        functools.partial(on_device, sizes),
        mesh=mesh,
        in_specs=in_specs,
        out_specs=out_specs,
        check_vma=False,
    )
```

```python
import functools

import jax
import jax.numpy as jnp
from jax import lax
from jax.experimental import pallas as pl
from jax.experimental.pallas import tpu as pltpu
from jax.sharding import PartitionSpec as P

F = jnp.float32
B = jnp.bfloat16
ORDER = (0, 1, 3, 2)


def wide_add(*terms):
    total = terms[0].astype(F)
    for term in terms[1:]:
        total = total + term.astype(F)
    return total


def together(*values):
    return lax.optimization_barrier(values)


class Links:
    def __init__(self, sizes):
        self.sizes = sizes
        self.s = lax.axis_index("shard")
        self.c = lax.axis_index("context")
        self.t = lax.axis_index("tensor")
        self.core = self.c % 2

    def perm_t(self, value, step):
        n = self.sizes["tensor"]
        return lax.ppermute(value, "tensor", [(i, (i + step) % n) for i in range(n)])

    def by_length(self):
        n = self.sizes["tensor"]
        return sorted(range(1, n), key=lambda d: -min(d, n - d))

    def perm_s(self, value, mask):
        n = self.sizes["shard"]
        return lax.ppermute(value, "shard", [(i, i ^ mask) for i in range(n)])

    def perm_c(self, value, mask=1):
        n = self.sizes["context"]
        return lax.ppermute(value, "context", [(i, i ^ mask) for i in range(n)])

    def undeal_some(self, rows, steps):
        n = self.sizes["tensor"]
        rows = rows.reshape(n, rows.shape[0] // n, rows.shape[1])
        return {d: self.perm_t(rows[d], n - d) for d in steps if d < n}

    def undealt(self, rows, moved, dtype):
        n = self.sizes["tensor"]
        rows = rows.reshape(n, rows.shape[0] // n, rows.shape[1])
        return lay(self.t, [rows[0]] + [moved[d] for d in range(1, n)], dtype)

    def half(self, local):
        rows = local.shape[0] // 2
        return lax.dynamic_slice_in_dim(local, self.core * rows, rows, 0)

    def spread_t(self, local):
        n = self.sizes["tensor"]
        steps = self.by_length()
        moved = dict(zip(steps, together(*[self.perm_t(local, d) for d in steps])))
        return jnp.stack([local] + [moved[d] for d in range(1, n)])

    def spread_near(self, block):
        return self.perm_s(block, 1), self.perm_s(block, 2)

    def spread_far(self, near):
        h = self.sizes["tensor"] // 2
        over_x, over_y = near
        return self.perm_s(over_x[:h], 2), self.perm_s(over_y[h:], 1)

    def carry(self, rows, extra, steps):
        n = self.sizes["tensor"]
        take = lambda d: lax.dynamic_index_in_dim(rows, (self.t + d) % n, 0, keepdims=False)
        return {d: self.perm_t(jnp.concatenate([take(d), extra]), d) for d in steps if d < n}

    def unload(self, rows, extra, moved):
        length = rows.shape[1]
        own = lax.dynamic_index_in_dim(rows, self.t, 0, keepdims=False)
        steps = sorted(moved)
        return (
            jnp.concatenate([own] + [moved[d][:length] for d in steps]),
            jnp.stack([extra] + [moved[d][length:] for d in steps]),
        )

    def swap(self, values):
        return tuple(self.perm_c(value) for value in values)

    def collect_one(self, low, high):
        return (
            self.perm_s(wide_add(*[term[1:3] for term in high]).astype(B), 1),
            self.perm_s(wide_add(*[term[2:4] for term in low]).astype(B), 2),
        )

    def collect_two(self, low, high, one):
        return (
            self.perm_s(wide_add(*[term[1] for term in low], one[1][0]).astype(B), 1),
            self.perm_s(wide_add(*[term[3] for term in high], one[0][1]).astype(B), 2),
        )

    def sums(self, low, high, one, two):
        return jnp.concatenate(
            [
                wide_add(*[term[0] for term in low], two[0], one[1][1]).astype(B),
                wide_add(*[term[0] for term in high], one[0][0], two[1]).astype(B),
            ]
        )

    def collect_t(self, total, slots):
        n = self.sizes["tensor"]
        return [self.perm_t(total[i], n - i) for i in slots if i < n]

    def collect_end(self, terms):
        total = wide_add(*terms)
        mask = 2
        while mask < self.sizes["context"]:
            low = total.astype(B)
            total = wide_add(low, self.perm_c(low, mask))
            mask *= 2
        low = total.astype(B)
        other = self.perm_c(low)
        first = jnp.where(self.core == 0, low, other)
        second = jnp.where(self.core == 0, other, low)
        return jnp.concatenate([first, second])


def dot(a, b, ca=1, cb=0):
    return lax.dot_general(a, b, (((ca,), (cb,)), ((), ())), preferred_element_type=F)


def iota(shape, axis):
    return lax.broadcasted_iota(jnp.int32, shape, axis)


def block_diagonal(compact, heads):
    k, m = compact.shape[0], compact.shape[1] // heads
    zero = jnp.zeros((k, m), compact.dtype)
    rows = []
    for h in range(heads):
        row = [zero] * heads
        row[h] = compact[:, h * m : (h + 1) * m]
        rows.append(jnp.concatenate(row, axis=1))
    return jnp.concatenate(rows, axis=0)


def diagonal_blocks(full, heads):
    k, m = full.shape[0] // heads, full.shape[1] // heads
    return jnp.concatenate(
        [full[h * k : (h + 1) * k, h * m : (h + 1) * m] for h in range(heads)], axis=1
    )


def stacked(upper, lower, heads):
    a, b = block_diagonal(upper, heads), block_diagonal(lower, heads)
    gap = jnp.zeros((second_start(a.shape[0]) - a.shape[0], a.shape[1]), a.dtype)
    return jnp.concatenate([a, gap, b], axis=0)


def second_start(width):
    return -(-width // 128) * 128


def beside(left, right):
    gap = jnp.zeros((left.shape[0], second_start(left.shape[1]) - left.shape[1]), left.dtype)
    return jnp.concatenate([left, gap, right], axis=1)


def rows_to_lanes(rows, lanes):
    k = rows.shape[1]
    tile = (iota((k, lanes), 1) % k == iota((k, lanes), 0)).astype(F).astype(B)
    spread = dot(rows, tile)
    hit = iota(spread.shape, 1) // k == iota(spread.shape, 0)
    return jnp.sum(jnp.where(hit, spread, 0.0), axis=0, keepdims=True)


class Pieces:
    def __init__(self, n, m, where, refs, dest, sems, start, cols, slots=None):
        self.n, self.m, self.where, self.refs = n, m, where, refs
        self.slots = slots or range(n)
        self.dest, self.sems, self.start_col, self.cols = dest, sems, start, cols
        self.rows = refs[0].shape[1]

    def copies(self, t):
        s, c = self.where[0], self.where[1]
        made = []
        for i in range(2):
            half = c if i == 0 else 1 - c
            for j in range(self.m):
                row = pl.multiple_of((s ^ j) * (2 * self.rows) + half * self.rows, 8)
                src = self.refs[i * self.m + j].at[t]
                src = src.at[:, pl.ds(self.start_col, self.cols)]
                u = t - self.slots[0]
                target = self.dest.at[u, pl.ds(row, self.rows)]
                made.append(pltpu.make_async_copy(src, target, self.sems.at[u, i * self.m + j]))
        return made

    def start(self):
        for t in self.slots:
            for copy in self.copies(t):
                copy.start()

    def wait(self, t):
        for u in self.slots:

            @pl.when(t == u - self.slots[0])
            def _():
                for copy in self.copies(u):
                    copy.wait()


ANY = pl.BlockSpec(memory_space=pl.ANY)
SCALARS = pl.BlockSpec(memory_space=pltpu.SMEM)


def slot(*shape, first=0):
    zeros = (0,) * len(shape)
    return pl.BlockSpec((1,) + shape, lambda t: (t + first,) + zeros)


def fixed(*shape):
    zeros = (0,) * len(shape)
    return pl.BlockSpec(shape, lambda *_: zeros)


COST = {
    "project": 11,
    "attend": 6,
    "widen": 10,
    "narrow": 13,
    "ffn_grad": 9,
    "widen_back": 10,
    "attend_back": 7,
    "project_back": 11,
}


def call(body, grid, in_specs, out_specs, outs, scratch, name, flops=0):
    return pl.pallas_call(
        body,
        grid=grid,
        in_specs=in_specs,
        out_specs=out_specs,
        out_shape=[jax.ShapeDtypeStruct(s, d) for s, d in outs],
        scratch_shapes=scratch,
        compiler_params=pltpu.CompilerParams(
            dimension_semantics=("arbitrary",) * len(grid), vmem_limit_bytes=60 * 1024 * 1024
        ),
        cost_estimate=pl.CostEstimate(
            flops=COST[name] * 300_000_000, transcendentals=0, bytes_accessed=COST[name] * 800_000
        ),
        name=name,
    )


def lay(t, chunks, dtype):
    n, shape = len(chunks), chunks[0].shape

    def body(t, *refs):
        for d in range(n):

            @pl.when(pl.program_id(0) == d)
            def _():
                refs[n][0] = refs[d][...].astype(dtype)

    return pl.pallas_call(
        body,
        grid_spec=pltpu.PrefetchScalarGridSpec(
            num_scalar_prefetch=1,
            grid=(n,),
            in_specs=[pl.BlockSpec(shape, lambda d, t: (0, 0))] * n,
            out_specs=pl.BlockSpec((1,) + shape, lambda d, t: ((t[0] + d) % n, 0, 0)),
        ),
        out_shape=jax.ShapeDtypeStruct((n,) + shape, dtype),
        cost_estimate=pl.CostEstimate(flops=0, transcendentals=0, bytes_accessed=800_000),
        compiler_params=pltpu.CompilerParams(dimension_semantics=("arbitrary",)),
        name="lay",
    )(t[None].astype(jnp.int32), *chunks)


def gather_rows(vectors, count):
    def body(*refs):
        row, k = iota((count, 64), 0), 0
        total = jnp.zeros((count, 64), F)
        for ref in refs[:-1]:
            value = ref[...].astype(F).reshape(1, ref.shape[0])
            for start in range(0, ref.shape[0], 64):
                total = jnp.where(row == k, value[:, start : start + 64], total)
                k += 1
        refs[-1][...] = total.astype(B)

    return pl.pallas_call(
        body,
        out_shape=jax.ShapeDtypeStruct((count, 64), B),
        cost_estimate=pl.CostEstimate(flops=0, transcendentals=0, bytes_accessed=8_000),
        name="gather_rows",
    )(*vectors)


def norm_stats(res):
    mean = jnp.mean(res, axis=-1, keepdims=True)
    centered = res - mean
    var = jnp.mean(centered * centered, axis=-1, keepdims=True)
    inverse = lax.rsqrt(var + 1e-05)
    return centered * inverse, inverse


def norm_back(normal, inverse, gain, upstream):
    scaled = upstream * gain
    inner = (
        scaled
        - jnp.mean(scaled, axis=-1, keepdims=True)
        - normal * jnp.mean(scaled * normal, axis=-1, keepdims=True)
    )
    return inner * inverse


def as_rows(vectors, first):
    width = vectors[0].shape[1]
    row = iota((8, width), 0)
    total = jnp.zeros((8, width), F)
    for i, vector in enumerate(vectors):
        total = jnp.where(row == first + i, vector, total)
    return total


def turn(dest, spare, value, where, m):
    spare[...] = value
    rows = value.shape[0] // (2 * m)
    s, c = where[0], where[1]
    for part in range(2):
        half = c if part == 0 else 1 - c
        for i in range(m):
            src = pl.multiple_of(((s ^ ORDER[i]) * 2 + half) * rows, 16)
            row = (part * m + i) * rows
            dest[row : row + rows] = spare[pl.ds(src, rows)]


def store_turned(value, col, keep, give, m):
    rows, cols = value.shape[0] // (2 * m), value.shape[1]
    for i in range(m):
        keep[i, 0, :, col : col + cols] = value[i * rows : (i + 1) * rows].astype(B)
        give[i, 0, :, col : col + cols] = value[(m + i) * rows : (m + i + 1) * rows].astype(B)


def folded(laid):
    pair = laid[:, :128]
    for k in range(128, laid.shape[1], 128):
        pair = pair + laid[:, k : k + 128]
    return jnp.concatenate([jnp.zeros((laid.shape[0], 64), F), pair[:, :64] + pair[:, 64:]], axis=1)


def over_rows(span, step_rows):
    step = 256 if span % 256 == 0 else span

    def one(i, carry):
        step_rows(pl.ds(pl.multiple_of(i * step, step), step))
        return carry

    lax.fori_loop(0, span // step, one, 0)


class Shape:
    def __init__(self, sizes, features, tokens, b_up):
        self.n, self.m = sizes["tensor"], sizes["shard"]
        self.hl, self.feats, self.hd = features.shape
        self.chunk, self.width = tokens.shape[1], tokens.shape[2]
        self.span = self.chunk * self.n
        self.share = self.width // self.m
        self.rows = self.share // 2
        self.oc = self.hl * self.hd
        self.qc = 3 * self.oc
        self.hm = self.hl * self.feats
        self.ff = b_up.size * self.m
        self.q_cols = self.qc + 64
        self.a_cols = self.q_cols + self.oc + 64
        self.scale = self.hd ** (-0.25)


def project(z, where, pieces, x, feat, valid, slots):
    cnt, first = len(slots), slots[0]
    n, span, hl, feats, hd = z.n, z.span, z.hl, z.feats, z.hd

    def body(where, *refs):
        pcs, refs = refs[:8], refs[8:]
        x, feat, valid, q_out, k_out, v_out, qf_out, kf_out, st_out, top_out, w, k_dash, peak, sems = refs
        t = pl.program_id(0)
        fetch = Pieces(n, z.m, where, pcs, w, sems, 0, z.q_cols, slots)
        pl.when(t == 0)(fetch.start)
        fetch.wait(t)
        bias = jnp.zeros((16, 64), F)
        for s in range(z.m):
            bias = bias + w[t, s * z.share : s * z.share + 16, z.qc :].astype(F)
        bias = rows_to_lanes(bias.astype(B), z.qc)
        table = block_diagonal(feat[0], hl)
        peak[...] = jnp.full((8, z.hm), -1e30, F)

        def queries_keys(r):
            qkv = dot(x[r], w[t, :, : z.qc]) + bias
            q = (qkv[:, : z.oc] * z.scale).astype(B)
            k = (qkv[:, z.oc : 2 * z.oc] * z.scale).astype(B)
            q_out[0, r], k_out[0, r], v_out[0, r] = q, k, qkv[:, 2 * z.oc :].astype(B)
            qd, kd = dot(q, table), dot(k, table)
            qs, ks = q.astype(F), k.astype(F)
            qs, ks = qs * qs, ks * ks
            live = valid[r] > 0
            for h in range(hl):
                seg, cols = slice(h * hd, (h + 1) * hd), slice(h * feats, (h + 1) * feats)
                dash = qd[:, cols] - 0.5 * jnp.sum(qs[:, seg], axis=-1, keepdims=True)
                qf_out[0, r, cols] = jnp.exp(
                    dash - jnp.floor(jnp.max(dash, axis=-1, keepdims=True))
                ).astype(B)
                dash = kd[:, cols] - 0.5 * jnp.sum(ks[:, seg], axis=-1, keepdims=True)
                k_dash[r, cols] = dash
                top = jnp.max(jnp.where(live, dash, -1e30), axis=0, keepdims=True)
                peak[:, cols] = jnp.maximum(peak[:, cols], top)

        over_rows(span, queries_keys)
        tops = []
        for h in range(hl):
            top = jnp.max(peak[0:1, h * feats : (h + 1) * feats], axis=1, keepdims=True)
            tops.append(jnp.broadcast_to(jnp.floor(top), (8, feats)))
        top = jnp.concatenate(tops, axis=1)
        top_out[0] = top

        def keys(r):
            live = valid[r] > 0
            kf_out[0, r] = jnp.where(live, jnp.exp(k_dash[r] - top[0:1]), 0.0).astype(B)

        over_rows(span, keys)
        vx = jnp.concatenate([v_out[0], jnp.ones((span, 64), B)], axis=1)
        state = dot(vx, kf_out[0], 0, 0)
        high = top.astype(B).astype(F)
        mid = (top - high).astype(B).astype(F)
        row, last = iota((8, z.hm), 0), state[z.oc : z.oc + 8]
        for i, term in enumerate((high, mid, top - high - mid)):
            last = jnp.where(row == i + 1, term, last)
        st_out[0] = jnp.concatenate([diagonal_blocks(state[: z.oc], hl), last], axis=0).astype(B)

    return call(
        body,
        (cnt,),
        [SCALARS] + [ANY] * 8 + [fixed(span, z.width), slot(hd, z.hm, first=first), fixed(span, 1)],
        [slot(span, z.oc)] * 3 + [slot(span, z.hm)] * 2 + [slot(hd + 8, z.hm), slot(8, z.hm)],
        [((cnt, span, z.oc), B)] * 3
        + [((cnt, span, z.hm), B)] * 2
        + [((cnt, hd + 8, z.hm), B), ((cnt, 8, z.hm), F)],
        [
            pltpu.VMEM((cnt, z.width, z.q_cols), B),
            pltpu.VMEM((span, z.hm), F),
            pltpu.VMEM((8, z.hm), F),
            pltpu.SemaphoreType.DMA((cnt, 2 * z.m)),
        ],
        "project",
    )(where, *pieces, x, feat, valid)


def attend(z, where, pieces, qf, state, slots, x=None, before=None):
    cnt, first, last = len(slots), slots[0], x is not None
    n, span, hl, hd = z.n, z.span, z.hl, z.hd

    def body(where, *refs):
        pcs, refs = refs[:8], refs[8:]
        qf, state, refs = refs[0], refs[1], refs[2:]
        if last:
            x, before, refs = refs[0], refs[1], refs[2:]
        mixed_out, den_out, bup_out, refs = refs[0], refs[1], refs[2], refs[3:]
        if last:
            normal_out, inverse_out, vec_out, w, acc, sems = refs
        else:
            acc, w, sems = refs
        t = pl.program_id(0)
        fetch = Pieces(n, z.m, where, pcs, w, sems, z.q_cols, z.oc + 64, slots)
        pl.when(t == 0)(fetch.start)
        compact = state[0, :hd]
        total = jnp.broadcast_to(state[0, hd : hd + 1], (hd, z.hm))
        table = stacked(compact, total, hl)
        fetch.wait(t)

        def ratios(r):
            both = dot(qf[0, r], table, 1, 1)
            den = both[:, second_start(z.oc) :]
            mixed = (both[:, : z.oc] / den).astype(B)
            mixed_out[0, r] = mixed
            den_out[0, r] = den
            so_far = jnp.where(t == 0, before[r] if last else 0.0, acc[r])
            acc[r] = dot(mixed, w[t, :, : z.oc], 1, 1) + so_far

        over_rows(span, ratios)
        bias = jnp.zeros((16, 64), F)
        for s in range(z.m):
            bias = bias + w[t, s * z.share + 24 : s * z.share + 40, z.oc :].astype(F)
        bup_out[0] = jnp.broadcast_to(rows_to_lanes(bias.astype(B), z.ff), (8, z.ff))
        if not last:
            return

        @pl.when(t == cnt - 1)
        def _():
            lanes = z.width
            per = z.share // 64
            tile = (iota((64, lanes), 1) % 64 == iota((64, lanes), 0)).astype(F).astype(B)
            found = jnp.zeros((24, lanes), F)
            for s in range(z.m):
                spread = dot(w[0, s * z.share : s * z.share + 24, z.oc :], tile)
                hit = iota((24, lanes), 1) // 64 == per * s + iota((24, lanes), 0) % per
                found = found + jnp.where(hit, spread, 0.0)
            pick = (iota((8, 24), 1) // per == iota((8, 24), 0)).astype(F).astype(B)
            vec = dot(pick, found.astype(B))
            vec_out[...] = vec

            def norm(r):
                res = acc[r] + vec[0:1] + x[r].astype(F)
                normal_out[r], inverse_out[r] = norm_stats(res)

            over_rows(span, norm)

    wide = fixed(span, z.width)
    ins, extra = [slot(span, z.hm), slot(hd + 8, z.hm)], []
    outs = [slot(span, z.oc), slot(span, z.oc), slot(8, z.ff)]
    shapes = [((cnt, span, z.oc), B), ((cnt, span, z.oc), F), ((cnt, 8, z.ff), F)]
    scratch = [pltpu.VMEM((cnt, z.width, z.oc + 64), B)]
    if last:
        ins, extra = ins + [wide, wide], [x, before]
        outs += [wide, fixed(span, 1), fixed(8, z.width)]
        shapes += [((span, z.width), F), ((span, 1), F), ((8, z.width), F)]
        scratch += [pltpu.VMEM((span, z.width), F)]
    else:
        outs, shapes = outs + [wide], shapes + [((span, z.width), F)]
    return call(
        body,
        (cnt,),
        [SCALARS] + [ANY] * 8 + ins,
        outs,
        shapes,
        scratch + [pltpu.SemaphoreType.DMA((cnt, 2 * z.m))],
        "attend",
    )(where, *pieces, qf, state, *extra)


def widen(z, where, pieces, normal, vec, bup):
    n, span = z.n, z.span

    def body(where, *refs):
        pcs, refs = refs[:8], refs[8:]
        normal, vec, bup, act_out, slope_out, w, low, sems = refs
        t = pl.program_id(0)
        fetch = Pieces(n, z.m, where, pcs, w, sems, 0, z.ff)

        @pl.when(t == 0)
        def _():
            fetch.start()
            low[...] = (normal[...] * vec[1:2] + vec[2:3]).astype(B)

        fetch.wait(t)

        def hidden(r):
            up = dot(low[r], w[t]) + bup[0, 0:1]
            share = 0.5 * (1.0 + lax.erf(up * 0.7071067811865476))
            act_out[0, r] = (up * share).astype(B)
            slope_out[0, r] = (share + up * jnp.exp(-0.5 * up * up) * 0.3989422804014327).astype(B)

        over_rows(span, hidden)

    return call(
        body,
        (n,),
        [SCALARS] + [ANY] * 8 + [fixed(span, z.width), fixed(8, z.width), slot(8, z.ff)],
        [slot(span, z.ff)] * 2,
        [((n, span, z.ff), B)] * 2,
        [
            pltpu.VMEM((n, z.width, z.ff), B),
            pltpu.VMEM((span, z.width), B),
            pltpu.SemaphoreType.DMA((n, 2 * z.m)),
        ],
        "widen",
    )(where, *pieces, normal, vec, bup)


def narrow(z, where, pieces, normal, vec, cot, act, slope):
    n, span, rows, m = z.n, z.span, z.rows, z.m

    def body(where, *refs):
        pcs, refs = refs[:8], refs[8:]
        normal, vec, cot, act, slope = refs[:5]
        out, dres_out, low, dup_out, small_out = refs[5:10]
        w, acc, sems = refs[10:]
        p, t = pl.program_id(0), pl.program_id(1)
        fetch = Pieces(n, m, where, pcs, w, sems, 0, z.ff)

        @pl.when((p == 0) & (t == 0))
        def _():
            fetch.start()

        @pl.when(p == 0)
        def _():
            fetch.wait(t)

            def down(r):
                acc[r] = dot(act[0, r], w[t], 1, 1) + jnp.where(t == 0, 0.0, acc[r])

            over_rows(span, down)

        @pl.when((p == 0) & (t == n - 1))
        def _():
            small_out[...] = jnp.zeros((8, z.width), F)

            def norm(r):
                normed = normal[r] * vec[1:2] + vec[2:3]
                second, inverse = norm_stats(acc[r] + vec[3:4] + normed)
                out[r] = (second * vec[4:5] + vec[5:6]).astype(B)
                up = cot[r].astype(F)
                dres = norm_back(second, inverse, vec[4:5], up)
                dres_out[r] = dres
                low[r] = dres.astype(B)
                small_out[...] += as_rows(
                    [
                        jnp.sum(dres, axis=0, keepdims=True),
                        jnp.sum(up * second, axis=0, keepdims=True),
                        jnp.sum(up, axis=0, keepdims=True),
                    ],
                    3,
                )

            over_rows(span, norm)

        @pl.when(p == 1)
        def _():
            def up_back(r):
                dup_out[0, r] = (dot(low[r], w[t]) * slope[0, r].astype(F)).astype(B)

            over_rows(span, up_back)

    second = lambda *shape: pl.BlockSpec((1,) + shape, lambda p, t: (p * t,) + (0,) * len(shape))
    return call(
        body,
        (2, n),
        [SCALARS]
        + [ANY] * 8
        + [
            fixed(span, z.width),
            fixed(8, z.width),
            fixed(span, z.width),
            pl.BlockSpec((1, span, z.ff), lambda p, t: (t * (1 - p) + (n - 1) * p, 0, 0)),
            second(span, z.ff),
        ],
        [fixed(span, z.width)] * 3 + [second(span, z.ff), fixed(8, z.width)],
        [
            ((span, z.width), B),
            ((span, z.width), F),
            ((span, z.width), B),
            ((n, span, z.ff), B),
            ((8, z.width), F),
        ],
        [
            pltpu.VMEM((n, z.width, z.ff), B),
            pltpu.VMEM((span, z.width), F),
            pltpu.SemaphoreType.DMA((n, 2 * m)),
        ],
        "narrow",
    )(where, *pieces, normal, vec, cot, act, slope)


def ffn_grad(z, where, normal, vec, d_ffn, act, dup):
    n, span, rows, m = z.n, z.span, z.rows, z.m

    def body(where, normal, vec, d_ffn, act, dup, keep, give, bup_out, low_t, normed_t, spare):
        t = pl.program_id(0)

        @pl.when(t == 0)
        def _():
            turn(low_t, spare, d_ffn[...].astype(F).T.astype(B), where, m)
            turn(normed_t, spare, (normal[...] * vec[1:2] + vec[2:3]).T.astype(B), where, m)

        store_turned(dot(low_t[...], act[0]), 0, keep, give, m)
        store_turned(dot(normed_t[...], dup[0]), z.ff, keep, give, m)
        bup_out[0] = jnp.broadcast_to(
            jnp.sum(dup[0].astype(F), axis=0, keepdims=True), (8, z.ff)
        )

    wide, grads = fixed(span, z.width), pl.BlockSpec((m, 1, rows, 2 * z.ff), lambda t: (0, t, 0, 0))
    return call(
        body,
        (n,),
        [SCALARS, wide, fixed(8, z.width), wide, slot(span, z.ff), slot(span, z.ff)],
        [grads, grads, slot(8, z.ff)],
        [((m, n, rows, 2 * z.ff), B)] * 2 + [((n, 8, z.ff), F)],
        [pltpu.VMEM((z.width, span), B)] * 3,
        "ffn_grad",
    )(where, normal, vec, d_ffn, act, dup)


def widen_back(z, where, pieces, normal, inverse, vec, dup, dres):
    n, span = z.n, z.span

    def body(where, *refs):
        pcs, refs = refs[:8], refs[8:]
        normal, inverse, vec, dup, dres, out, small_out, w, acc, sems = refs
        t = pl.program_id(0)
        fetch = Pieces(n, z.m, where, pcs, w, sems, 0, z.ff)
        pl.when(t == 0)(fetch.start)
        fetch.wait(t)

        def back(r):
            acc[r] = dot(dup[0, r], w[t], 1, 1) + jnp.where(t == 0, dres[r], acc[r])

        over_rows(span, back)

        @pl.when(t == n - 1)
        def _():
            small_out[...] = jnp.zeros((8, z.width), F)

            def norm(r):
                up = acc[r]
                back = norm_back(normal[r], inverse[r], vec[1:2], up)
                out[r] = back
                small_out[...] += as_rows(
                    [
                        jnp.sum(back, axis=0, keepdims=True),
                        jnp.sum(up * normal[r], axis=0, keepdims=True),
                        jnp.sum(up, axis=0, keepdims=True),
                    ],
                    0,
                )

            over_rows(span, norm)

    return call(
        body,
        (n,),
        [SCALARS]
        + [ANY] * 8
        + [
            fixed(span, z.width),
            fixed(span, 1),
            fixed(8, z.width),
            slot(span, z.ff),
            fixed(span, z.width),
        ],
        [fixed(span, z.width), fixed(8, z.width)],
        [((span, z.width), F), ((8, z.width), F)],
        [
            pltpu.VMEM((n, z.width, z.ff), B),
            pltpu.VMEM((span, z.width), F),
            pltpu.SemaphoreType.DMA((n, 2 * z.m)),
        ],
        "widen_back",
    )(where, *pieces, normal, inverse, vec, dup, dres)


def attend_back(z, where, pieces, dres, mixed, den, qf, q, state, feat, slots):
    cnt, first = len(slots), slots[0]
    n, span, hl, hd, m = z.n, z.span, z.hl, z.hd, z.m

    def body(where, *refs):
        pcs, refs = refs[:8], refs[8:]
        dres, mixed, den, qf, q, state, feat, dq_out, dstate_out, w, low, pair, sems = refs
        t = pl.program_id(0)
        fetch = Pieces(n, m, where, pcs, w, sems, z.q_cols, z.oc + 64, slots)

        @pl.when(t == 0)
        def _():
            fetch.start()
            low[...] = dres[...].astype(B)

        fetch.wait(t)
        start = second_start(z.oc)
        compact = state[0, :hd]
        total = jnp.broadcast_to(state[0, hd : hd + 1], (hd, z.hm))
        states, tables = stacked(compact, total, hl), stacked(feat[0], jnp.ones((hd, z.hm), B), hl)

        def back(r):
            d_mixed = dot(low[r], w[t, :, : z.oc]).astype(B).astype(F)
            d_num = d_mixed / den[0, r]
            d_den = -(d_num * mixed[0, r].astype(F))
            both = beside(d_num.astype(B), d_den.astype(B))
            pair[r] = both
            dash = (dot(both, states) * qf[0, r].astype(F)).astype(B)
            back = dot(dash, tables, 1, 1)
            dq_out[0, r] = ((back[:, : z.oc] - q[0, r].astype(F) * back[:, start:]) * z.scale).astype(B)

        over_rows(span, back)
        full = dot(pair[...], qf[0], 0, 0)
        row = jnp.concatenate(
            [
                jnp.sum(
                    full[start + h * hd : start + (h + 1) * hd, h * z.feats : (h + 1) * z.feats],
                    axis=0,
                    keepdims=True,
                )
                for h in range(hl)
            ],
            axis=1,
        )
        dstate_out[0] = jnp.concatenate(
            [diagonal_blocks(full[: z.oc], hl), jnp.broadcast_to(row, (8, z.hm))], axis=0
        ).astype(B)

    return call(
        body,
        (cnt,),
        [SCALARS]
        + [ANY] * 8
        + [
            fixed(span, z.width),
            slot(span, z.oc),
            slot(span, z.oc),
            slot(span, z.hm),
            slot(span, z.oc),
            slot(hd + 8, z.hm),
            slot(hd, z.hm, first=first),
        ],
        [slot(span, z.oc), slot(hd + 8, z.hm)],
        [((cnt, span, z.oc), B), ((cnt, hd + 8, z.hm), B)],
        [
            pltpu.VMEM((cnt, z.width, z.oc + 64), B),
            pltpu.VMEM((span, z.width), B),
            pltpu.VMEM((span, second_start(z.oc) + z.oc), B),
            pltpu.SemaphoreType.DMA((cnt, 2 * m)),
        ],
        "attend_back",
    )(where, *pieces, dres, mixed, den, qf, q, state, feat)


def project_back(z, where, pieces, x, dres, dq, k, v, kf, dstate, feat, mixed, small_a, small_b, dbup, slots, before=None):
    cnt, first, last = len(slots), slots[0], before is not None
    n, span, hl, hd, m, rows = z.n, z.span, z.hl, z.hd, z.m, z.rows
    cols = z.a_cols

    def body(where, *refs):
        pcs, refs = refs[:8], refs[8:]
        x, dres, dq, k, v, kf, dstate, feat, mixed, small_a, small_b, dbup = refs[:12]
        refs = refs[12:]
        if last:
            before, refs = refs[0], refs[1:]
            keep, give, out, w, x_t, low_t, spare, dqkv_low, acc, sems = refs
        else:
            keep, give, acc, w, x_t, low_t, spare, dqkv_low, sems = refs
        t = pl.program_id(0)
        fetch = Pieces(n, m, where, pcs, w, sems, 0, z.q_cols, slots)

        @pl.when(t == 0)
        def _():
            fetch.start()
            turn(x_t, spare, x[...].astype(F).T.astype(B), where, m)
            turn(low_t, spare, dres[...].T.astype(B), where, m)

        start = second_start(z.oc)
        table = block_diagonal(dstate[0, :hd], hl)
        total = dstate[0, hd : hd + 1].astype(F)
        dash = ((dot(v[0], table) + total) * kf[0].astype(F)).astype(B)
        dv = dot(kf[0], table, 1, 1)
        back = dot(dash, stacked(feat[0], jnp.ones((hd, z.hm), B), hl), 1, 1)
        dk = (back[:, : z.oc] - k[0].astype(F) * back[:, start:]) * z.scale
        dqkv = jnp.concatenate(
            [dq[0], dk.astype(B), dv.astype(B), jnp.zeros((span, 64), B)], axis=1
        )
        dqkv_low[...] = dqkv
        bias = jnp.sum(dqkv.astype(F), axis=0, keepdims=True)
        laid = jnp.broadcast_to(bias, (rows, z.q_cols))
        laid = jnp.where(iota(laid.shape, 1) // 64 == iota(laid.shape, 0), laid, 0.0)
        grad = dot(x_t[...], dqkv)
        edge = z.q_cols - 128
        store_turned(grad[:, :edge], 0, keep, give, m)
        store_turned(
            grad[:, edge:] + jnp.concatenate([folded(laid)] * (2 * m), axis=0), edge, keep, give, m
        )
        grad = dot(low_t[...], jnp.concatenate([mixed[0], jnp.zeros((span, 64), B)], axis=1))
        packed = small_a[...] + small_b[...] + as_rows([dbup[0, 0:1]], 6)
        per = z.width // 64
        one = (iota((rows, 8), 0) // per == iota((rows, 8), 1)).astype(F).astype(B)
        laid = dot(one, packed.astype(B))
        laid = jnp.where(iota(laid.shape, 1) // 64 == iota(laid.shape, 0) % per, laid, 0.0)
        edge = z.oc + 64 - 128
        store_turned(grad[:, :edge], z.q_cols, keep, give, m)
        store_turned(
            grad[:, edge:] + jnp.concatenate([folded(laid)] * (2 * m), axis=0),
            z.q_cols + edge,
            keep,
            give,
            m,
        )
        fetch.wait(t)

        def tokens_back(r):
            so_far = jnp.where(t == 0, before[r] if last else dres[r], acc[r])
            acc[r] = dot(dqkv_low[r], w[t], 1, 1) + so_far

        over_rows(span, tokens_back)

        if last:

            @pl.when(t == cnt - 1)
            def _():
                out[...] = acc[...].astype(B)

    grads = pl.BlockSpec((m, 1, rows, cols), lambda t: (0, t, 0, 0))
    wide, scratch = fixed(span, z.width), [pltpu.VMEM((cnt, z.width, z.q_cols), B)]
    scratch += [pltpu.VMEM((z.width, span), B)] * 3 + [pltpu.VMEM((span, z.q_cols), B)]
    if last:
        scratch += [pltpu.VMEM((span, z.width), F)]
    return call(
        body,
        (cnt,),
        [SCALARS]
        + [ANY] * 8
        + [
            wide,
            wide,
            slot(span, z.oc),
            slot(span, z.oc),
            slot(span, z.oc),
            slot(span, z.hm),
            slot(hd + 8, z.hm),
            slot(hd, z.hm, first=first),
            slot(span, z.oc),
            fixed(8, z.width),
            fixed(8, z.width),
            slot(8, z.ff, first=first),
        ]
        + ([wide] if last else []),
        [grads, grads, wide],
        [((m, cnt, rows, cols), B)] * 2 + [((span, z.width), B if last else F)],
        scratch + [pltpu.SemaphoreType.DMA((cnt, 2 * m))],
        "project_back",
    )(
        where, *pieces, x, dres, dq, k, v, kf, dstate, feat, mixed, small_a, small_b, dbup,
        *([before] if last else []),
    )


def place(part, axis, index, count):
    shape = list(part.shape)
    shape[axis] *= count
    return lax.dynamic_update_slice_in_dim(
        jnp.zeros(shape, part.dtype), part, index * part.shape[axis], axis
    )


def on_device(
    sizes,
    tokens,
    lengths,
    features,
    w_qkv,
    b_qkv,
    w_out,
    b_out,
    gain_one,
    shift_one,
    w_up,
    b_up,
    w_down,
    b_down,
    gain_two,
    shift_two,
    cotangent,
):
    links = Links(sizes)
    z = Shape(sizes, features, tokens, b_up)
    n, m, share = z.n, z.m, z.share
    where = jnp.stack([links.s, links.core]).astype(jnp.int32)
    def tall(value):
        return jnp.pad(value, ((0, share - value.shape[0]), (0, 0)))

    biases = place(b_qkv, 2, links.s, m).reshape(3 * z.hl, z.hd)
    vectors = gather_rows([b_out, gain_one, shift_one, b_down, gain_two, shift_two], 24)
    vectors = jnp.concatenate([vectors, place(b_up, 1, links.s, m).reshape(-1, 64)])
    local_a = links.half(
        jnp.concatenate([w_qkv.reshape(share, z.qc), tall(biases), w_out.T, tall(vectors)], axis=1)
    )
    feat_half = links.half(features.transpose(2, 0, 1).reshape(z.hd, z.hm))
    local_u, local_d = links.half(w_up), links.half(w_down.T)
    length = lax.dynamic_index_in_dim(lengths, links.t, 0, keepdims=False)
    order = (links.t - jnp.arange(n)) % n
    position = links.c * z.span + order[:, None] * z.chunk + jnp.arange(z.chunk)[None]
    valid = (position.reshape(-1, 1) < length).astype(F)
    halves = (range(n // 2), range(n // 2, n))
    lo, hi = halves

    def join_states(state, top, came):
        row, mask = z.hd + 1, 1
        own = most = top[:, :1]
        while mask < sizes["context"]:
            if mask > 1:
                came = links.perm_c(state, mask), links.perm_c(top, mask)
                other, other_top = came[0], came[1][:, :1]
            else:
                other = came
                other_top = wide_add(*[other[:, row + i : row + i + 1] for i in range(3)])
            joint = jnp.maximum(most, other_top)
            state = (
                state.astype(F) * jnp.exp(most - joint) + other.astype(F) * jnp.exp(other_top - joint)
            ).astype(B)
            most, mask = joint, 2 * mask
            top = jnp.broadcast_to(most, top.shape)
        return state, jnp.exp(own - most)

    def join_grads(state, came, fall):
        mask = 1
        while mask < sizes["context"]:
            other = came if mask == 1 else links.perm_c(state, mask)
            state = wide_add(state, other).astype(B)
            mask *= 2
        return (state.astype(F) * fall).astype(B)

    block_a = links.spread_t(local_a)
    block_a, tokens, feat_half = together(block_a, tokens, feat_half)
    near_a = links.spread_near(block_a)
    moved = links.carry(tokens, feat_half, links.by_length())
    steps = links.by_length()
    *moved, block_a, near_a, local_u, tokens, feat_half = together(
        *[moved[d] for d in steps], block_a, near_a, local_u, tokens, feat_half
    )
    moved = dict(zip(steps, moved))
    far_a = links.spread_far(near_a)
    other_a = links.swap((block_a,) + near_a)
    x, feat_mine = links.unload(tokens, feat_half, moved)
    far_a, feat_mine, other_a, local_u, valid, x = together(far_a, feat_mine, other_a, local_u, valid, x)
    far_a = (jnp.concatenate(far_a),)
    other_a += links.swap(far_a)
    feat_other = links.perm_c(feat_mine)
    feat_low = jnp.where(links.core == 0, feat_mine, feat_other)
    feat_high = jnp.where(links.core == 0, feat_other, feat_mine)
    feat = jnp.concatenate([feat_low, feat_high], axis=1)
    feat, other_a, local_u = together(feat, other_a, local_u)
    pieces_a = (block_a,) + near_a + far_a + other_a
    block_u = links.spread_t(local_u)
    first = project(z, where, pieces_a, x, feat, valid, lo)
    first, block_u, local_d, valid, cot = together(first, block_u, local_d, valid, cotangent)
    near_u = links.spread_near(block_u)
    moved = links.carry(cot, local_d, (2,))
    other_u = links.swap((block_u,))
    came = links.perm_c(first[5])
    second = project(z, where, pieces_a, x, feat, valid, hi)
    first, second, near_u, block_u, other_u, moved, came, cot, local_d = together(
        first, second, near_u, block_u, other_u, moved, came, cot, local_d
    )
    made = (first, second)
    far_u = links.spread_far(near_u)
    moved.update(links.carry(cot, local_d, (1, 3)))
    came_b = links.perm_c(second[5])
    state_a, fall_a = join_states(first[5], first[6], came)
    one = attend(z, where, pieces_a, first[3], state_a, lo)
    one, far_u, near_u, other_u, moved, came_b, cot, local_d = together(
        one, far_u, near_u, other_u, moved, came_b, cot, local_d
    )
    mixed_a, den_a, bup_a, acc = one
    far_u = (jnp.concatenate(far_u),)
    cot, block_d = links.unload(cot, local_d, moved)
    near_d = links.spread_near(block_d)
    other_u += links.swap(near_u + far_u)
    state_b, fall_b = join_states(second[5], second[6], came_b)
    two = attend(z, where, pieces_a, second[3], state_b, hi, x, acc)
    two, near_d, block_d, other_u, cot = together(two, near_d, block_d, other_u, cot)
    mixed_b, den_b, bup_b, normal, inverse, vec = two
    states, falls = (state_a, state_b), (fall_a, fall_b)
    bup = jnp.concatenate([bup_a, bup_b])
    mixed, den = (mixed_a, mixed_b), (den_a, den_b)
    pieces_u = (block_u,) + near_u + far_u + other_u
    far_d = links.spread_far(near_d)
    other_d = links.swap((block_d,) + near_d)
    act, slope = widen(z, where, pieces_u, normal, vec, bup)
    act, slope, far_d, other_d = together(act, slope, far_d, other_d)
    far_d = (jnp.concatenate(far_d),)
    other_d += links.swap(far_d)
    pieces_d = (block_d,) + near_d + far_d + other_d
    out, d_res_two, d_ffn, dup, small_b = narrow(
        z, where, pieces_d, normal, vec, cot, act, slope
    )
    sent = links.undeal_some(out, (2,))
    keep, give, dbup = ffn_grad(z, where, normal, vec, d_ffn, act, dup)
    keep, give, out, dup, sent = together(keep, give, out, dup, sent)
    other = links.perm_c(give)
    sent.update(links.undeal_some(out, (1, 3)))
    d_res_one, small_a = widen_back(z, where, pieces_u, normal, inverse, vec, dup, d_res_two)
    d_res_one, keep, other, sent = together(d_res_one, keep, other, sent)
    result = links.undealt(out, sent, B)
    slots_f = keep, other
    split = lambda slots: ([term[:, : n // 2] for term in slots], [term[:, n // 2 :] for term in slots])
    one_f = links.collect_one(*split(slots_f))
    dq_a, d_state_a = attend_back(
        z, where, pieces_a, d_res_one, mixed[0], den[0], made[0][3], made[0][0], states[0], feat, lo
    )
    dq_a, d_state_a, d_res_one, slots_f = together(dq_a, d_state_a, d_res_one, slots_f)
    came = links.perm_c(d_state_a)
    dq_b, d_state_b = attend_back(
        z, where, pieces_a, d_res_one, mixed[1], den[1], made[1][3], made[1][0], states[1], feat, hi
    )
    dq_b, d_state_b, came, one_f, slots_f, x = together(dq_b, d_state_b, came, one_f, slots_f, x)
    two_f = links.collect_two(*split(slots_f), one_f)
    came_b = links.perm_c(d_state_b)
    d_state_a = join_grads(d_state_a, came, falls[0])
    dq = (dq_a, dq_b)

    def run_back(i, d_state, x, before):
        return project_back(
            z, where, pieces_a, x, d_res_one, dq[i], made[i][1], made[i][2], made[i][4],
            d_state, feat, mixed[i], small_a, small_b, dbup, halves[i], before,
        )

    keep, give, acc = run_back(0, d_state_a, x, None)
    keep, give, acc, two_f, came_b, slots_f, x = together(keep, give, acc, two_f, came_b, slots_f, x)
    sums_f = links.sums(*split(slots_f), one_f, two_f)
    terms_f = links.collect_t(sums_f, (2, 1))
    other = links.perm_c(give)
    d_state_b = join_grads(d_state_b, came_b, falls[1])
    keep_b, give_b, grad_x = run_back(1, d_state_b, x, acc)
    keep_b, give_b, grad_x, keep, other, terms_f, sums_f = together(
        keep_b, give_b, grad_x, keep, other, terms_f, sums_f
    )
    other_b = links.perm_c(give_b)
    terms_f += links.collect_t(sums_f, range(3, n))
    keep_b, other_b, grad_x = together(keep_b, other_b, grad_x)
    low, high = (keep, other), (keep_b, other_b)
    one = links.collect_one(low, high)
    sent = links.undeal_some(grad_x, (2,))
    one, low, high, sent, grad_x, terms_f = together(one, low, high, sent, grad_x, terms_f)
    two = links.collect_two(low, high, one)
    sent.update(links.undeal_some(grad_x, (1, 3)))
    two, one, low, high, sent, grad_x = together(two, one, low, high, sent, grad_x)
    grad_tokens = links.undealt(grad_x, sent, F)
    sums = links.sums(low, high, one, two)
    terms = [sums[0]] + links.collect_t(sums, links.by_length())
    terms_f = [sums_f[0]] + terms_f
    own_ffn = links.collect_end(terms_f)
    grad_up, grad_down = own_ffn[:, z.ff :].astype(F), own_ffn[:, : z.ff].T.astype(F)
    terms, grad_tokens, result, grad_up, grad_down = together(
        terms, grad_tokens, result, grad_up, grad_down
    )
    own_qkv = links.collect_end(terms)
    def mine(value, axis):
        size = value.shape[axis] // m
        return lax.dynamic_slice_in_dim(value, links.s * size, size, axis).astype(F)

    own_b_qkv = mine(own_qkv[: 3 * z.hl, z.qc : z.q_cols].reshape(3, z.hl, z.hd), 2)
    own_out = own_qkv[:, z.q_cols : z.q_cols + z.oc]
    tail = own_qkv[: z.rows, z.q_cols + z.oc :]
    vecs = mine(tail[: 6 * z.width // 64].reshape(6, z.width), 1)
    start = 6 * z.width // 64
    own_b_up = mine(tail[start : start + z.ff // 64].reshape(b_up.shape[0], -1), 1)
    return (
        result,
        grad_tokens,
        own_qkv[:, : z.qc].reshape(w_qkv.shape).astype(F),
        own_b_qkv,
        own_out.T.astype(F),
        vecs[0],
        vecs[1],
        vecs[2],
        grad_up,
        own_b_up,
        grad_down,
        vecs[3],
        vecs[4],
        vecs[5],
    )


def solution(mesh):
    sizes = dict(mesh.shape)
    in_specs = (
        P("shard", ("context", "tensor"), None),
        P("shard"),
        P("tensor", None, None),
        P("shard", None, "tensor", None),
        P(None, "tensor", "shard"),
        P("tensor", "shard"),
        P("shard"),
        P("shard"),
        P("shard"),
        P("shard", "tensor"),
        P("tensor", "shard"),
        P("tensor", "shard"),
        P("shard"),
        P("shard"),
        P("shard"),
        P("shard", ("context", "tensor"), None),
    )
    out_specs = (
        P("shard", ("context", "tensor"), None),
        P("shard", ("context", "tensor"), None),
        P("shard", None, "tensor", None),
        P(None, "tensor", "shard"),
        P("tensor", "shard"),
        P("shard"),
        P("shard"),
        P("shard"),
        P("shard", "tensor"),
        P("tensor", "shard"),
        P("tensor", "shard"),
        P("shard"),
        P("shard"),
        P("shard"),
    )
    return jax.shard_map(
        functools.partial(on_device, sizes),
        mesh=mesh,
        in_specs=in_specs,
        out_specs=out_specs,
        check_vma=False,
    )
```
